32 devices in a mesh: dp: 8 (over y, x, core), mp: 4 (over z).
Axes of the slice: x: 2, y: 2, z: 4, core: 2. Of those that a mesh axis runs over, the one named last changes fastest.
Arguments:
- inputs: bfloat16 [2, 16384, 1024], P(None, ('dp', 'mp')), may hold values from -6 to 6
- segments: int32 [2, 8, 2048], P(None, 'dp'), may hold values from 0 to 3, as said below
- w_query: bfloat16 [1024, 1024], P('dp', 'mp'), may hold values from -0.1875 to 0.1875
- w_key: bfloat16 [1024, 1024], P('dp', 'mp'), may hold values from -0.1875 to 0.1875
- w_value: bfloat16 [1024, 1024], P('dp', 'mp'), may hold values from -0.1875 to 0.1875
- w_output: bfloat16 [1024, 1024], P('mp', 'dp'), may hold values from -0.75 to 0.75
- w_gate: bfloat16 [1024, 2816], P('dp', 'mp'), may hold values from -0.1875 to 0.1875
- w_up: bfloat16 [1024, 2816], P('dp', 'mp'), may hold values from -0.1875 to 0.1875
- w_down: bfloat16 [2816, 1024], P('mp', 'dp'), may hold values from -0.109375 to 0.109375
- gain_attn: float32 [1024], P('dp'), may hold values from 0.25 to 1.75
- gain_ffn: float32 [1024], P('dp'), may hold values from 0.25 to 1.75
- cotangent: bfloat16 [2, 16384, 1024], P(None, ('dp', 'mp')), may hold values from -6 to 6
Outputs:
- result: bfloat16 [2, 16384, 1024], P(None, ('dp', 'mp'))
- grad_inputs: bfloat16 [2, 16384, 1024], P(None, ('dp', 'mp'))
- grad_query: float32 [1024, 1024], P('dp', 'mp')
- grad_key: float32 [1024, 1024], P('dp', 'mp')
- grad_value: float32 [1024, 1024], P('dp', 'mp')
- grad_output: float32 [1024, 1024], P('mp', 'dp')
- grad_gate: float32 [1024, 2816], P('dp', 'mp')
- grad_up: float32 [1024, 2816], P('dp', 'mp')
- grad_down: float32 [2816, 1024], P('mp', 'dp')
- grad_norm_attn: float32 [1024], P(('dp', 'mp'))
- grad_norm_ffn: float32 [1024], P(('dp', 'mp'))
The draws below stay inside these ranges and needn't reach their ends.
Inputs may be any that keep to these rules, and one draw needn't show every extreme that they name: `segments`: within each packed row the segment numbers never fall and each number names one run of consecutive patches; every row holds four documents, one of exactly 1024 patches and three of 204 patches or more.
All inputs are finite; a program needn't handle non-finite values.
Results may differ from the reference program's by a relative error of at most 0.035.
Values may be sent and summed in bfloat16 or wider, within the bound.
A program may use at most 320 MiB of HBM per device.

```python
import math
import jax
import jax.numpy as jnp
from jax import lax

D = 1024
HD = 64
FF = 2816
SEQ = 2048
MB = 2
PATCHES = 16384
N_DP = 8


def draw_segments(key, part):
    row_keys = jax.random.split(key, MB * N_DP)

    def one_row(row_key):
        half_run = SEQ // 2
        least_run = SEQ // 10
        spare = SEQ - half_run - 3 * least_run
        key_cuts, key_slot = jax.random.split(row_key, 2)
        cuts = jax.random.randint(key_cuts, (2,), 0, spare + 1)
        first_cut = jnp.min(cuts)
        second_cut = jnp.max(cuts)
        small_runs = jnp.stack([first_cut, second_cut - first_cut, spare - second_cut]) + least_run
        slot = jax.random.randint(key_slot, (), 0, 4)
        index_runs = jnp.arange(4, dtype=jnp.int32)
        source = jnp.clip(index_runs - (index_runs > slot).astype(jnp.int32), 0, 2)
        run_sizes = jnp.where(index_runs == slot, half_run, small_runs[source])
        run_ends = jnp.cumsum(run_sizes)
        places = jnp.arange(SEQ, dtype=jnp.int32)
        return jnp.sum((places[:, None] >= run_ends[None, :3]).astype(jnp.int32), axis=1).astype(jnp.int32)
    return jax.vmap(one_row)(row_keys).reshape(MB, N_DP, SEQ)


def block_scale(own_key, shape, pieces, smallest, top_value):
    def one(dim, blocks):
        draws = jax.random.uniform(jax.random.fold_in(jax.random.fold_in(own_key, 6), dim), (blocks,), jnp.float32, smallest / len(pieces), top_value / len(pieces))
        return jnp.repeat(jnp.exp(draws), shape[dim] // blocks).reshape((-1,) + (1,) * (len(shape) - dim - 1))

    factor_of = one(*pieces[0])
    for cut in pieces[1:]:
        factor_of = factor_of * one(*cut)
    return factor_of


def centred(stream_key, extent, spread, reach, cuts=(), kind=jnp.bfloat16):
    factor_of = block_scale(stream_key, extent, cuts, -0.22, 0.18) if cuts else 1.0
    drawn = jax.random.normal(stream_key, extent, jnp.float32) * spread * factor_of
    return jnp.minimum(jnp.maximum(drawn, -reach), reach).astype(kind)


def setup_inputs(seed: int = 0) -> dict:
    seeds = jax.random.split(jax.random.key(seed), 13)
    inputs = centred(seeds[0], (MB, PATCHES, D), 1.0, 6.0, ((1, 32),))
    segments = draw_segments(jax.random.fold_in(seeds[12], 71), 0)
    w_query = centred(seeds[2], (D, D), D ** -0.5, 0.1875, ((0, 8), (1, 4)))
    w_key = centred(seeds[3], (D, D), D ** -0.5, 0.1875, ((0, 8), (1, 4)))
    w_value = centred(seeds[4], (D, D), D ** -0.5, 0.1875, ((0, 8), (1, 4)))
    w_output = centred(seeds[5], (D, D), (D // 16) ** -0.5, 0.75, ((0, 4), (1, 8)))
    w_gate = centred(seeds[6], (D, FF), D ** -0.5, 0.1875, ((0, 8), (1, 4)))
    w_up = centred(seeds[7], (D, FF), D ** -0.5, 0.1875, ((0, 8), (1, 4)))
    w_down = centred(seeds[8], (FF, D), FF ** -0.5, 0.109375, ((0, 4), (1, 8)))
    gain_attn = jnp.clip(1.0 + 0.15 * jax.random.normal(seeds[9], (D,), jnp.float32), 0.25, 1.75)
    gain_ffn = jnp.clip(1.0 + 0.15 * jax.random.normal(seeds[10], (D,), jnp.float32), 0.25, 1.75)
    cotangent = centred(seeds[11], (MB, PATCHES, D), 1.0, 6.0, ((1, 32),))
    return dict(inputs=inputs, segments=segments, w_query=w_query, w_key=w_key, w_value=w_value, w_output=w_output, w_gate=w_gate, w_up=w_up, w_down=w_down, gain_attn=gain_attn, gain_ffn=gain_ffn, cotangent=cotangent)


@jax.custom_vjp
def low(v):
    return lax.optimization_barrier(v.astype(jnp.bfloat16)).astype(jnp.float32)

@jax.custom_vjp
def low_back(v):
    return v

def low_keep(v):
    return (low(v), None)

def low_pass(kept, grad):
    return (grad,)

def back_keep(v):
    return (v, None)

def back_low(kept, grad):
    return (low(grad),)
low.defvjp(low_keep, low_pass)
low_back.defvjp(back_keep, back_low)
highest = lax.Precision.HIGHEST
eps_norm = 1e-05

def matmul(left, right):
    return jnp.dot(left, right, precision=highest)

def rope_tables(seg_row):
    length = seg_row.shape[0]
    places = jnp.arange(length, dtype=jnp.int32)
    earlier = jnp.concatenate([seg_row[:1] - 1, seg_row[:-1]])
    begins = lax.cummax(jnp.where(seg_row != earlier, places, 0), axis=0)
    offsets = (places - begins).astype(jnp.float32)
    half_dim = HD // 2
    frequency = jnp.exp(jnp.arange(half_dim, dtype=jnp.float32) * (-math.log(10000.0) / half_dim))
    angles = offsets[:, None] * frequency[None, :]
    cos_table = jnp.concatenate([jnp.cos(angles), jnp.cos(angles)], axis=1)
    sin_table = jnp.concatenate([jnp.sin(angles), jnp.sin(angles)], axis=1)
    return (cos_table, sin_table)

def rotate(tensor, cos_table, sin_table):
    half_dim = tensor.shape[-1] // 2
    turned = jnp.concatenate([-tensor[..., half_dim:], tensor[..., :half_dim]], axis=-1)
    return tensor * cos_table[:, None, :] + turned * sin_table[:, None, :]

def rms_scale(tensor, gain):
    factor = lax.rsqrt(lax.optimization_barrier(jnp.mean(tensor * tensor, axis=-1, keepdims=True)) + eps_norm)
    return tensor * factor * gain

def forward_row(params, row_in, seg_row):
    w_query, w_key, w_value, w_output, w_gate, w_up, w_down, gain_attn, gain_ffn = params
    length = row_in.shape[0]
    heads = w_query.shape[1] // HD
    cos_table, sin_table = rope_tables(seg_row)
    normed = low(rms_scale(row_in, gain_attn))
    query_pre = low_back(matmul(normed, w_query)).reshape(length, heads, HD)
    key_pre = low_back(matmul(normed, w_key)).reshape(length, heads, HD)
    queries = low(rotate(query_pre, cos_table, sin_table))
    key_rows = low(rotate(key_pre, cos_table, sin_table))
    value_rows = low(low_back(matmul(normed, w_value))).reshape(length, heads, HD)
    places = jnp.arange(length, dtype=jnp.int32)
    allowed = (seg_row[:, None] == seg_row[None, :]) & (places[None, :] <= places[:, None])
    scores = low_back(jnp.einsum('qhd,khd->hqk', queries, key_rows, precision=highest) * HD ** (-0.5))
    scores = jnp.where(allowed[None], scores, -1e+30)
    probs = low(jax.nn.softmax(scores, axis=-1))
    mixed = low(low_back(jnp.einsum('hqk,khd->qhd', probs, value_rows, precision=highest)))
    mixed = mixed.reshape(length, heads * HD)
    hidden_in = row_in + low_back(matmul(mixed, w_output))
    normed_ffn = low(rms_scale(hidden_in, gain_ffn))
    gate_pre = low_back(matmul(normed_ffn, w_gate))
    up_pre = low_back(matmul(normed_ffn, w_up))
    hidden = low(jax.nn.silu(gate_pre) * up_pre)
    return hidden_in + low_back(matmul(hidden, w_down))

def reference(inputs, segments, w_query, w_key, w_value, w_output, w_gate, w_up, w_down, gain_attn, gain_ffn, cotangent):
    params = (w_query.astype(jnp.float32), w_key.astype(jnp.float32), w_value.astype(jnp.float32), w_output.astype(jnp.float32), w_gate.astype(jnp.float32), w_up.astype(jnp.float32), w_down.astype(jnp.float32), gain_attn.astype(jnp.float32), gain_ffn.astype(jnp.float32))
    rows_in = inputs.astype(jnp.float32).reshape(MB * N_DP, SEQ, D)
    seg_rows = segments.reshape(MB * N_DP, SEQ)
    cot_rows = cotangent.astype(jnp.float32).reshape(MB * N_DP, SEQ, D)

    def one_row(totals, items):
        row_in, seg_row, row_cot = items

        def forward_fixed(param_set, values_in):
            return forward_row(param_set, values_in, seg_row)
        row_out, pullback = jax.vjp(forward_fixed, params, row_in)
        grad_params, grad_row = pullback(row_cot)
        totals = jax.tree.map(jnp.add, totals, grad_params)
        return (totals, (row_out.astype(jnp.bfloat16), grad_row.astype(jnp.bfloat16)))
    zeros_start = jax.tree.map(jnp.zeros_like, params)
    totals, (outputs, grads_in) = lax.scan(one_row, zeros_start, (rows_in, seg_rows, cot_rows))
    result = outputs.reshape(MB, N_DP * SEQ, D)
    grad_inputs = grads_in.reshape(MB, N_DP * SEQ, D)
    return (result, grad_inputs, totals[0], totals[1], totals[2], totals[3], totals[4], totals[5], totals[6], totals[7], totals[8])
```

```python
import functools
import math

import jax
import jax.numpy as jnp
from jax import lax
from jax.experimental import pallas as pl
from jax.experimental.pallas import tpu as pltpu
from jax.sharding import PartitionSpec as P

HD = 64
BQ = 512
BK = 256
HPS = 2

def attn_fwd_kernel(lo_ref, q_ref, k_ref, v_ref, start_ref, o_ref, lse_ref, k_scr, *, bq, bk, heads):
    length = q_ref.shape[1]
    k_scr[...] = k_ref[...].T
    def q_step(qi, carry):
        q0 = pl.multiple_of(qi * bq, bq)
        qcols = pl.ds(q0, bq)
        q_blk = q_ref[:, qcols]
        start = start_ref[:, qcols]
        q_idx = q0 + lax.broadcasted_iota(jnp.int32, (1, bq), 1)
        def k_step(kb, state):
            k0 = pl.multiple_of(kb * bk, bk)
            k_idx = k0 + lax.broadcasted_iota(jnp.int32, (bk, bq), 0)
            allowed = (k_idx >= start) & (k_idx <= q_idx)
            out = []
            for h in range(heads):
                peak, total, acc = state[h]
                s = jnp.dot(k_scr[pl.ds(k0, bk), h * HD:(h + 1) * HD], q_blk[h * HD:(h + 1) * HD], preferred_element_type=jnp.float32)
                s = jnp.where(allowed, s, -1e30)
                new_peak = jnp.maximum(peak, jnp.max(s, axis=0, keepdims=True))
                p = jnp.exp(s - new_peak)
                fade = jnp.exp(peak - new_peak)
                total = total * fade + jnp.sum(p, axis=0, keepdims=True)
                acc = acc * fade + jnp.dot(v_ref[h * HD:(h + 1) * HD, pl.ds(k0, bk)], p.astype(jnp.bfloat16), preferred_element_type=jnp.float32)
                out.append((new_peak, total, acc))
            return tuple(out)
        init = tuple((jnp.full((1, bq), -1e30, jnp.float32), jnp.zeros((1, bq), jnp.float32), jnp.zeros((HD, bq), jnp.float32)) for _ in range(heads))
        hi = (q0 + bq - 1) // bk
        state = lax.fori_loop(lo_ref[qi], hi + 1, k_step, init)
        for h in range(heads):
            peak, total, acc = state[h]
            o_ref[h * HD:(h + 1) * HD, qcols] = (acc / total).astype(jnp.bfloat16)
            lse_ref[h, :, qcols] = peak + jnp.log(total)
        return carry
    lax.fori_loop(0, length // bq, q_step, 0)

def attn_bwd_kernel(lo_ref, q_ref, k_ref, v_ref, do_ref, o_ref, lse_ref, start_ref, cos_ref, sin_ref, out_ref, k_scr, v_scr, dk_scr, dv_scr, *, bq, bk, heads):
    length = q_ref.shape[1]
    k_scr[...] = k_ref[...].T
    v_scr[...] = v_ref[...].T
    dk_scr[...] = jnp.zeros_like(dk_scr)
    dv_scr[...] = jnp.zeros_like(dv_scr)
    half = HD // 2
    def unrotate(g, cos, sin):
        a, b = g[:half], g[half:]
        return jnp.concatenate([a * cos + b * sin, b * cos - a * sin], axis=0).astype(jnp.bfloat16)
    def q_step(qi, carry):
        q0 = pl.multiple_of(qi * bq, bq)
        qcols = pl.ds(q0, bq)
        q_blk = q_ref[:, qcols]
        do_blk = do_ref[:, qcols]
        q_t = q_blk.T
        do_t = do_blk.T
        prod = do_blk.astype(jnp.float32) * o_ref[:, qcols].astype(jnp.float32)
        start = start_ref[:, qcols]
        q_idx = q0 + lax.broadcasted_iota(jnp.int32, (1, bq), 1)
        deltas = [jnp.sum(prod[h * HD:(h + 1) * HD], axis=0, keepdims=True) for h in range(heads)]
        lses = [lse_ref[h, :, qcols] for h in range(heads)]
        def k_step(kb, state):
            k0 = pl.multiple_of(kb * bk, bk)
            rows = pl.ds(k0, bk)
            k_idx = k0 + lax.broadcasted_iota(jnp.int32, (bk, bq), 0)
            allowed = (k_idx >= start) & (k_idx <= q_idx)
            out = []
            for h in range(heads):
                hs = slice(h * HD, (h + 1) * HD)
                s = jnp.dot(k_scr[rows, hs], q_blk[hs], preferred_element_type=jnp.float32)
                p = jnp.exp(jnp.where(allowed, s - lses[h], -1e30))
                dp = jnp.dot(v_scr[rows, hs], do_blk[hs], preferred_element_type=jnp.float32)
                ds = (p * (dp - deltas[h])).astype(jnp.bfloat16)
                dv_scr[h, rows, :] += jnp.dot(p.astype(jnp.bfloat16), do_t[:, hs], preferred_element_type=jnp.float32)
                dk_scr[h, rows, :] += jnp.dot(ds, q_t[:, hs], preferred_element_type=jnp.float32)
                out.append(state[h] + jnp.dot(k_ref[hs, rows], ds, preferred_element_type=jnp.float32))
            return tuple(out)
        init = tuple(jnp.zeros((HD, bq), jnp.float32) for _ in range(heads))
        hi = (q0 + bq - 1) // bk
        state = lax.fori_loop(lo_ref[qi], hi + 1, k_step, init)
        cos, sin = cos_ref[:, qcols], sin_ref[:, qcols]
        for h in range(heads):
            out_ref[0, h * HD:(h + 1) * HD, qcols] = unrotate(state[h] * HD ** -0.5, cos, sin)
        return carry
    lax.fori_loop(0, length // bq, q_step, 0)
    for h in range(heads):
        out_ref[1, h * HD:(h + 1) * HD, :] = unrotate(dk_scr[h].T, cos_ref[...], sin_ref[...])
        out_ref[2, h * HD:(h + 1) * HD, :] = dv_scr[h].T.astype(jnp.bfloat16)

def attn_fwd(qkv_t, start, lo, bq=BQ, bk=BK, hps=HPS):
    cols3, length = qkv_t.shape
    cols = cols3 // 3
    steps = cols // (HD * hps)
    blk = (HD * hps, length)
    area = cols * length * length // 4
    return pl.pallas_call(
        functools.partial(attn_fwd_kernel, bq=bq, bk=bk, heads=hps),
        out_shape=(jax.ShapeDtypeStruct((cols, length), jnp.bfloat16), jax.ShapeDtypeStruct((cols // HD, 1, length), jnp.float32)),
        grid_spec=pltpu.PrefetchScalarGridSpec(
            num_scalar_prefetch=1, grid=(steps,),
            in_specs=[pl.BlockSpec(blk, lambda i, lo: (i, 0)), pl.BlockSpec(blk, lambda i, lo: (i + steps, 0)), pl.BlockSpec(blk, lambda i, lo: (i + 2 * steps, 0)),
                      pl.BlockSpec((1, length), lambda i, lo: (0, 0))],
            out_specs=[pl.BlockSpec(blk, lambda i, lo: (i, 0)), pl.BlockSpec((hps, 1, length), lambda i, lo: (i, 0, 0))],
            scratch_shapes=[pltpu.VMEM((length, HD * hps), jnp.bfloat16)]),
        cost_estimate=pl.CostEstimate(flops=16 * area, bytes_accessed=cols * length * 8, transcendentals=area // HD),
        name="attn_fwd",
    )(lo, qkv_t, qkv_t, qkv_t, start)

def attn_bwd(qkv_t, do_t, o_t, lse, start, lo, cos, sin, bq=BQ, bk=BK, hps=HPS):
    cols3, length = qkv_t.shape
    cols = cols3 // 3
    steps = cols // (HD * hps)
    blk = (HD * hps, length)
    area = cols * length * length // 4
    return pl.pallas_call(
        functools.partial(attn_bwd_kernel, bq=bq, bk=bk, heads=hps),
        out_shape=jax.ShapeDtypeStruct((3, cols, length), jnp.bfloat16),
        grid_spec=pltpu.PrefetchScalarGridSpec(
            num_scalar_prefetch=1, grid=(steps,),
            in_specs=[pl.BlockSpec(blk, lambda i, lo: (i, 0)), pl.BlockSpec(blk, lambda i, lo: (i + steps, 0)), pl.BlockSpec(blk, lambda i, lo: (i + 2 * steps, 0)),
                      pl.BlockSpec(blk, lambda i, lo: (i, 0)), pl.BlockSpec(blk, lambda i, lo: (i, 0)),
                      pl.BlockSpec((hps, 1, length), lambda i, lo: (i, 0, 0)),
                      pl.BlockSpec((1, length), lambda i, lo: (0, 0)),
                      pl.BlockSpec((HD // 2, length), lambda i, lo: (0, 0)), pl.BlockSpec((HD // 2, length), lambda i, lo: (0, 0))],
            out_specs=pl.BlockSpec((3,) + blk, lambda i, lo: (0, i, 0)),
            scratch_shapes=[pltpu.VMEM((length, HD * hps), jnp.bfloat16)] * 2 + [pltpu.VMEM((hps, length, HD), jnp.float32)] * 2),
        cost_estimate=pl.CostEstimate(flops=40 * area, bytes_accessed=cols * length * 20, transcendentals=area // HD),
        name="attn_bwd",
    )(lo, qkv_t, qkv_t, qkv_t, do_t, o_t, lse, start, cos, sin)

eps_norm = 1e-05


def dot_dims(left, right, left_dim, right_dim):
    return lax.dot_general(
        left, right, (((left_dim,), (right_dim,)), ((), ())), preferred_element_type=jnp.float32
    )


def row_starts(seg_row):
    ones = [jnp.sum((seg_row < s).astype(jnp.int32)) for s in (1, 2, 3)]
    start = jnp.zeros_like(seg_row)
    before = 0
    for s, count in zip((1, 2, 3), ones):
        start = start + jnp.where(seg_row >= s, count - before, 0)
        before = count
    return start


def rope_tables(start):
    half_dim = HD // 2
    offsets = (jnp.arange(start.shape[0], dtype=jnp.int32) - start).astype(jnp.float32)
    frequency = jnp.exp(jnp.arange(half_dim, dtype=jnp.float32) * (-math.log(10000.0) / half_dim))
    angles = frequency[:, None] * offsets[None, :]
    return jnp.cos(angles), jnp.sin(angles)


def rotate(rows, cos_table, sin_table):
    count, length = rows.shape
    parts = rows.reshape(count // HD, 2, HD // 2, length)
    low, high = parts[:, 0], parts[:, 1]
    turned = jnp.stack(
        [low * cos_table - high * sin_table, high * cos_table + low * sin_table], axis=1
    )
    return turned.reshape(count, length)


def rms_factor(values):
    return lax.rsqrt(jnp.mean(values * values, axis=-1, keepdims=True) + eps_norm)


def rms_back(values_in, factor, gain, grad_normed):
    scaled = grad_normed * gain
    gain_part = jnp.sum(grad_normed * values_in * factor, axis=0)
    inner = jnp.mean(scaled * values_in, axis=-1, keepdims=True)
    return factor * scaled - values_in * (factor * factor * factor) * inner, gain_part


def scatter(partial_sum, axis, dim):
    return lax.psum_scatter(partial_sum, axis, scatter_dimension=dim, tiled=True)


def local(
    inputs, segments, w_query, w_key, w_value, w_output, w_gate, w_up, w_down,
    gain_attn, gain_ffn, cotangent,
):
    low = jnp.bfloat16
    n_dp, n_mp = lax.axis_size("dp"), lax.axis_size("mp")
    batches, tokens, width = inputs.shape
    cols = w_query.shape[1]
    depth = w_query.shape[0]
    hidden_part = w_gate.shape[1]

    def split16(gain):
        high = gain.astype(low)
        return high, (gain - high.astype(jnp.float32)).astype(low)

    pieces = split16(gain_attn) + split16(gain_ffn)
    gain_row = jnp.concatenate(pieces + (jnp.zeros((3 * cols - 4 * depth,), low),))
    qkv_piece = jnp.concatenate(
        [
            jnp.concatenate([w_query, w_key, w_value], axis=1),
            jnp.pad(gain_row[None], ((0, 15), (0, 0))),
        ],
        axis=0,
    )
    qkv_all = lax.all_gather(qkv_piece, "dp", axis=0, tiled=False)
    w_qkv = qkv_all[:, :depth].reshape(width, 3 * cols)
    gains = qkv_all[:, depth, : 4 * depth].astype(jnp.float32).reshape(n_dp, 4, depth)
    gain_one = (gains[:, 0] + gains[:, 1]).reshape(width)
    gain_two = (gains[:, 2] + gains[:, 3]).reshape(width)

    rows_all = [lax.all_gather(inputs[m], "mp", axis=0, tiled=True) for m in range(batches)]

    rest_piece = jnp.concatenate([w_output, w_gate.T, w_up.T, w_down], axis=0)
    rest_all = lax.all_gather(rest_piece, ("dp", "mp"), axis=0, tiled=False)
    rest_all = rest_all.reshape(n_dp, n_mp, rest_piece.shape[0], depth)

    def whole(first, count):
        part = rest_all[:, :, first : first + count]
        return part.transpose(1, 2, 0, 3).reshape(n_mp * count, width)

    output_full = whole(0, cols)
    gate_full = whole(cols, hidden_part)
    up_full = whole(cols + hidden_part, hidden_part)
    down_full = whole(cols + 2 * hidden_part, hidden_part)

    normed, qkv, tables, starts, lows, mixed, logs = [], [], [], [], [], [], []
    for m in range(batches):
        start = row_starts(segments[m, 0])
        cos_table, sin_table = rope_tables(start)
        tables.append((cos_table, sin_table))
        starts.append(start[None])
        lows.append(start[::BQ] // BK)
        rows = rows_all[m].astype(jnp.float32)
        normed.append((rows * rms_factor(rows) * gain_one).astype(low))
        pre = dot_dims(w_qkv, normed[m], 0, 1)
        turned_q = rotate(pre[:cols], cos_table, sin_table) * HD ** -0.5
        turned_k = rotate(pre[cols : 2 * cols], cos_table, sin_table)
        qkv.append(jnp.concatenate([turned_q, turned_k, pre[2 * cols :]], axis=0).astype(low))
        out, log = attn_fwd(qkv[m], starts[m], lows[m])
        mixed.append(out)
        logs.append(log)
    mixed_own = [
        lax.all_to_all(mixed[m], "mp", split_axis=1, concat_axis=0, tiled=True)
        for m in range(batches)
    ]
    in_float = inputs.astype(jnp.float32).reshape(batches * tokens, width)
    mixed_both = jnp.concatenate(mixed_own, axis=1)
    hidden_in = in_float + dot_dims(mixed_both, output_full, 0, 0)
    factor_ffn = rms_factor(hidden_in)
    normed_ffn = (hidden_in * factor_ffn * gain_two).astype(low)
    gate_pre = dot_dims(normed_ffn, gate_full, 1, 1)
    up_pre = dot_dims(normed_ffn, up_full, 1, 1)
    sig_gate = jax.nn.sigmoid(gate_pre)
    silu_gate = gate_pre * sig_gate
    hidden = (silu_gate * up_pre).astype(low)
    result = (hidden_in + dot_dims(hidden, down_full, 1, 0)).astype(low)

    grad_top = cotangent.reshape(batches * tokens, width)
    grad_down = dot_dims(hidden, grad_top, 0, 0).astype(low)
    grad_hidden = dot_dims(grad_top, down_full, 1, 1)
    grad_gate_pre = (
        grad_hidden * up_pre * sig_gate * (1.0 + gate_pre * (1.0 - sig_gate))
    ).astype(low)
    grad_up_pre = (grad_hidden * silu_gate).astype(low)
    grad_gate = dot_dims(grad_gate_pre, normed_ffn, 0, 0).astype(low)
    grad_up = dot_dims(grad_up_pre, normed_ffn, 0, 0).astype(low)
    grad_normed_ffn = dot_dims(grad_gate_pre, gate_full, 1, 0) + dot_dims(
        grad_up_pre, up_full, 1, 0
    )
    grad_middle, gain_ffn_part = rms_back(hidden_in, factor_ffn, gain_two, grad_normed_ffn)
    grad_hidden_in = grad_top.astype(jnp.float32) + grad_middle
    grad_branch = grad_hidden_in.astype(low)
    grad_mixed = dot_dims(output_full, grad_branch, 1, 1).astype(low)
    grad_mixed_rows = [
        lax.all_to_all(
            grad_mixed[:, m * tokens : (m + 1) * tokens], "mp", split_axis=0, concat_axis=1,
            tiled=True,
        )
        for m in range(batches)
    ]
    grad_output = dot_dims(mixed_both, grad_branch, 1, 0).astype(low)

    def owned(partial_sum):
        return scatter(scatter(partial_sum, "dp", 1), "mp", 0).astype(jnp.float32)

    own_down, own_gate, own_up, own_output = (
        owned(g) for g in (grad_down, grad_gate, grad_up, grad_output)
    )

    grad_qkv, grad_normed = [], []
    for m in range(batches):
        cos_table, sin_table = tables[m]
        back = attn_bwd(
            qkv[m], grad_mixed_rows[m], mixed[m], logs[m], starts[m], lows[m], cos_table, sin_table
        ).reshape(3 * cols, n_mp * tokens)
        grad_qkv.append(back)
        grad_normed.append(scatter(dot_dims(back, w_qkv, 0, 1).astype(low), "mp", 0))
    grad_w = sum(dot_dims(normed[m], grad_qkv[m], 0, 1) for m in range(batches))
    own_qkv = scatter(grad_w.astype(low), "dp", 0).astype(jnp.float32)

    grad_normed_attn = jnp.concatenate(grad_normed, axis=0).astype(jnp.float32)
    grad_lower, gain_attn_part = rms_back(in_float, rms_factor(in_float), gain_one, grad_normed_attn)
    grad_inputs = (grad_hidden_in + grad_lower).astype(low)
    grad_norms = lax.psum_scatter(
        jnp.stack([gain_attn_part, gain_ffn_part]), ("dp", "mp"), scatter_dimension=1, tiled=True
    )
    return (
        result.reshape(inputs.shape),
        grad_inputs.reshape(inputs.shape),
        own_qkv[:, :cols],
        own_qkv[:, cols : 2 * cols],
        own_qkv[:, 2 * cols :],
        own_output,
        own_gate.T,
        own_up.T,
        own_down,
        grad_norms[0],
        grad_norms[1],
    )


def solution(mesh):
    row_spec = P(None, ("dp", "mp"), None)
    first, second = P("dp", "mp"), P("mp", "dp")
    both = P(("dp", "mp"))
    return jax.shard_map(
        local,
        mesh=mesh,
        in_specs=(
            row_spec, P(None, "dp", None), first, first, first, second, first, first, second,
            P("dp"), P("dp"), row_spec,
        ),
        out_specs=(
            row_spec, row_spec, first, first, first, second, first, first, second, both, both,
        ),
        check_vma=False,
    )
```

```python
import functools
import math

import jax
import jax.numpy as jnp
from jax import lax
from jax.experimental import pallas as pl
from jax.experimental.pallas import tpu as pltpu
from jax.sharding import PartitionSpec as P


HD = 64
BQ = 512
BK = 256
HPS = 2


def attn_fwd_kernel(lo_ref, q_ref, k_ref, v_ref, start_ref, o_ref, lse_ref, k_scr, *, bq, bk, heads):
    length = q_ref.shape[1]
    k_scr[...] = k_ref[...].T

    def q_step(qi, carry):
        q0 = pl.multiple_of(qi * bq, bq)
        qcols = pl.ds(q0, bq)
        q_blk = q_ref[:, qcols]
        start = start_ref[:, qcols]
        q_idx = q0 + lax.broadcasted_iota(jnp.int32, (1, bq), 1)

        def k_step(kb, state):
            k0 = pl.multiple_of(kb * bk, bk)
            k_idx = k0 + lax.broadcasted_iota(jnp.int32, (bk, bq), 0)
            allowed = (k_idx >= start) & (k_idx <= q_idx)
            out = []
            for h in range(heads):
                peak, total, acc = state[h]
                s = jnp.dot(k_scr[pl.ds(k0, bk), h * HD:(h + 1) * HD], q_blk[h * HD:(h + 1) * HD], preferred_element_type=jnp.float32)
                s = jnp.where(allowed, s, -1e30)
                new_peak = jnp.maximum(peak, jnp.max(s, axis=0, keepdims=True))
                p = jnp.exp(s - new_peak)
                fade = jnp.exp(peak - new_peak)
                total = total * fade + jnp.sum(p, axis=0, keepdims=True)
                acc = acc * fade + jnp.dot(v_ref[h * HD:(h + 1) * HD, pl.ds(k0, bk)], p.astype(jnp.bfloat16), preferred_element_type=jnp.float32)
                out.append((new_peak, total, acc))
            return tuple(out)

        init = tuple((jnp.full((1, bq), -1e30, jnp.float32), jnp.zeros((1, bq), jnp.float32), jnp.zeros((HD, bq), jnp.float32)) for _ in range(heads))
        hi = (q0 + bq - 1) // bk
        state = lax.fori_loop(lo_ref[qi], hi + 1, k_step, init)
        for h in range(heads):
            peak, total, acc = state[h]
            o_ref[h * HD:(h + 1) * HD, qcols] = (acc / total).astype(jnp.bfloat16)
            lse_ref[h, :, qcols] = peak + jnp.log(total)
        return carry

    lax.fori_loop(0, length // bq, q_step, 0)


def attn_bwd_kernel(lo_ref, q_ref, k_ref, v_ref, do_ref, o_ref, lse_ref, start_ref, cos_ref, sin_ref, out_ref, k_scr, v_scr, dk_scr, dv_scr, *, bq, bk, heads):
    length = q_ref.shape[1]
    k_scr[...] = k_ref[...].T
    v_scr[...] = v_ref[...].T
    dk_scr[...] = jnp.zeros_like(dk_scr)
    dv_scr[...] = jnp.zeros_like(dv_scr)
    half = HD // 2

    def unrotate(g, cos, sin):
        a, b = g[:half], g[half:]
        return jnp.concatenate([a * cos + b * sin, b * cos - a * sin], axis=0).astype(jnp.bfloat16)

    def q_step(qi, carry):
        q0 = pl.multiple_of(qi * bq, bq)
        qcols = pl.ds(q0, bq)
        q_blk = q_ref[:, qcols]
        do_blk = do_ref[:, qcols]
        q_t = q_blk.T
        do_t = do_blk.T
        prod = do_blk.astype(jnp.float32) * o_ref[:, qcols].astype(jnp.float32)
        start = start_ref[:, qcols]
        q_idx = q0 + lax.broadcasted_iota(jnp.int32, (1, bq), 1)
        deltas = [jnp.sum(prod[h * HD:(h + 1) * HD], axis=0, keepdims=True) for h in range(heads)]
        lses = [lse_ref[h, :, qcols] for h in range(heads)]

        def k_step(kb, state):
            k0 = pl.multiple_of(kb * bk, bk)
            rows = pl.ds(k0, bk)
            k_idx = k0 + lax.broadcasted_iota(jnp.int32, (bk, bq), 0)
            allowed = (k_idx >= start) & (k_idx <= q_idx)
            out = []
            for h in range(heads):
                hs = slice(h * HD, (h + 1) * HD)
                s = jnp.dot(k_scr[rows, hs], q_blk[hs], preferred_element_type=jnp.float32)
                p = jnp.exp(jnp.where(allowed, s - lses[h], -1e30))
                dp = jnp.dot(v_scr[rows, hs], do_blk[hs], preferred_element_type=jnp.float32)
                ds = (p * (dp - deltas[h])).astype(jnp.bfloat16)
                dv_scr[h, rows, :] += jnp.dot(p.astype(jnp.bfloat16), do_t[:, hs], preferred_element_type=jnp.float32)
                dk_scr[h, rows, :] += jnp.dot(ds, q_t[:, hs], preferred_element_type=jnp.float32)
                out.append(state[h] + jnp.dot(k_ref[hs, rows], ds, preferred_element_type=jnp.float32))
            return tuple(out)

        init = tuple(jnp.zeros((HD, bq), jnp.float32) for _ in range(heads))
        hi = (q0 + bq - 1) // bk
        state = lax.fori_loop(lo_ref[qi], hi + 1, k_step, init)
        cos, sin = cos_ref[:, qcols], sin_ref[:, qcols]
        for h in range(heads):
            out_ref[0, h * HD:(h + 1) * HD, qcols] = unrotate(state[h] * HD ** -0.5, cos, sin)
        return carry

    lax.fori_loop(0, length // bq, q_step, 0)
    for h in range(heads):
        out_ref[1, h * HD:(h + 1) * HD, :] = unrotate(dk_scr[h].T, cos_ref[...], sin_ref[...])
        out_ref[2, h * HD:(h + 1) * HD, :] = dv_scr[h].T.astype(jnp.bfloat16)


def attn_fwd(qkv_t, start, lo, bq=BQ, bk=BK, hps=HPS):
    cols3, length = qkv_t.shape
    cols = cols3 // 3
    steps = cols // (HD * hps)
    blk = (HD * hps, length)
    area = cols * length * length // 4
    return pl.pallas_call(
        functools.partial(attn_fwd_kernel, bq=bq, bk=bk, heads=hps),
        out_shape=(jax.ShapeDtypeStruct((cols, length), jnp.bfloat16), jax.ShapeDtypeStruct((cols // HD, 1, length), jnp.float32)),
        grid_spec=pltpu.PrefetchScalarGridSpec(
            num_scalar_prefetch=1, grid=(steps,),
            in_specs=[pl.BlockSpec(blk, lambda i, lo: (i, 0)), pl.BlockSpec(blk, lambda i, lo: (i + steps, 0)), pl.BlockSpec(blk, lambda i, lo: (i + 2 * steps, 0)),
                      pl.BlockSpec((1, length), lambda i, lo: (0, 0))],
            out_specs=[pl.BlockSpec(blk, lambda i, lo: (i, 0)), pl.BlockSpec((hps, 1, length), lambda i, lo: (i, 0, 0))],
            scratch_shapes=[pltpu.VMEM((length, HD * hps), jnp.bfloat16)]),
        cost_estimate=pl.CostEstimate(flops=16 * area, bytes_accessed=cols * length * 8, transcendentals=area // HD),
        name="attn_fwd",
    )(lo, qkv_t, qkv_t, qkv_t, start)


def attn_bwd(qkv_t, do_t, o_t, lse, start, lo, cos, sin, bq=BQ, bk=BK, hps=HPS):
    cols3, length = qkv_t.shape
    cols = cols3 // 3
    steps = cols // (HD * hps)
    blk = (HD * hps, length)
    area = cols * length * length // 4
    return pl.pallas_call(
        functools.partial(attn_bwd_kernel, bq=bq, bk=bk, heads=hps),
        out_shape=jax.ShapeDtypeStruct((3, cols, length), jnp.bfloat16),
        grid_spec=pltpu.PrefetchScalarGridSpec(
            num_scalar_prefetch=1, grid=(steps,),
            in_specs=[pl.BlockSpec(blk, lambda i, lo: (i, 0)), pl.BlockSpec(blk, lambda i, lo: (i + steps, 0)), pl.BlockSpec(blk, lambda i, lo: (i + 2 * steps, 0)),
                      pl.BlockSpec(blk, lambda i, lo: (i, 0)), pl.BlockSpec(blk, lambda i, lo: (i, 0)),
                      pl.BlockSpec((hps, 1, length), lambda i, lo: (i, 0, 0)),
                      pl.BlockSpec((1, length), lambda i, lo: (0, 0)),
                      pl.BlockSpec((HD // 2, length), lambda i, lo: (0, 0)), pl.BlockSpec((HD // 2, length), lambda i, lo: (0, 0))],
            out_specs=pl.BlockSpec((3,) + blk, lambda i, lo: (0, i, 0)),
            scratch_shapes=[pltpu.VMEM((length, HD * hps), jnp.bfloat16)] * 2 + [pltpu.VMEM((hps, length, HD), jnp.float32)] * 2),
        cost_estimate=pl.CostEstimate(flops=40 * area, bytes_accessed=cols * length * 20, transcendentals=area // HD),
        name="attn_bwd",
    )(lo, qkv_t, qkv_t, qkv_t, do_t, o_t, lse, start, cos, sin)


eps_norm = 1e-05


def dot_dims(left, right, left_dim, right_dim):
    return lax.dot_general(
        left, right, (((left_dim,), (right_dim,)), ((), ())), preferred_element_type=jnp.float32
    )


def row_starts(seg_row):
    ones = [jnp.sum((seg_row < s).astype(jnp.int32)) for s in (1, 2, 3)]
    start = jnp.zeros_like(seg_row)
    before = 0
    for s, count in zip((1, 2, 3), ones):
        start = start + jnp.where(seg_row >= s, count - before, 0)
        before = count
    return start


def rope_tables(start):
    half_dim = HD // 2
    offsets = (jnp.arange(start.shape[0], dtype=jnp.int32) - start).astype(jnp.float32)
    frequency = jnp.exp(jnp.arange(half_dim, dtype=jnp.float32) * (-math.log(10000.0) / half_dim))
    angles = frequency[:, None] * offsets[None, :]
    return jnp.cos(angles), jnp.sin(angles)


def rotate(rows, cos_table, sin_table):
    count, length = rows.shape
    parts = rows.reshape(count // HD, 2, HD // 2, length)
    low, high = parts[:, 0], parts[:, 1]
    turned = jnp.stack(
        [low * cos_table - high * sin_table, high * cos_table + low * sin_table], axis=1
    )
    return turned.reshape(count, length)


def rms_factor(values):
    return lax.rsqrt(jnp.mean(values * values, axis=-1, keepdims=True) + eps_norm)


def rms_back(values_in, factor, gain, grad_normed):
    scaled = grad_normed * gain
    gain_part = jnp.sum(grad_normed * values_in * factor, axis=0)
    inner = jnp.mean(scaled * values_in, axis=-1, keepdims=True)
    return factor * scaled - values_in * (factor * factor * factor) * inner, gain_part


def scatter(partial_sum, axis, dim):
    return lax.psum_scatter(partial_sum, axis, scatter_dimension=dim, tiled=True)


def line_steps(count):
    near_right = [(i, i + 1) for i in range(count - 1)]
    near_left = [(i, i - 1) for i in range(1, count)]
    return near_right, near_left


def line_gather(piece, axis, hold=lambda *arrays: arrays):
    count, me = lax.axis_size(axis), lax.axis_index(axis)
    assert count == 4
    near_right, near_left = line_steps(count)
    one_left = lax.ppermute(piece, axis, near_right)
    one_right = lax.ppermute(piece, axis, near_left)
    one_left, one_right = hold(one_left, one_right)
    two_left = lax.ppermute(one_left, axis, [(1, 2), (2, 3)])
    two_right = lax.ppermute(one_right, axis, [(1, 0), (2, 1)])
    three_left = lax.ppermute(one_left, axis, [(1, 3)])
    three_right = lax.ppermute(one_right, axis, [(2, 0)])
    slots = jnp.concatenate(
        [three_left, two_left, one_left, piece, one_right, two_right, three_right], axis=0
    )
    rows = piece.shape[0]
    return lax.dynamic_slice_in_dim(slots, (count - 1 - me) * rows, count * rows, axis=0)


def line_scatter(partial_sum, axis):
    count, me = lax.axis_size(axis), lax.axis_index(axis)
    assert count == 4
    rows = partial_sum.shape[0] // count
    near_right, near_left = line_steps(count)

    def block(offset):
        first = jnp.clip(me + offset, 0, count - 1) * rows
        return lax.dynamic_slice_in_dim(partial_sum, first, rows, axis=0)

    two_right = lax.ppermute(block(2), axis, [(0, 1), (1, 2)])
    two_left = lax.ppermute(block(-2), axis, [(3, 2), (2, 1)])
    three_right = lax.ppermute(block(3), axis, [(0, 2)])
    three_left = lax.ppermute(block(-3), axis, [(3, 1)])

    def total(*parts):
        return sum(part.astype(jnp.float32) for part in parts)

    right = lax.ppermute(
        total(block(1), two_right, three_right).astype(jnp.bfloat16), axis, near_right
    )
    left = lax.ppermute(
        total(block(-1), two_left, three_left).astype(jnp.bfloat16), axis, near_left
    )
    return total(block(0), right, left)


def exchange_sum(partial_sum, axis):
    count = lax.axis_size(axis)
    parts = partial_sum.reshape((count, partial_sum.shape[0] // count) + partial_sum.shape[1:])
    swapped = lax.all_to_all(parts, axis, split_axis=0, concat_axis=0, tiled=True)
    return jnp.sum(swapped.astype(jnp.float32), axis=0)


def local(
    inputs, segments, w_query, w_key, w_value, w_output, w_gate, w_up, w_down,
    gain_attn, gain_ffn, cotangent,
):
    low = jnp.bfloat16
    n_dp, n_mp = lax.axis_size("dp"), lax.axis_size("mp")
    batches, tokens, width = inputs.shape
    cols = w_query.shape[1]
    depth = w_query.shape[0]

    def split16(gain):
        high = gain.astype(low)
        return high, (gain - high.astype(jnp.float32)).astype(low)

    pieces = split16(gain_attn) + split16(gain_ffn)
    gain_row = jnp.concatenate(pieces + (jnp.zeros((3 * cols - 4 * depth,), low),))
    qkv_piece = jnp.concatenate(
        [
            jnp.concatenate([w_query, w_key, w_value], axis=1),
            jnp.pad(gain_row[None], ((0, 15), (0, 0))),
        ],
        axis=0,
    )
    qkv_all = lax.all_gather(qkv_piece, "dp", axis=0, tiled=False)
    w_qkv = qkv_all[:, :depth].reshape(width, 3 * cols)
    gains = qkv_all[:, depth, : 4 * depth].astype(jnp.float32).reshape(n_dp, 4, depth)
    gain_one = (gains[:, 0] + gains[:, 1]).reshape(width)
    gain_two = (gains[:, 2] + gains[:, 3]).reshape(width)

    first_rows = line_gather(inputs[0], "mp")
    first_rows, second_piece, w_output, gate_t, up_t, w_down = lax.optimization_barrier(
        (first_rows, inputs[1], w_output, w_gate.T, w_up.T, w_down)
    )
    rows_all = [first_rows, None]

    def whole(piece):
        every = lax.all_gather(piece, ("dp", "mp"), axis=0, tiled=False)
        every = every.reshape((n_dp, n_mp) + piece.shape)
        return every.transpose(1, 2, 0, 3).reshape(n_mp * piece.shape[0], width)

    output_full, gate_full, up_full, down_full = (
        whole(piece) for piece in (w_output, gate_t, up_t, w_down)
    )

    normed, factors, qkv, tables, starts, lows, mixed, logs = [], [], [], [], [], [], [], []
    for m in range(batches):
        start = row_starts(segments[m, 0])
        cos_table, sin_table = rope_tables(start)
        tables.append((cos_table, sin_table))
        starts.append(start[None])
        lows.append(start[::BQ] // BK)
        if m == 1:
            def after_first(left, right):
                left, right, mixed[0] = lax.optimization_barrier((left, right, mixed[0]))
                return left, right

            rows_all[1] = line_gather(second_piece, "mp", after_first)
        rows = rows_all[m].astype(jnp.float32)
        factors.append(rms_factor(rows))
        normed.append((rows * factors[m] * gain_one).astype(low))
        pre = dot_dims(w_qkv, normed[m], 0, 1)
        turned_q = rotate(pre[:cols], cos_table, sin_table) * HD ** -0.5
        turned_k = rotate(pre[cols : 2 * cols], cos_table, sin_table)
        qkv.append(jnp.concatenate([turned_q, turned_k, pre[2 * cols :]], axis=0).astype(low))
        out, log = attn_fwd(qkv[m], starts[m], lows[m])
        mixed.append(out)
        logs.append(log)
    mixed_own = [
        lax.all_to_all(mixed[m], "mp", split_axis=1, concat_axis=0, tiled=True)
        for m in range(batches)
    ]
    in_float = inputs.astype(jnp.float32).reshape(batches * tokens, width)
    mixed_both = jnp.concatenate(mixed_own, axis=1)
    hidden_in = in_float + dot_dims(mixed_both, output_full, 0, 0)
    factor_ffn = rms_factor(hidden_in)
    normed_ffn = (hidden_in * factor_ffn * gain_two).astype(low)
    gate_pre = dot_dims(normed_ffn, gate_full, 1, 1)
    up_pre = dot_dims(normed_ffn, up_full, 1, 1)
    sig_gate = jax.nn.sigmoid(gate_pre)
    silu_gate = gate_pre * sig_gate
    hidden = (silu_gate * up_pre).astype(low)
    result = (hidden_in + dot_dims(hidden, down_full, 1, 0)).astype(low)

    grad_top = cotangent.reshape(batches * tokens, width)
    grad_down = dot_dims(grad_top, hidden, 0, 0).astype(low)
    grad_hidden = dot_dims(grad_top, down_full, 1, 1)
    grad_gate_pre = (
        grad_hidden * up_pre * sig_gate * (1.0 + gate_pre * (1.0 - sig_gate))
    ).astype(low)
    grad_up_pre = (grad_hidden * silu_gate).astype(low)
    grad_gate = dot_dims(normed_ffn, grad_gate_pre, 0, 0).astype(low)
    grad_up = dot_dims(normed_ffn, grad_up_pre, 0, 0).astype(low)
    grad_normed_ffn = dot_dims(grad_gate_pre, gate_full, 1, 0) + dot_dims(
        grad_up_pre, up_full, 1, 0
    )
    grad_middle, gain_ffn_part = rms_back(hidden_in, factor_ffn, gain_two, grad_normed_ffn)
    grad_hidden_in = grad_top.astype(jnp.float32) + grad_middle
    grad_branch = grad_hidden_in.astype(low)
    grad_mixed = dot_dims(output_full, grad_branch, 1, 1).astype(low)
    grad_mixed_rows = []
    for m in range(batches):
        grad_mixed_rows.append(
            lax.all_to_all(
                grad_mixed[:, m * tokens : (m + 1) * tokens], "mp", split_axis=0,
                concat_axis=1, tiled=True,
            )
        )
    grad_output = dot_dims(grad_branch, mixed_both, 0, 1).astype(low)
    grad_mixed_rows[0], grad_down, grad_gate, grad_up, grad_output = lax.optimization_barrier(
        (grad_mixed_rows[0], grad_down, grad_gate, grad_up, grad_output)
    )

    mine = [scatter(g, "dp", 0) for g in (grad_down, grad_gate, grad_up, grad_output)]


    grad_qkv, grad_normed = [], []
    gain_attn_part = jnp.zeros((width,), jnp.float32)
    for m in range(batches):
        cos_table, sin_table = tables[m]
        back = attn_bwd(
            qkv[m], grad_mixed_rows[m], mixed[m], logs[m], starts[m], lows[m], cos_table,
            sin_table,
        ).reshape(3 * cols, n_mp * tokens)
        grad_qkv.append(back)
        spread = dot_dims(back, w_qkv, 0, 1).astype(low)
        if m == 0:
            spread, grad_mixed_rows[1] = lax.optimization_barrier((spread, grad_mixed_rows[1]))
        grad_normed.append(line_scatter(spread, "mp"))
        gain_attn_part = gain_attn_part + jnp.sum(
            spread.astype(jnp.float32) * rows_all[m].astype(jnp.float32) * factors[m], axis=0
        )
    grad_w = sum(dot_dims(normed[m], grad_qkv[m], 0, 1) for m in range(batches))

    def owned(part):
        parts = part.reshape(depth, n_mp, -1).transpose(1, 0, 2)
        return scatter(parts, "mp", 0)[0].astype(jnp.float32)

    own_down, own_gate, own_up, own_output = (owned(part) for part in mine)
    own_qkv = exchange_sum(grad_w.astype(low), "dp")

    grad_normed_attn = jnp.concatenate(grad_normed, axis=0)
    grad_lower, _ = rms_back(in_float, rms_factor(in_float), gain_one, grad_normed_attn)
    grad_inputs = (grad_hidden_in + grad_lower).astype(low)
    grad_norms = exchange_sum(jnp.stack([gain_attn_part, gain_ffn_part], axis=1), ("dp", "mp")).T
    return (
        result.reshape(inputs.shape),
        grad_inputs.reshape(inputs.shape),
        own_qkv[:, :cols],
        own_qkv[:, cols : 2 * cols],
        own_qkv[:, 2 * cols :],
        own_output.T,
        own_gate,
        own_up,
        own_down.T,
        grad_norms[0],
        grad_norms[1],
    )


def solution(mesh):
    row_spec = P(None, ("dp", "mp"), None)
    first, second = P("dp", "mp"), P("mp", "dp")
    both = P(("dp", "mp"))

    return jax.shard_map(
        local,
        mesh=mesh,
        in_specs=(
            row_spec, P(None, "dp", None), first, first, first, second, first, first, second,
            P("dp"), P("dp"), row_spec,
        ),
        out_specs=(
            row_spec, row_spec, first, first, first, second, first, first, second, both, both,
        ),
        check_vma=False,
    )
```

```python
import functools
import math

import jax
import jax.numpy as jnp
from jax import lax
from jax.experimental import pallas as pl
from jax.experimental.pallas import tpu as pltpu
from jax.sharding import PartitionSpec as P


HD = 64
BQ = 512
BK = 256
HPS = 2


def attn_fwd_kernel(lo_ref, q_ref, k_ref, v_ref, start_ref, o_ref, lse_ref, k_scr, *, bq, bk, heads):
    length = q_ref.shape[1]
    k_scr[...] = k_ref[...].T

    def q_step(qi, carry):
        q0 = pl.multiple_of(qi * bq, bq)
        qcols = pl.ds(q0, bq)
        q_blk = q_ref[:, qcols]
        start = start_ref[:, qcols]
        q_idx = q0 + lax.broadcasted_iota(jnp.int32, (1, bq), 1)

        def k_step(kb, state):
            k0 = pl.multiple_of(kb * bk, bk)
            k_idx = k0 + lax.broadcasted_iota(jnp.int32, (bk, bq), 0)
            allowed = (k_idx >= start) & (k_idx <= q_idx)
            out = []
            for h in range(heads):
                peak, total, acc = state[h]
                s = jnp.dot(k_scr[pl.ds(k0, bk), h * HD:(h + 1) * HD], q_blk[h * HD:(h + 1) * HD], preferred_element_type=jnp.float32)
                s = jnp.where(allowed, s, -1e30)
                new_peak = jnp.maximum(peak, jnp.max(s, axis=0, keepdims=True))
                p = jnp.exp(s - new_peak)
                fade = jnp.exp(peak - new_peak)
                total = total * fade + jnp.sum(p, axis=0, keepdims=True)
                acc = acc * fade + jnp.dot(v_ref[h * HD:(h + 1) * HD, pl.ds(k0, bk)], p.astype(jnp.bfloat16), preferred_element_type=jnp.float32)
                out.append((new_peak, total, acc))
            return tuple(out)

        init = tuple((jnp.full((1, bq), -1e30, jnp.float32), jnp.zeros((1, bq), jnp.float32), jnp.zeros((HD, bq), jnp.float32)) for _ in range(heads))
        hi = (q0 + bq - 1) // bk
        state = lax.fori_loop(lo_ref[qi], hi + 1, k_step, init)
        for h in range(heads):
            peak, total, acc = state[h]
            o_ref[h * HD:(h + 1) * HD, qcols] = (acc / total).astype(jnp.bfloat16)
            lse_ref[h, :, qcols] = peak + jnp.log(total)
        return carry

    lax.fori_loop(0, length // bq, q_step, 0)


def attn_bwd_kernel(lo_ref, q_ref, k_ref, v_ref, do_ref, o_ref, lse_ref, start_ref, cos_ref, sin_ref, out_ref, k_scr, v_scr, dk_scr, dv_scr, *, bq, bk, heads):
    length = q_ref.shape[1]
    k_scr[...] = k_ref[...].T
    v_scr[...] = v_ref[...].T
    dk_scr[...] = jnp.zeros_like(dk_scr)
    dv_scr[...] = jnp.zeros_like(dv_scr)
    half = HD // 2

    def unrotate(g, cos, sin):
        a, b = g[:half], g[half:]
        return jnp.concatenate([a * cos + b * sin, b * cos - a * sin], axis=0).astype(jnp.bfloat16)

    def q_step(qi, carry):
        q0 = pl.multiple_of(qi * bq, bq)
        qcols = pl.ds(q0, bq)
        q_blk = q_ref[:, qcols]
        do_blk = do_ref[:, qcols]
        q_t = q_blk.T
        do_t = do_blk.T
        prod = do_blk.astype(jnp.float32) * o_ref[:, qcols].astype(jnp.float32)
        start = start_ref[:, qcols]
        q_idx = q0 + lax.broadcasted_iota(jnp.int32, (1, bq), 1)
        deltas = [jnp.sum(prod[h * HD:(h + 1) * HD], axis=0, keepdims=True) for h in range(heads)]
        lses = [lse_ref[h, :, qcols] for h in range(heads)]

        def k_step(kb, state):
            k0 = pl.multiple_of(kb * bk, bk)
            rows = pl.ds(k0, bk)
            k_idx = k0 + lax.broadcasted_iota(jnp.int32, (bk, bq), 0)
            allowed = (k_idx >= start) & (k_idx <= q_idx)
            out = []
            for h in range(heads):
                hs = slice(h * HD, (h + 1) * HD)
                s = jnp.dot(k_scr[rows, hs], q_blk[hs], preferred_element_type=jnp.float32)
                p = jnp.exp(jnp.where(allowed, s - lses[h], -1e30))
                dp = jnp.dot(v_scr[rows, hs], do_blk[hs], preferred_element_type=jnp.float32)
                ds = (p * (dp - deltas[h])).astype(jnp.bfloat16)
                dv_scr[h, rows, :] += jnp.dot(p.astype(jnp.bfloat16), do_t[:, hs], preferred_element_type=jnp.float32)
                dk_scr[h, rows, :] += jnp.dot(ds, q_t[:, hs], preferred_element_type=jnp.float32)
                out.append(state[h] + jnp.dot(k_ref[hs, rows], ds, preferred_element_type=jnp.float32))
            return tuple(out)

        init = tuple(jnp.zeros((HD, bq), jnp.float32) for _ in range(heads))
        hi = (q0 + bq - 1) // bk
        state = lax.fori_loop(lo_ref[qi], hi + 1, k_step, init)
        cos, sin = cos_ref[:, qcols], sin_ref[:, qcols]
        for h in range(heads):
            out_ref[0, h * HD:(h + 1) * HD, qcols] = unrotate(state[h] * HD ** -0.5, cos, sin)
        return carry

    lax.fori_loop(0, length // bq, q_step, 0)
    for h in range(heads):
        out_ref[1, h * HD:(h + 1) * HD, :] = unrotate(dk_scr[h].T, cos_ref[...], sin_ref[...])
        out_ref[2, h * HD:(h + 1) * HD, :] = dv_scr[h].T.astype(jnp.bfloat16)


def attn_fwd(qkv_t, start, lo, bq=BQ, bk=BK, hps=HPS):
    cols3, length = qkv_t.shape
    cols = cols3 // 3
    steps = cols // (HD * hps)
    blk = (HD * hps, length)
    area = cols * length * length // 4
    return pl.pallas_call(
        functools.partial(attn_fwd_kernel, bq=bq, bk=bk, heads=hps),
        out_shape=(jax.ShapeDtypeStruct((cols, length), jnp.bfloat16), jax.ShapeDtypeStruct((cols // HD, 1, length), jnp.float32)),
        grid_spec=pltpu.PrefetchScalarGridSpec(
            num_scalar_prefetch=1, grid=(steps,),
            in_specs=[pl.BlockSpec(blk, lambda i, lo: (i, 0)), pl.BlockSpec(blk, lambda i, lo: (i + steps, 0)), pl.BlockSpec(blk, lambda i, lo: (i + 2 * steps, 0)),
                      pl.BlockSpec((1, length), lambda i, lo: (0, 0))],
            out_specs=[pl.BlockSpec(blk, lambda i, lo: (i, 0)), pl.BlockSpec((hps, 1, length), lambda i, lo: (i, 0, 0))],
            scratch_shapes=[pltpu.VMEM((length, HD * hps), jnp.bfloat16)]),
        cost_estimate=pl.CostEstimate(flops=16 * area, bytes_accessed=cols * length * 8, transcendentals=area // HD),
        name="attn_fwd",
    )(lo, qkv_t, qkv_t, qkv_t, start)


def attn_bwd(qkv_t, do_t, o_t, lse, start, lo, cos, sin, bq=BQ, bk=BK, hps=HPS):
    cols3, length = qkv_t.shape
    cols = cols3 // 3
    steps = cols // (HD * hps)
    blk = (HD * hps, length)
    area = cols * length * length // 4
    return pl.pallas_call(
        functools.partial(attn_bwd_kernel, bq=bq, bk=bk, heads=hps),
        out_shape=jax.ShapeDtypeStruct((3, cols, length), jnp.bfloat16),
        grid_spec=pltpu.PrefetchScalarGridSpec(
            num_scalar_prefetch=1, grid=(steps,),
            in_specs=[pl.BlockSpec(blk, lambda i, lo: (i, 0)), pl.BlockSpec(blk, lambda i, lo: (i + steps, 0)), pl.BlockSpec(blk, lambda i, lo: (i + 2 * steps, 0)),
                      pl.BlockSpec(blk, lambda i, lo: (i, 0)), pl.BlockSpec(blk, lambda i, lo: (i, 0)),
                      pl.BlockSpec((hps, 1, length), lambda i, lo: (i, 0, 0)),
                      pl.BlockSpec((1, length), lambda i, lo: (0, 0)),
                      pl.BlockSpec((HD // 2, length), lambda i, lo: (0, 0)), pl.BlockSpec((HD // 2, length), lambda i, lo: (0, 0))],
            out_specs=pl.BlockSpec((3,) + blk, lambda i, lo: (0, i, 0)),
            scratch_shapes=[pltpu.VMEM((length, HD * hps), jnp.bfloat16)] * 2 + [pltpu.VMEM((hps, length, HD), jnp.float32)] * 2),
        cost_estimate=pl.CostEstimate(flops=40 * area, bytes_accessed=cols * length * 20, transcendentals=area // HD),
        name="attn_bwd",
    )(lo, qkv_t, qkv_t, qkv_t, do_t, o_t, lse, start, cos, sin)


eps_norm = 1e-05


def dot_dims(left, right, left_dim, right_dim):
    return lax.dot_general(
        left, right, (((left_dim,), (right_dim,)), ((), ())), preferred_element_type=jnp.float32
    )


def row_starts(seg_row):
    ones = [jnp.sum((seg_row < s).astype(jnp.int32)) for s in (1, 2, 3)]
    start = jnp.zeros_like(seg_row)
    before = 0
    for s, count in zip((1, 2, 3), ones):
        start = start + jnp.where(seg_row >= s, count - before, 0)
        before = count
    return start


def rope_tables(start):
    half_dim = HD // 2
    offsets = (jnp.arange(start.shape[0], dtype=jnp.int32) - start).astype(jnp.float32)
    frequency = jnp.exp(jnp.arange(half_dim, dtype=jnp.float32) * (-math.log(10000.0) / half_dim))
    angles = frequency[:, None] * offsets[None, :]
    return jnp.cos(angles), jnp.sin(angles)


def rotate(rows, cos_table, sin_table):
    count, length = rows.shape
    parts = rows.reshape(count // HD, 2, HD // 2, length)
    low, high = parts[:, 0], parts[:, 1]
    turned = jnp.stack(
        [low * cos_table - high * sin_table, high * cos_table + low * sin_table], axis=1
    )
    return turned.reshape(count, length)


def rms_factor(values):
    return lax.rsqrt(jnp.mean(values * values, axis=-1, keepdims=True) + eps_norm)


def rms_back(values_in, factor, gain, grad_normed):
    scaled = grad_normed * gain
    gain_part = jnp.sum(grad_normed * values_in * factor, axis=0)
    inner = jnp.mean(scaled * values_in, axis=-1, keepdims=True)
    return factor * scaled - values_in * (factor * factor * factor) * inner, gain_part


def scatter(partial_sum, axis, dim):
    return lax.psum_scatter(partial_sum, axis, scatter_dimension=dim, tiled=True)


def line_steps(count):
    near_right = [(i, i + 1) for i in range(count - 1)]
    near_left = [(i, i - 1) for i in range(1, count)]
    return near_right, near_left


def line_gather(piece, axis, hold=lambda *arrays: arrays):
    count, me = lax.axis_size(axis), lax.axis_index(axis)
    assert count == 4
    near_right, near_left = line_steps(count)
    one_left = lax.ppermute(piece, axis, near_right)
    one_right = lax.ppermute(piece, axis, near_left)
    one_left, one_right = hold(one_left, one_right)
    two_left = lax.ppermute(one_left, axis, [(1, 2), (2, 3)])
    two_right = lax.ppermute(one_right, axis, [(1, 0), (2, 1)])
    three_left = lax.ppermute(one_left, axis, [(1, 3)])
    three_right = lax.ppermute(one_right, axis, [(2, 0)])
    slots = jnp.concatenate(
        [three_left, two_left, one_left, piece, one_right, two_right, three_right], axis=0
    )
    rows = piece.shape[0]
    return lax.dynamic_slice_in_dim(slots, (count - 1 - me) * rows, count * rows, axis=0)


def line_scatter(partial_sum, axis):
    count, me = lax.axis_size(axis), lax.axis_index(axis)
    assert count == 4
    rows = partial_sum.shape[0] // count
    near_right, near_left = line_steps(count)

    def block(offset):
        first = jnp.clip(me + offset, 0, count - 1) * rows
        return lax.dynamic_slice_in_dim(partial_sum, first, rows, axis=0)

    two_right = lax.ppermute(block(2), axis, [(0, 1), (1, 2)])
    two_left = lax.ppermute(block(-2), axis, [(3, 2), (2, 1)])
    three_right = lax.ppermute(block(3), axis, [(0, 2)])
    three_left = lax.ppermute(block(-3), axis, [(3, 1)])

    def total(*parts):
        return sum(part.astype(jnp.float32) for part in parts)

    right = lax.ppermute(
        total(block(1), two_right, three_right).astype(jnp.bfloat16), axis, near_right
    )
    left = lax.ppermute(
        total(block(-1), two_left, three_left).astype(jnp.bfloat16), axis, near_left
    )
    return total(block(0), right, left)


def plane_gather(piece, axis):
    core, across, along = ([(i, i ^ bit) for i in range(8)] for bit in (1, 2, 4))
    half = piece.shape[0] // 2
    top, low = piece[:half], piece[half:]

    def partner(part):
        return lax.ppermute(part, axis, core)

    top_x, low_y = lax.ppermute(top, axis, across), lax.ppermute(low, axis, along)
    top_y, low_x = lax.ppermute(top, axis, along), lax.ppermute(low, axis, across)
    top_xy, low_xy = lax.ppermute(top_x, axis, along), lax.ppermute(low_y, axis, across)
    held = [(top, low), (top_x, low_x), (top_y, low_y), (top_xy, low_xy)]
    parts = []
    for pair in held:
        parts += [pair, tuple(partner(part) for part in pair)]

    def ordered(me):
        def branch(*flat):
            lanes = [
                jnp.concatenate([flat[2 * (i ^ me)], flat[2 * (i ^ me) + 1]], axis=0)
                for i in range(8)
            ]
            return jnp.concatenate(lanes, axis=1)

        return branch

    flat = [part for pair in parts for part in pair]
    return lax.switch(lax.axis_index(axis), [ordered(me) for me in range(8)], *flat)


def exchange_sum(partial_sum, axis):
    count = lax.axis_size(axis)
    parts = partial_sum.reshape((count, partial_sum.shape[0] // count) + partial_sum.shape[1:])
    swapped = lax.all_to_all(parts, axis, split_axis=0, concat_axis=0, tiled=True)
    return jnp.sum(swapped.astype(jnp.float32), axis=0)


def local(
    inputs, segments, w_query, w_key, w_value, w_output, w_gate, w_up, w_down,
    gain_attn, gain_ffn, cotangent,
):
    low = jnp.bfloat16
    n_dp, n_mp = lax.axis_size("dp"), lax.axis_size("mp")
    batches, tokens, width = inputs.shape
    cols = w_query.shape[1]
    depth = w_query.shape[0]
    hidden_part = w_gate.shape[1]

    def split16(gain):
        high = gain.astype(low)
        return high, (gain - high.astype(jnp.float32)).astype(low)

    pieces = split16(gain_attn) + split16(gain_ffn)
    gain_row = jnp.concatenate(pieces + (jnp.zeros((3 * cols - 4 * depth,), low),))
    qkv_piece = jnp.concatenate(
        [
            jnp.concatenate([w_query, w_key, w_value], axis=1),
            jnp.pad(gain_row[None], ((0, 15), (0, 0))),
        ],
        axis=0,
    )
    qkv_all = lax.all_gather(qkv_piece, "dp", axis=0, tiled=False)
    w_qkv = qkv_all[:, :depth].reshape(width, 3 * cols)
    gains = qkv_all[:, depth, : 4 * depth].astype(jnp.float32).reshape(n_dp, 4, depth)
    gain_one = (gains[:, 0] + gains[:, 1]).reshape(width)
    gain_two = (gains[:, 2] + gains[:, 3]).reshape(width)

    rest_piece = jnp.concatenate([w_output, w_gate.T, w_up.T, w_down], axis=0)
    sizes = (cols, hidden_part, hidden_part, hidden_part)
    firsts = (0, cols, cols + hidden_part, cols + 2 * hidden_part)
    if n_dp == 8:
        rest_every = plane_gather(line_gather(rest_piece, "mp"), "dp")
        rest_every = rest_every.reshape(n_mp, rest_piece.shape[0], width)
    else:
        rest_every = lax.all_gather(rest_piece, ("dp", "mp"), axis=0, tiled=False)
        rest_every = rest_every.reshape((n_dp, n_mp) + rest_piece.shape).transpose(1, 2, 0, 3)
        rest_every = rest_every.reshape(n_mp, rest_piece.shape[0], width)
    output_full, gate_full, up_full, down_full = (
        rest_every[:, first : first + size].reshape(n_mp * size, width)
        for first, size in zip(firsts, sizes)
    )

    first_rows = line_gather(inputs[0], "mp")
    first_rows, second_piece = lax.optimization_barrier((first_rows, inputs[1]))
    rows_all = [first_rows, None]

    normed, factors, qkv, tables, starts, lows, mixed, logs = [], [], [], [], [], [], [], []
    for m in range(batches):
        start = row_starts(segments[m, 0])
        cos_table, sin_table = rope_tables(start)
        tables.append((cos_table, sin_table))
        starts.append(start[None])
        lows.append(start[::BQ] // BK)
        if m == 1:
            def after_first(left, right):
                left, right, mixed[0] = lax.optimization_barrier((left, right, mixed[0]))
                return left, right

            rows_all[1] = line_gather(second_piece, "mp", after_first)
        rows = rows_all[m].astype(jnp.float32)
        factors.append(rms_factor(rows))
        normed.append((rows * factors[m] * gain_one).astype(low))
        pre = dot_dims(w_qkv, normed[m], 0, 1)
        turned_q = rotate(pre[:cols], cos_table, sin_table) * HD ** -0.5
        turned_k = rotate(pre[cols : 2 * cols], cos_table, sin_table)
        qkv.append(jnp.concatenate([turned_q, turned_k, pre[2 * cols :]], axis=0).astype(low))
        out, log = attn_fwd(qkv[m], starts[m], lows[m])
        mixed.append(out)
        logs.append(log)
    mixed_own = [
        lax.all_to_all(mixed[m], "mp", split_axis=1, concat_axis=0, tiled=True)
        for m in range(batches)
    ]
    in_float = inputs.astype(jnp.float32).reshape(batches * tokens, width)
    mixed_both = jnp.concatenate(mixed_own, axis=1)
    hidden_in = in_float + dot_dims(mixed_both, output_full, 0, 0)
    factor_ffn = rms_factor(hidden_in)
    normed_ffn = (hidden_in * factor_ffn * gain_two).astype(low)
    gate_pre = dot_dims(normed_ffn, gate_full, 1, 1)
    up_pre = dot_dims(normed_ffn, up_full, 1, 1)
    sig_gate = jax.nn.sigmoid(gate_pre)
    silu_gate = gate_pre * sig_gate
    hidden = (silu_gate * up_pre).astype(low)
    result = (hidden_in + dot_dims(hidden, down_full, 1, 0)).astype(low)

    grad_top = cotangent.reshape(batches * tokens, width)
    grad_down = dot_dims(grad_top, hidden, 0, 0).astype(low)
    grad_hidden = dot_dims(grad_top, down_full, 1, 1)
    grad_gate_pre = (
        grad_hidden * up_pre * sig_gate * (1.0 + gate_pre * (1.0 - sig_gate))
    ).astype(low)
    grad_up_pre = (grad_hidden * silu_gate).astype(low)
    grad_gate = dot_dims(normed_ffn, grad_gate_pre, 0, 0).astype(low)
    grad_up = dot_dims(normed_ffn, grad_up_pre, 0, 0).astype(low)
    grad_normed_ffn = dot_dims(grad_gate_pre, gate_full, 1, 0) + dot_dims(
        grad_up_pre, up_full, 1, 0
    )
    grad_middle, gain_ffn_part = rms_back(hidden_in, factor_ffn, gain_two, grad_normed_ffn)
    grad_hidden_in = grad_top.astype(jnp.float32) + grad_middle
    grad_branch = grad_hidden_in.astype(low)
    grad_mixed = dot_dims(output_full, grad_branch, 1, 1).astype(low)
    grad_mixed_rows = []
    for m in range(batches):
        grad_mixed_rows.append(
            lax.all_to_all(
                grad_mixed[:, m * tokens : (m + 1) * tokens], "mp", split_axis=0,
                concat_axis=1, tiled=True,
            )
        )
    grad_output = dot_dims(grad_branch, mixed_both, 0, 1).astype(low)

    every_grad = jnp.concatenate([grad_output, grad_gate, grad_up, grad_down], axis=1)
    grad_mixed_rows[0], every_grad = lax.optimization_barrier((grad_mixed_rows[0], every_grad))
    mine = scatter(every_grad, "dp", 0)


    grad_qkv, grad_normed = [], []
    gain_attn_part = jnp.zeros((width,), jnp.float32)
    for m in range(batches):
        cos_table, sin_table = tables[m]
        back = attn_bwd(
            qkv[m], grad_mixed_rows[m], mixed[m], logs[m], starts[m], lows[m], cos_table,
            sin_table,
        ).reshape(3 * cols, n_mp * tokens)
        grad_qkv.append(back)
        spread = dot_dims(back, w_qkv, 0, 1).astype(low)
        if m == 0:
            spread, grad_mixed_rows[1] = lax.optimization_barrier((spread, grad_mixed_rows[1]))
        grad_normed.append(line_scatter(spread, "mp"))
        gain_attn_part = gain_attn_part + jnp.sum(
            spread.astype(jnp.float32) * rows_all[m].astype(jnp.float32) * factors[m], axis=0
        )
    grad_w = sum(dot_dims(normed[m], grad_qkv[m], 0, 1) for m in range(batches))

    own_parts = [
        mine[:, n_mp * first : n_mp * (first + size)].reshape(depth, n_mp, size)
        for first, size in zip(firsts, sizes)
    ]
    own_rest = jnp.concatenate(own_parts, axis=2).transpose(1, 2, 0)
    own_rest = line_scatter(own_rest.reshape(-1, depth), "mp")
    own_output, own_gate, own_up, own_down = (
        own_rest[first : first + size] for first, size in zip(firsts, sizes)
    )
    own_qkv = exchange_sum(grad_w.astype(low), "dp")

    grad_normed_attn = jnp.concatenate(grad_normed, axis=0)
    grad_lower, _ = rms_back(in_float, rms_factor(in_float), gain_one, grad_normed_attn)
    grad_inputs = (grad_hidden_in + grad_lower).astype(low)
    grad_norms = exchange_sum(jnp.stack([gain_attn_part, gain_ffn_part], axis=1), ("dp", "mp")).T
    return (
        result.reshape(inputs.shape),
        grad_inputs.reshape(inputs.shape),
        own_qkv[:, :cols],
        own_qkv[:, cols : 2 * cols],
        own_qkv[:, 2 * cols :],
        own_output,
        own_gate.T,
        own_up.T,
        own_down,
        grad_norms[0],
        grad_norms[1],
    )


def solution(mesh):
    row_spec = P(None, ("dp", "mp"), None)
    first, second = P("dp", "mp"), P("mp", "dp")
    both = P(("dp", "mp"))

    return jax.shard_map(
        local,
        mesh=mesh,
        in_specs=(
            row_spec, P(None, "dp", None), first, first, first, second, first, first, second,
            P("dp"), P("dp"), row_spec,
        ),
        out_specs=(
            row_spec, row_spec, first, first, first, second, first, first, second, both, both,
        ),
        check_vma=False,
    )
```

```python
import functools
import math

import jax
import jax.numpy as jnp
from jax import lax
from jax.experimental import pallas as pl
from jax.experimental.pallas import tpu as pltpu
from jax.sharding import PartitionSpec as P


HD = 64
BQ = 512
BK = 256
HPS = 2


def attn_fwd_kernel(lo_ref, q_ref, k_ref, v_ref, start_ref, o_ref, lse_ref, k_scr, *, bq, bk, heads):
    length = q_ref.shape[1]
    k_scr[...] = k_ref[...].T

    def q_step(qi, carry):
        q0 = pl.multiple_of(qi * bq, bq)
        qcols = pl.ds(q0, bq)
        q_blk = q_ref[:, qcols]
        start = start_ref[:, qcols]
        q_idx = q0 + lax.broadcasted_iota(jnp.int32, (1, bq), 1)

        def k_step(kb, state):
            k0 = pl.multiple_of(kb * bk, bk)
            k_idx = k0 + lax.broadcasted_iota(jnp.int32, (bk, bq), 0)
            allowed = (k_idx >= start) & (k_idx <= q_idx)
            out = []
            for h in range(heads):
                peak, total, acc = state[h]
                s = jnp.dot(k_scr[pl.ds(k0, bk), h * HD:(h + 1) * HD], q_blk[h * HD:(h + 1) * HD], preferred_element_type=jnp.float32)
                s = jnp.where(allowed, s, -1e30)
                new_peak = jnp.maximum(peak, jnp.max(s, axis=0, keepdims=True))
                p = jnp.exp(s - new_peak)
                fade = jnp.exp(peak - new_peak)
                total = total * fade + jnp.sum(p, axis=0, keepdims=True)
                acc = acc * fade + jnp.dot(v_ref[h * HD:(h + 1) * HD, pl.ds(k0, bk)], p.astype(jnp.bfloat16), preferred_element_type=jnp.float32)
                out.append((new_peak, total, acc))
            return tuple(out)

        init = tuple((jnp.full((1, bq), -1e30, jnp.float32), jnp.zeros((1, bq), jnp.float32), jnp.zeros((HD, bq), jnp.float32)) for _ in range(heads))
        hi = (q0 + bq - 1) // bk
        state = lax.fori_loop(lo_ref[qi], hi + 1, k_step, init)
        for h in range(heads):
            peak, total, acc = state[h]
            o_ref[h * HD:(h + 1) * HD, qcols] = (acc / total).astype(jnp.bfloat16)
            lse_ref[h, :, qcols] = peak + jnp.log(total)
        return carry

    lax.fori_loop(0, length // bq, q_step, 0)


def attn_bwd_kernel(lo_ref, q_ref, k_ref, v_ref, do_ref, o_ref, lse_ref, start_ref, cos_ref, sin_ref, out_ref, k_scr, v_scr, dk_scr, dv_scr, *, bq, bk, heads):
    length = q_ref.shape[1]
    k_scr[...] = k_ref[...].T
    v_scr[...] = v_ref[...].T
    dk_scr[...] = jnp.zeros_like(dk_scr)
    dv_scr[...] = jnp.zeros_like(dv_scr)
    half = HD // 2

    def unrotate(g, cos, sin):
        a, b = g[:half], g[half:]
        return jnp.concatenate([a * cos + b * sin, b * cos - a * sin], axis=0).astype(jnp.bfloat16)

    def q_step(qi, carry):
        q0 = pl.multiple_of(qi * bq, bq)
        qcols = pl.ds(q0, bq)
        q_blk = q_ref[:, qcols]
        do_blk = do_ref[:, qcols]
        q_t = q_blk.T
        do_t = do_blk.T
        prod = do_blk.astype(jnp.float32) * o_ref[:, qcols].astype(jnp.float32)
        start = start_ref[:, qcols]
        q_idx = q0 + lax.broadcasted_iota(jnp.int32, (1, bq), 1)
        deltas = [jnp.sum(prod[h * HD:(h + 1) * HD], axis=0, keepdims=True) for h in range(heads)]
        lses = [lse_ref[h, :, qcols] for h in range(heads)]

        def k_step(kb, state):
            k0 = pl.multiple_of(kb * bk, bk)
            rows = pl.ds(k0, bk)
            k_idx = k0 + lax.broadcasted_iota(jnp.int32, (bk, bq), 0)
            allowed = (k_idx >= start) & (k_idx <= q_idx)
            out = []
            for h in range(heads):
                hs = slice(h * HD, (h + 1) * HD)
                s = jnp.dot(k_scr[rows, hs], q_blk[hs], preferred_element_type=jnp.float32)
                p = jnp.exp(jnp.where(allowed, s - lses[h], -1e30))
                dp = jnp.dot(v_scr[rows, hs], do_blk[hs], preferred_element_type=jnp.float32)
                ds = (p * (dp - deltas[h])).astype(jnp.bfloat16)
                dv_scr[h, rows, :] += jnp.dot(p.astype(jnp.bfloat16), do_t[:, hs], preferred_element_type=jnp.float32)
                dk_scr[h, rows, :] += jnp.dot(ds, q_t[:, hs], preferred_element_type=jnp.float32)
                out.append(state[h] + jnp.dot(k_ref[hs, rows], ds, preferred_element_type=jnp.float32))
            return tuple(out)

        init = tuple(jnp.zeros((HD, bq), jnp.float32) for _ in range(heads))
        hi = (q0 + bq - 1) // bk
        state = lax.fori_loop(lo_ref[qi], hi + 1, k_step, init)
        cos, sin = cos_ref[:, qcols], sin_ref[:, qcols]
        for h in range(heads):
            out_ref[0, h * HD:(h + 1) * HD, qcols] = unrotate(state[h] * HD ** -0.5, cos, sin)
        return carry

    lax.fori_loop(0, length // bq, q_step, 0)
    for h in range(heads):
        out_ref[1, h * HD:(h + 1) * HD, :] = unrotate(dk_scr[h].T, cos_ref[...], sin_ref[...])
        out_ref[2, h * HD:(h + 1) * HD, :] = dv_scr[h].T.astype(jnp.bfloat16)


def attn_fwd(qkv_t, start, lo, bq=BQ, bk=BK, hps=HPS):
    cols3, length = qkv_t.shape
    cols = cols3 // 3
    steps = cols // (HD * hps)
    blk = (HD * hps, length)
    area = cols * length * length // 4
    return pl.pallas_call(
        functools.partial(attn_fwd_kernel, bq=bq, bk=bk, heads=hps),
        out_shape=(jax.ShapeDtypeStruct((cols, length), jnp.bfloat16), jax.ShapeDtypeStruct((cols // HD, 1, length), jnp.float32)),
        grid_spec=pltpu.PrefetchScalarGridSpec(
            num_scalar_prefetch=1, grid=(steps,),
            in_specs=[pl.BlockSpec(blk, lambda i, lo: (i, 0)), pl.BlockSpec(blk, lambda i, lo: (i + steps, 0)), pl.BlockSpec(blk, lambda i, lo: (i + 2 * steps, 0)),
                      pl.BlockSpec((1, length), lambda i, lo: (0, 0))],
            out_specs=[pl.BlockSpec(blk, lambda i, lo: (i, 0)), pl.BlockSpec((hps, 1, length), lambda i, lo: (i, 0, 0))],
            scratch_shapes=[pltpu.VMEM((length, HD * hps), jnp.bfloat16)]),
        cost_estimate=pl.CostEstimate(flops=16 * area, bytes_accessed=cols * length * 8, transcendentals=area // HD),
        name="attn_fwd",
    )(lo, qkv_t, qkv_t, qkv_t, start)


def attn_bwd(qkv_t, do_t, o_t, lse, start, lo, cos, sin, bq=BQ, bk=BK, hps=HPS):
    cols3, length = qkv_t.shape
    cols = cols3 // 3
    steps = cols // (HD * hps)
    blk = (HD * hps, length)
    area = cols * length * length // 4
    return pl.pallas_call(
        functools.partial(attn_bwd_kernel, bq=bq, bk=bk, heads=hps),
        out_shape=jax.ShapeDtypeStruct((3, cols, length), jnp.bfloat16),
        grid_spec=pltpu.PrefetchScalarGridSpec(
            num_scalar_prefetch=1, grid=(steps,),
            in_specs=[pl.BlockSpec(blk, lambda i, lo: (i, 0)), pl.BlockSpec(blk, lambda i, lo: (i + steps, 0)), pl.BlockSpec(blk, lambda i, lo: (i + 2 * steps, 0)),
                      pl.BlockSpec(blk, lambda i, lo: (i, 0)), pl.BlockSpec(blk, lambda i, lo: (i, 0)),
                      pl.BlockSpec((hps, 1, length), lambda i, lo: (i, 0, 0)),
                      pl.BlockSpec((1, length), lambda i, lo: (0, 0)),
                      pl.BlockSpec((HD // 2, length), lambda i, lo: (0, 0)), pl.BlockSpec((HD // 2, length), lambda i, lo: (0, 0))],
            out_specs=pl.BlockSpec((3,) + blk, lambda i, lo: (0, i, 0)),
            scratch_shapes=[pltpu.VMEM((length, HD * hps), jnp.bfloat16)] * 2 + [pltpu.VMEM((hps, length, HD), jnp.float32)] * 2),
        cost_estimate=pl.CostEstimate(flops=40 * area, bytes_accessed=cols * length * 20, transcendentals=area // HD),
        name="attn_bwd",
    )(lo, qkv_t, qkv_t, qkv_t, do_t, o_t, lse, start, cos, sin)


def assemble_kernel(lane_ref, *refs, sizes, parts):
    pieces, outs = refs[: 2 * parts], refs[2 * parts : 2 * parts + len(sizes)]
    held, in_sem, out_sem = refs[2 * parts + len(sizes) :]
    slots = held.shape[0]
    total = sum(sizes)
    steps = [
        (block, part, sum(sizes[:part])) for block in range(4) for part in range(len(sizes))
    ]

    def fetch(step):
        block, part, first = steps[step]
        rows = pl.ds((block % 2) * total + first, sizes[part])
        slot = step % slots
        return [
            pltpu.make_async_copy(
                pieces[2 * r + block // 2].at[rows],
                held.at[slot, pl.ds(0, sizes[part]), pl.ds(pl.multiple_of(lane_ref[r], 128), 128)],
                in_sem.at[slot, r],
            )
            for r in range(parts)
        ]

    def put(step):
        block, part, _ = steps[step]
        slot = step % slots
        return pltpu.make_async_copy(
            held.at[slot, pl.ds(0, sizes[part])],
            outs[part].at[pl.ds(block * sizes[part], sizes[part])],
            out_sem.at[slot],
        )

    ahead = slots // 2
    for step in range(ahead):
        for copy in fetch(step):
            copy.start()
    for step in range(len(steps)):
        later = step + ahead
        if later < len(steps):
            if later >= slots:
                put(later - slots).wait()
            for copy in fetch(later):
                copy.start()
        for copy in fetch(step):
            copy.wait()
        put(step).start()
    for step in range(len(steps) - slots, len(steps)):
        put(step).wait()


def assemble(lanes, pieces, sizes, width):
    parts = len(pieces) // 2
    whole = pl.BlockSpec(memory_space=pl.ANY)
    return pl.pallas_call(
        functools.partial(assemble_kernel, sizes=sizes, parts=parts),
        out_shape=[jax.ShapeDtypeStruct((4 * size, width), jnp.bfloat16) for size in sizes],
        grid_spec=pltpu.PrefetchScalarGridSpec(
            num_scalar_prefetch=1,
            grid=(1,),
            in_specs=[whole] * len(pieces),
            out_specs=[whole] * len(sizes),
            scratch_shapes=[
                pltpu.VMEM((4, max(sizes), width), jnp.bfloat16),
                pltpu.SemaphoreType.DMA((4, parts)),
                pltpu.SemaphoreType.DMA((4,)),
            ],
        ),
        cost_estimate=pl.CostEstimate(
            flops=0, bytes_accessed=16 * sum(sizes) * width, transcendentals=0
        ),
        name="assemble",
    )(lanes, *pieces)


def dot_in(left, right, left_dim, right_dim):
    return lax.dot_general(
        left, right, (((left_dim,), (right_dim,)), ((), ())), preferred_element_type=jnp.float32
    )


def ffn_main_kernel(x_ref, c_ref, gate_ref, up_ref, down_ref, h_ref, dg_ref, du_ref, *, step):
    for first in range(0, x_ref.shape[0], step):
        rows = slice(first, first + step)
        gate = dot_in(x_ref[rows], gate_ref[...], 1, 1)
        up = dot_in(x_ref[rows], up_ref[...], 1, 1)
        grad_hidden = dot_in(c_ref[rows], down_ref[...], 1, 1)
        sig = jax.nn.sigmoid(gate)
        silu = gate * sig
        h_ref[rows] = (silu * up).astype(jnp.bfloat16)
        dg = (grad_hidden * up * sig * (1.0 + gate * (1.0 - sig))).astype(jnp.bfloat16)
        du = (grad_hidden * silu).astype(jnp.bfloat16)
        dg_ref[rows] = dg
        du_ref[rows] = du


def ffn_grad_kernel(x_ref, c_ref, h_ref, dg_ref, du_ref, g_ref):
    for place, (left, right) in enumerate(((dg_ref, x_ref), (du_ref, x_ref), (h_ref, c_ref))):
        grad = dot_in(left[...], right[...], 0, 0).astype(jnp.bfloat16)
        for i in range(g_ref.shape[0]):
            g_ref[i, place] = grad[:, i * g_ref.shape[3] : (i + 1) * g_ref.shape[3]]


def ffn_main(x, c, gate, up, down, tile=256, step=256):
    tokens, width = x.shape
    units = gate.shape[0]
    full = pl.BlockSpec((tokens, width), lambda t: (0, 0))
    weight = pl.BlockSpec((tile, width), lambda t: (t, 0))
    column = pl.BlockSpec((tokens, tile), lambda t: (0, t))
    return pl.pallas_call(
        functools.partial(ffn_main_kernel, step=step),
        out_shape=[jax.ShapeDtypeStruct((tokens, units), jnp.bfloat16)] * 3,
        grid=(units // tile,),
        in_specs=[full, full, weight, weight, weight],
        out_specs=[column, column, column],
        cost_estimate=pl.CostEstimate(
            flops=6 * tokens * width * units, bytes_accessed=6 * units * (width + tokens),
            transcendentals=tokens * units,
        ),
        name="ffn_main",
    )(x, c, gate, up, down)


def ffn_grad(x, c, hidden, dg, du, chunks, tile=256):
    tokens, width = x.shape
    units = hidden.shape[1]
    full = pl.BlockSpec((tokens, width), lambda t: (0, 0))
    column = pl.BlockSpec((tokens, tile), lambda t: (0, t))
    piece = width // chunks
    return pl.pallas_call(
        ffn_grad_kernel,
        out_shape=jax.ShapeDtypeStruct((chunks, 3, units, piece), jnp.bfloat16),
        grid=(units // tile,),
        in_specs=[full, full, column, column, column],
        out_specs=pl.BlockSpec((chunks, 3, tile, piece), lambda t: (0, 0, t, 0)),
        cost_estimate=pl.CostEstimate(
            flops=6 * tokens * width * units, bytes_accessed=6 * units * (width + tokens),
            transcendentals=0,
        ),
        name="ffn_grad",
    )(x, c, hidden, dg, du)


eps_norm = 1e-05


def dot_dims(left, right, left_dim, right_dim):
    return lax.dot_general(
        left, right, (((left_dim,), (right_dim,)), ((), ())), preferred_element_type=jnp.float32
    )


def row_starts(seg_row):
    ones = [jnp.sum((seg_row < s).astype(jnp.int32)) for s in (1, 2, 3)]
    start = jnp.zeros_like(seg_row)
    before = 0
    for s, count in zip((1, 2, 3), ones):
        start = start + jnp.where(seg_row >= s, count - before, 0)
        before = count
    return start


def rope_tables(start):
    half_dim = HD // 2
    offsets = (jnp.arange(start.shape[0], dtype=jnp.int32) - start).astype(jnp.float32)
    frequency = jnp.exp(jnp.arange(half_dim, dtype=jnp.float32) * (-math.log(10000.0) / half_dim))
    angles = frequency[:, None] * offsets[None, :]
    return jnp.cos(angles), jnp.sin(angles)


def rotate(rows, cos_table, sin_table):
    count, length = rows.shape
    parts = rows.reshape(count // HD, 2, HD // 2, length)
    low, high = parts[:, 0], parts[:, 1]
    turned = jnp.stack(
        [low * cos_table - high * sin_table, high * cos_table + low * sin_table], axis=1
    )
    return turned.reshape(count, length)


def rms_factor(values):
    return lax.rsqrt(jnp.mean(values * values, axis=-1, keepdims=True) + eps_norm)


def rms_back(values_in, factor, gain, grad_normed):
    scaled = grad_normed * gain
    gain_part = jnp.sum(grad_normed * values_in * factor, axis=0)
    inner = jnp.mean(scaled * values_in, axis=-1, keepdims=True)
    return factor * scaled - values_in * (factor * factor * factor) * inner, gain_part


def scatter(partial_sum, axis, dim):
    return lax.psum_scatter(partial_sum, axis, scatter_dimension=dim, tiled=True)


def line_steps(count):
    near_right = [(i, i + 1) for i in range(count - 1)]
    near_left = [(i, i - 1) for i in range(1, count)]
    return near_right, near_left


def line_gather(piece, axis, hold=lambda *arrays: arrays):
    count, me = lax.axis_size(axis), lax.axis_index(axis)
    assert count == 4
    near_right, near_left = line_steps(count)
    one_left = lax.ppermute(piece, axis, near_right)
    one_right = lax.ppermute(piece, axis, near_left)
    one_left, one_right = hold(one_left, one_right)
    two_left = lax.ppermute(one_left, axis, [(1, 2), (2, 3)])
    two_right = lax.ppermute(one_right, axis, [(1, 0), (2, 1)])
    three_left = lax.ppermute(one_left, axis, [(1, 3)])
    three_right = lax.ppermute(one_right, axis, [(2, 0)])
    slots = jnp.concatenate(
        [three_left, two_left, one_left, piece, one_right, two_right, three_right], axis=0
    )
    rows = piece.shape[0]
    return lax.dynamic_slice_in_dim(slots, (count - 1 - me) * rows, count * rows, axis=0)


def line_scatter(partial_sum, axis):
    count, me = lax.axis_size(axis), lax.axis_index(axis)
    assert count == 4
    rows = partial_sum.shape[0] // count
    near_right, near_left = line_steps(count)

    def block(offset):
        first = jnp.clip(me + offset, 0, count - 1) * rows
        return lax.dynamic_slice_in_dim(partial_sum, first, rows, axis=0)

    two_right = lax.ppermute(block(2), axis, [(0, 1), (1, 2)])
    two_left = lax.ppermute(block(-2), axis, [(3, 2), (2, 1)])
    three_right = lax.ppermute(block(3), axis, [(0, 2)])
    three_left = lax.ppermute(block(-3), axis, [(3, 1)])

    def total(*parts):
        return sum(part.astype(jnp.float32) for part in parts)

    right = lax.ppermute(
        total(block(1), two_right, three_right).astype(jnp.bfloat16), axis, near_right
    )
    left = lax.ppermute(
        total(block(-1), two_left, three_left).astype(jnp.bfloat16), axis, near_left
    )
    return total(block(0), right, left)


def plane_gather(piece, axis, sizes):
    core, across, along = ([(i, i ^ bit) for i in range(8)] for bit in (1, 2, 4))
    half = piece.shape[0] // 2
    top, low = piece[:half], piece[half:]

    def partner(part):
        return lax.ppermute(part, axis, core)

    top_x, low_y = lax.ppermute(top, axis, across), lax.ppermute(low, axis, along)
    top_y, low_x = lax.ppermute(top, axis, along), lax.ppermute(low, axis, across)
    top_xy, low_xy = lax.ppermute(top_x, axis, along), lax.ppermute(low_y, axis, across)
    held = [(top, low), (top_x, low_x), (top_y, low_y), (top_xy, low_xy)]
    parts = []
    for pair in held:
        parts += [pair, tuple(partner(part) for part in pair)]

    flat = [part for pair in parts for part in pair]
    lanes = jnp.arange(8, dtype=jnp.int32) ^ lax.axis_index(axis).astype(jnp.int32)
    return assemble(lanes * piece.shape[1], flat, sizes, 8 * piece.shape[1])


def exchange_sum(partial_sum, axis):
    count = lax.axis_size(axis)
    parts = partial_sum.reshape((count, partial_sum.shape[0] // count) + partial_sum.shape[1:])
    swapped = lax.all_to_all(parts, axis, split_axis=0, concat_axis=0, tiled=True)
    return jnp.sum(swapped.astype(jnp.float32), axis=0)


def local(
    inputs, segments, w_query, w_key, w_value, w_output, w_gate, w_up, w_down,
    gain_attn, gain_ffn, cotangent,
):
    low = jnp.bfloat16
    n_dp, n_mp = lax.axis_size("dp"), lax.axis_size("mp")
    batches, tokens, width = inputs.shape
    cols = w_query.shape[1]
    depth = w_query.shape[0]
    hidden_part = w_gate.shape[1]

    def split16(gain):
        high = gain.astype(low)
        return high, (gain - high.astype(jnp.float32)).astype(low)

    pieces = split16(gain_attn) + split16(gain_ffn)
    gain_row = jnp.concatenate(pieces + (jnp.zeros((3 * cols - 4 * depth,), low),))
    qkv_piece = jnp.concatenate(
        [
            jnp.concatenate([w_query, w_key, w_value], axis=1),
            jnp.pad(gain_row[None], ((0, 15), (0, 0))),
        ],
        axis=0,
    )
    qkv_all = lax.all_gather(qkv_piece, "dp", axis=0, tiled=False)
    w_qkv = qkv_all[:, :depth].reshape(width, 3 * cols)
    gains = qkv_all[:, depth, : 4 * depth].astype(jnp.float32).reshape(n_dp, 4, depth)
    gain_one = (gains[:, 0] + gains[:, 1]).reshape(width)
    gain_two = (gains[:, 2] + gains[:, 3]).reshape(width)

    rest_piece = jnp.concatenate([w_output, w_gate.T, w_up.T, w_down], axis=0)
    sizes = (cols, hidden_part, hidden_part, hidden_part)
    firsts = (0, cols, cols + hidden_part, cols + 2 * hidden_part)
    if n_dp == 8 and depth == 128:
        output_full, gate_full, up_full, down_full = plane_gather(line_gather(rest_piece, "mp"), "dp", sizes)
    else:
        rest_every = lax.all_gather(rest_piece, ("dp", "mp"), axis=0, tiled=False)
        rest_every = rest_every.reshape((n_dp, n_mp) + rest_piece.shape).transpose(1, 2, 0, 3)
        rest_every = rest_every.reshape(n_mp, rest_piece.shape[0], width)
        output_full, gate_full, up_full, down_full = (
            rest_every[:, first : first + size].reshape(n_mp * size, width)
            for first, size in zip(firsts, sizes)
        )

    first_rows = line_gather(inputs[0], "mp")
    first_rows, second_piece = lax.optimization_barrier((first_rows, inputs[1]))
    rows_all = [first_rows, None]

    normed, factors, qkv, tables, starts, lows, mixed, logs = [], [], [], [], [], [], [], []
    for m in range(batches):
        start = row_starts(segments[m, 0])
        cos_table, sin_table = rope_tables(start)
        tables.append((cos_table, sin_table))
        starts.append(start[None])
        lows.append(start[::BQ] // BK)
        if m == 1:
            def after_first(left, right):
                left, right, mixed[0] = lax.optimization_barrier((left, right, mixed[0]))
                return left, right

            rows_all[1] = line_gather(second_piece, "mp", after_first)
        rows = rows_all[m].astype(jnp.float32)
        factors.append(rms_factor(rows))
        normed.append((rows * factors[m] * gain_one).astype(low))
        pre = dot_dims(w_qkv, normed[m], 0, 1)
        turned_q = rotate(pre[:cols], cos_table, sin_table) * HD ** -0.5
        turned_k = rotate(pre[cols : 2 * cols], cos_table, sin_table)
        qkv.append(jnp.concatenate([turned_q, turned_k, pre[2 * cols :]], axis=0).astype(low))
        out, log = attn_fwd(qkv[m], starts[m], lows[m])
        mixed.append(out)
        logs.append(log)
    mixed_own = []
    for m in range(batches):
        mixed_own.append(
            lax.all_to_all(mixed[m], "mp", split_axis=1, concat_axis=0, tiled=True)
        )
    in_float = inputs.astype(jnp.float32).reshape(batches * tokens, width)
    mixed_both = jnp.concatenate(mixed_own, axis=1)
    hidden_in = in_float + dot_dims(mixed_both, output_full, 0, 0)
    factor_ffn = rms_factor(hidden_in)
    normed_ffn = (hidden_in * factor_ffn * gain_two).astype(low)
    grad_top = cotangent.reshape(batches * tokens, width)
    hidden, grad_gate_pre, grad_up_pre = ffn_main(
        normed_ffn, grad_top, gate_full, up_full, down_full
    )
    grad_normed_ffn = dot_dims(grad_gate_pre, gate_full, 1, 0) + dot_dims(
        grad_up_pre, up_full, 1, 0
    )
    result = (hidden_in + dot_dims(hidden, down_full, 1, 0)).astype(low)
    chunks = width // 128
    every_grad = ffn_grad(normed_ffn, grad_top, hidden, grad_gate_pre, grad_up_pre, chunks)
    if n_dp != chunks:
        every_grad = every_grad.reshape(chunks, 3, n_mp * hidden_part, n_dp // chunks, depth)
        every_grad = every_grad.transpose(0, 3, 1, 2, 4).reshape(n_dp, 3, -1, depth)
    grad_middle, gain_ffn_part = rms_back(hidden_in, factor_ffn, gain_two, grad_normed_ffn)
    grad_hidden_in = grad_top.astype(jnp.float32) + grad_middle
    grad_branch = grad_hidden_in.astype(low)
    grad_mixed = dot_dims(output_full, grad_branch, 1, 1).astype(low)
    grad_mixed_rows = []
    for m in range(batches):
        grad_mixed_rows.append(
            lax.all_to_all(
                grad_mixed[:, m * tokens : (m + 1) * tokens], "mp", split_axis=0,
                concat_axis=1, tiled=True,
            )
        )
    grad_output = dot_dims(grad_branch, mixed_both, 0, 1).astype(low)

    grad_mixed_rows[0], every_grad = lax.optimization_barrier((grad_mixed_rows[0], every_grad))
    mine = scatter(every_grad, "dp", 0)


    grad_qkv, grad_normed = [], []
    gain_attn_part = jnp.zeros((width,), jnp.float32)
    for m in range(batches):
        cos_table, sin_table = tables[m]
        back = attn_bwd(
            qkv[m], grad_mixed_rows[m], mixed[m], logs[m], starts[m], lows[m], cos_table,
            sin_table,
        ).reshape(3 * cols, n_mp * tokens)
        grad_qkv.append(back)
        spread = dot_dims(back, w_qkv, 0, 1).astype(low)
        if m == 0:
            spread, grad_mixed_rows[1] = lax.optimization_barrier((spread, grad_mixed_rows[1]))
        grad_normed.append(line_scatter(spread, "mp"))
        gain_attn_part = gain_attn_part + jnp.sum(
            spread.astype(jnp.float32) * rows_all[m].astype(jnp.float32) * factors[m], axis=0
        )
    grad_w = sum(dot_dims(normed[m], grad_qkv[m], 0, 1) for m in range(batches))

    own_out = exchange_sum(grad_output, "dp").astype(low).T.reshape(n_mp, cols, depth)
    own_ffn = mine.reshape(3, n_mp, hidden_part, depth).transpose(1, 0, 2, 3)
    own_rest = jnp.concatenate([own_out, own_ffn.reshape(n_mp, -1, depth)], axis=1)
    own_rest = own_rest.reshape(-1, depth)
    own_rest = line_scatter(own_rest, "mp")
    own_output, own_gate, own_up, own_down = (
        own_rest[first : first + size] for first, size in zip(firsts, sizes)
    )
    own_qkv = exchange_sum(grad_w.astype(low), "dp")

    grad_normed_attn = jnp.concatenate(grad_normed, axis=0)
    grad_lower, _ = rms_back(in_float, rms_factor(in_float), gain_one, grad_normed_attn)
    grad_inputs = (grad_hidden_in + grad_lower).astype(low)
    grad_norms = exchange_sum(jnp.stack([gain_attn_part, gain_ffn_part], axis=1), ("dp", "mp")).T
    return (
        result.reshape(inputs.shape),
        grad_inputs.reshape(inputs.shape),
        own_qkv[:, :cols],
        own_qkv[:, cols : 2 * cols],
        own_qkv[:, 2 * cols :],
        own_output,
        own_gate.T,
        own_up.T,
        own_down,
        grad_norms[0],
        grad_norms[1],
    )


def solution(mesh):
    row_spec = P(None, ("dp", "mp"), None)
    first, second = P("dp", "mp"), P("mp", "dp")
    both = P(("dp", "mp"))

    return jax.shard_map(
        local,
        mesh=mesh,
        in_specs=(
            row_spec, P(None, "dp", None), first, first, first, second, first, first, second,
            P("dp"), P("dp"), row_spec,
        ),
        out_specs=(
            row_spec, row_spec, first, first, first, second, first, first, second, both, both,
        ),
        check_vma=False,
    )
```

```python
import functools
import math

import jax
import jax.numpy as jnp
from jax import lax
from jax.experimental import pallas as pl
from jax.experimental.pallas import tpu as pltpu
from jax.sharding import PartitionSpec as P


HD = 64
BQ = 512
BK = 256
HPS = 2


def attn_fwd_kernel(lo_ref, q_ref, k_ref, v_ref, start_ref, o_ref, lse_ref, k_scr, *, bq, bk, heads):
    length = q_ref.shape[1]
    k_scr[...] = k_ref[...].T

    def q_step(qi, carry):
        q0 = pl.multiple_of(qi * bq, bq)
        qcols = pl.ds(q0, bq)
        q_blk = q_ref[:, qcols]
        start = start_ref[:, qcols]
        q_idx = q0 + lax.broadcasted_iota(jnp.int32, (1, bq), 1)

        def k_step(kb, state):
            k0 = pl.multiple_of(kb * bk, bk)
            k_idx = k0 + lax.broadcasted_iota(jnp.int32, (bk, bq), 0)
            allowed = (k_idx >= start) & (k_idx <= q_idx)
            out = []
            for h in range(heads):
                peak, total, acc = state[h]
                s = jnp.dot(k_scr[pl.ds(k0, bk), h * HD:(h + 1) * HD], q_blk[h * HD:(h + 1) * HD], preferred_element_type=jnp.float32)
                s = jnp.where(allowed, s, -1e30)
                new_peak = jnp.maximum(peak, jnp.max(s, axis=0, keepdims=True))
                p = jnp.exp(s - new_peak)
                fade = jnp.exp(peak - new_peak)
                total = total * fade + jnp.sum(p, axis=0, keepdims=True)
                acc = acc * fade + jnp.dot(v_ref[h * HD:(h + 1) * HD, pl.ds(k0, bk)], p.astype(jnp.bfloat16), preferred_element_type=jnp.float32)
                out.append((new_peak, total, acc))
            return tuple(out)

        init = tuple((jnp.full((1, bq), -1e30, jnp.float32), jnp.zeros((1, bq), jnp.float32), jnp.zeros((HD, bq), jnp.float32)) for _ in range(heads))
        hi = (q0 + bq - 1) // bk
        state = lax.fori_loop(lo_ref[qi], hi + 1, k_step, init)
        for h in range(heads):
            peak, total, acc = state[h]
            o_ref[h * HD:(h + 1) * HD, qcols] = (acc / total).astype(jnp.bfloat16)
            lse_ref[h, :, qcols] = peak + jnp.log(total)
        return carry

    lax.fori_loop(0, length // bq, q_step, 0)


def attn_bwd_kernel(lo_ref, q_ref, k_ref, v_ref, do_ref, o_ref, lse_ref, start_ref, cos_ref, sin_ref, out_ref, k_scr, v_scr, dk_scr, dv_scr, *, bq, bk, heads):
    length = q_ref.shape[1]
    k_scr[...] = k_ref[...].T
    v_scr[...] = v_ref[...].T
    dk_scr[...] = jnp.zeros_like(dk_scr)
    dv_scr[...] = jnp.zeros_like(dv_scr)
    half = HD // 2

    def unrotate(g, cos, sin):
        a, b = g[:half], g[half:]
        return jnp.concatenate([a * cos + b * sin, b * cos - a * sin], axis=0).astype(jnp.bfloat16)

    def q_step(qi, carry):
        q0 = pl.multiple_of(qi * bq, bq)
        qcols = pl.ds(q0, bq)
        q_blk = q_ref[:, qcols]
        do_blk = do_ref[:, qcols]
        q_t = q_blk.T
        do_t = do_blk.T
        prod = do_blk.astype(jnp.float32) * o_ref[:, qcols].astype(jnp.float32)
        start = start_ref[:, qcols]
        q_idx = q0 + lax.broadcasted_iota(jnp.int32, (1, bq), 1)
        deltas = [jnp.sum(prod[h * HD:(h + 1) * HD], axis=0, keepdims=True) for h in range(heads)]
        lses = [lse_ref[h, :, qcols] for h in range(heads)]

        def k_step(kb, state):
            k0 = pl.multiple_of(kb * bk, bk)
            rows = pl.ds(k0, bk)
            k_idx = k0 + lax.broadcasted_iota(jnp.int32, (bk, bq), 0)
            allowed = (k_idx >= start) & (k_idx <= q_idx)
            out = []
            for h in range(heads):
                hs = slice(h * HD, (h + 1) * HD)
                s = jnp.dot(k_scr[rows, hs], q_blk[hs], preferred_element_type=jnp.float32)
                p = jnp.exp(jnp.where(allowed, s - lses[h], -1e30))
                dp = jnp.dot(v_scr[rows, hs], do_blk[hs], preferred_element_type=jnp.float32)
                ds = (p * (dp - deltas[h])).astype(jnp.bfloat16)
                dv_scr[h, rows, :] += jnp.dot(p.astype(jnp.bfloat16), do_t[:, hs], preferred_element_type=jnp.float32)
                dk_scr[h, rows, :] += jnp.dot(ds, q_t[:, hs], preferred_element_type=jnp.float32)
                out.append(state[h] + jnp.dot(k_ref[hs, rows], ds, preferred_element_type=jnp.float32))
            return tuple(out)

        init = tuple(jnp.zeros((HD, bq), jnp.float32) for _ in range(heads))
        hi = (q0 + bq - 1) // bk
        state = lax.fori_loop(lo_ref[qi], hi + 1, k_step, init)
        cos, sin = cos_ref[:, qcols], sin_ref[:, qcols]
        for h in range(heads):
            out_ref[0, h * HD:(h + 1) * HD, qcols] = unrotate(state[h] * HD ** -0.5, cos, sin)
        return carry

    lax.fori_loop(0, length // bq, q_step, 0)
    for h in range(heads):
        out_ref[1, h * HD:(h + 1) * HD, :] = unrotate(dk_scr[h].T, cos_ref[...], sin_ref[...])
        out_ref[2, h * HD:(h + 1) * HD, :] = dv_scr[h].T.astype(jnp.bfloat16)


def attn_fwd(qkv_t, start, lo, bq=BQ, bk=BK, hps=HPS):
    cols3, length = qkv_t.shape
    cols = cols3 // 3
    steps = cols // (HD * hps)
    blk = (HD * hps, length)
    area = cols * length * length // 4
    return pl.pallas_call(
        functools.partial(attn_fwd_kernel, bq=bq, bk=bk, heads=hps),
        out_shape=(jax.ShapeDtypeStruct((cols, length), jnp.bfloat16), jax.ShapeDtypeStruct((cols // HD, 1, length), jnp.float32)),
        grid_spec=pltpu.PrefetchScalarGridSpec(
            num_scalar_prefetch=1, grid=(steps,),
            in_specs=[pl.BlockSpec(blk, lambda i, lo: (i, 0)), pl.BlockSpec(blk, lambda i, lo: (i + steps, 0)), pl.BlockSpec(blk, lambda i, lo: (i + 2 * steps, 0)),
                      pl.BlockSpec((1, length), lambda i, lo: (0, 0))],
            out_specs=[pl.BlockSpec(blk, lambda i, lo: (i, 0)), pl.BlockSpec((hps, 1, length), lambda i, lo: (i, 0, 0))],
            scratch_shapes=[pltpu.VMEM((length, HD * hps), jnp.bfloat16)]),
        cost_estimate=pl.CostEstimate(flops=16 * area, bytes_accessed=cols * length * 8, transcendentals=area // HD),
        name="attn_fwd",
    )(lo, qkv_t, qkv_t, qkv_t, start)


def attn_bwd(qkv_t, do_t, o_t, lse, start, lo, cos, sin, bq=BQ, bk=BK, hps=HPS):
    cols3, length = qkv_t.shape
    cols = cols3 // 3
    steps = cols // (HD * hps)
    blk = (HD * hps, length)
    area = cols * length * length // 4
    return pl.pallas_call(
        functools.partial(attn_bwd_kernel, bq=bq, bk=bk, heads=hps),
        out_shape=jax.ShapeDtypeStruct((3, cols, length), jnp.bfloat16),
        grid_spec=pltpu.PrefetchScalarGridSpec(
            num_scalar_prefetch=1, grid=(steps,),
            in_specs=[pl.BlockSpec(blk, lambda i, lo: (i, 0)), pl.BlockSpec(blk, lambda i, lo: (i + steps, 0)), pl.BlockSpec(blk, lambda i, lo: (i + 2 * steps, 0)),
                      pl.BlockSpec(blk, lambda i, lo: (i, 0)), pl.BlockSpec(blk, lambda i, lo: (i, 0)),
                      pl.BlockSpec((hps, 1, length), lambda i, lo: (i, 0, 0)),
                      pl.BlockSpec((1, length), lambda i, lo: (0, 0)),
                      pl.BlockSpec((HD // 2, length), lambda i, lo: (0, 0)), pl.BlockSpec((HD // 2, length), lambda i, lo: (0, 0))],
            out_specs=pl.BlockSpec((3,) + blk, lambda i, lo: (0, i, 0)),
            scratch_shapes=[pltpu.VMEM((length, HD * hps), jnp.bfloat16)] * 2 + [pltpu.VMEM((hps, length, HD), jnp.float32)] * 2),
        cost_estimate=pl.CostEstimate(flops=40 * area, bytes_accessed=cols * length * 20, transcendentals=area // HD),
        name="attn_bwd",
    )(lo, qkv_t, qkv_t, qkv_t, do_t, o_t, lse, start, cos, sin)


def assemble_kernel(lane_ref, *refs, sizes, parts):
    pieces, outs = refs[: 2 * parts], refs[2 * parts : 2 * parts + len(sizes)]
    held, in_sem, out_sem = refs[2 * parts + len(sizes) :]
    slots = held.shape[0]
    total = sum(sizes)
    steps = [
        (block, part, sum(sizes[:part])) for block in range(4) for part in range(len(sizes))
    ]

    def fetch(step):
        block, part, first = steps[step]
        rows = pl.ds((block % 2) * total + first, sizes[part])
        slot = step % slots
        return [
            pltpu.make_async_copy(
                pieces[2 * r + block // 2].at[rows],
                held.at[slot, pl.ds(0, sizes[part]), pl.ds(pl.multiple_of(lane_ref[r], 128), 128)],
                in_sem.at[slot, r],
            )
            for r in range(parts)
        ]

    def put(step):
        block, part, _ = steps[step]
        slot = step % slots
        return pltpu.make_async_copy(
            held.at[slot, pl.ds(0, sizes[part])],
            outs[part].at[pl.ds(block * sizes[part], sizes[part])],
            out_sem.at[slot],
        )

    ahead = slots // 2
    for step in range(ahead):
        for copy in fetch(step):
            copy.start()
    for step in range(len(steps)):
        later = step + ahead
        if later < len(steps):
            if later >= slots:
                put(later - slots).wait()
            for copy in fetch(later):
                copy.start()
        for copy in fetch(step):
            copy.wait()
        put(step).start()
    for step in range(len(steps) - slots, len(steps)):
        put(step).wait()


def assemble(lanes, pieces, sizes, width):
    parts = len(pieces) // 2
    whole = pl.BlockSpec(memory_space=pl.ANY)
    return pl.pallas_call(
        functools.partial(assemble_kernel, sizes=sizes, parts=parts),
        out_shape=[jax.ShapeDtypeStruct((4 * size, width), jnp.bfloat16) for size in sizes],
        grid_spec=pltpu.PrefetchScalarGridSpec(
            num_scalar_prefetch=1,
            grid=(1,),
            in_specs=[whole] * len(pieces),
            out_specs=[whole] * len(sizes),
            scratch_shapes=[
                pltpu.VMEM((4, max(sizes), width), jnp.bfloat16),
                pltpu.SemaphoreType.DMA((4, parts)),
                pltpu.SemaphoreType.DMA((4,)),
            ],
        ),
        cost_estimate=pl.CostEstimate(
            flops=0, bytes_accessed=16 * sum(sizes) * width, transcendentals=0
        ),
        name="assemble",
    )(lanes, *pieces)


def dot_in(left, right, left_dim, right_dim):
    return lax.dot_general(
        left, right, (((left_dim,), (right_dim,)), ((), ())), preferred_element_type=jnp.float32
    )


def ffn_main_kernel(x_ref, c_ref, gate_ref, up_ref, down_ref, h_ref, dg_ref, du_ref, *, step):
    for first in range(0, x_ref.shape[0], step):
        rows = slice(first, first + step)
        gate = dot_in(x_ref[rows], gate_ref[...], 1, 1)
        up = dot_in(x_ref[rows], up_ref[...], 1, 1)
        grad_hidden = dot_in(c_ref[rows], down_ref[...], 1, 1)
        sig = jax.nn.sigmoid(gate)
        silu = gate * sig
        h_ref[rows] = (silu * up).astype(jnp.bfloat16)
        dg = (grad_hidden * up * sig * (1.0 + gate * (1.0 - sig))).astype(jnp.bfloat16)
        du = (grad_hidden * silu).astype(jnp.bfloat16)
        dg_ref[rows] = dg
        du_ref[rows] = du


def ffn_grad_kernel(x_ref, c_ref, h_ref, dg_ref, du_ref, g_ref):
    for place, (left, right) in enumerate(((dg_ref, x_ref), (du_ref, x_ref), (h_ref, c_ref))):
        grad = dot_in(left[...], right[...], 0, 0).astype(jnp.bfloat16)
        for i in range(g_ref.shape[0]):
            g_ref[i, place] = grad[:, i * g_ref.shape[3] : (i + 1) * g_ref.shape[3]]


def ffn_main(x, c, gate, up, down, tile=256, step=256):
    tokens, width = x.shape
    units = gate.shape[0]
    full = pl.BlockSpec((tokens, width), lambda t: (0, 0))
    weight = pl.BlockSpec((tile, width), lambda t: (t, 0))
    column = pl.BlockSpec((tokens, tile), lambda t: (0, t))
    return pl.pallas_call(
        functools.partial(ffn_main_kernel, step=step),
        out_shape=[jax.ShapeDtypeStruct((tokens, units), jnp.bfloat16)] * 3,
        grid=(units // tile,),
        in_specs=[full, full, weight, weight, weight],
        out_specs=[column, column, column],
        cost_estimate=pl.CostEstimate(
            flops=6 * tokens * width * units, bytes_accessed=6 * units * (width + tokens),
            transcendentals=tokens * units,
        ),
        name="ffn_main",
    )(x, c, gate, up, down)


def ffn_grad(x, c, hidden, dg, du, chunks, tile=256):
    tokens, width = x.shape
    units = hidden.shape[1]
    full = pl.BlockSpec((tokens, width), lambda t: (0, 0))
    column = pl.BlockSpec((tokens, tile), lambda t: (0, t))
    piece = width // chunks
    return pl.pallas_call(
        ffn_grad_kernel,
        out_shape=jax.ShapeDtypeStruct((chunks, 3, units, piece), jnp.bfloat16),
        grid=(units // tile,),
        in_specs=[full, full, column, column, column],
        out_specs=pl.BlockSpec((chunks, 3, tile, piece), lambda t: (0, 0, t, 0)),
        cost_estimate=pl.CostEstimate(
            flops=6 * tokens * width * units, bytes_accessed=6 * units * (width + tokens),
            transcendentals=0,
        ),
        name="ffn_grad",
    )(x, c, hidden, dg, du)


eps_norm = 1e-05


def dot_dims(left, right, left_dim, right_dim):
    return lax.dot_general(
        left, right, (((left_dim,), (right_dim,)), ((), ())), preferred_element_type=jnp.float32
    )


def row_starts(seg_row):
    ones = [jnp.sum((seg_row < s).astype(jnp.int32)) for s in (1, 2, 3)]
    start = jnp.zeros_like(seg_row)
    before = 0
    for s, count in zip((1, 2, 3), ones):
        start = start + jnp.where(seg_row >= s, count - before, 0)
        before = count
    return start


def rope_tables(start):
    half_dim = HD // 2
    offsets = (jnp.arange(start.shape[0], dtype=jnp.int32) - start).astype(jnp.float32)
    frequency = jnp.exp(jnp.arange(half_dim, dtype=jnp.float32) * (-math.log(10000.0) / half_dim))
    angles = frequency[:, None] * offsets[None, :]
    return jnp.cos(angles), jnp.sin(angles)


def rotate(rows, cos_table, sin_table):
    count, length = rows.shape
    parts = rows.reshape(count // HD, 2, HD // 2, length)
    low, high = parts[:, 0], parts[:, 1]
    turned = jnp.stack(
        [low * cos_table - high * sin_table, high * cos_table + low * sin_table], axis=1
    )
    return turned.reshape(count, length)


def rms_factor(values):
    return lax.rsqrt(jnp.mean(values * values, axis=-1, keepdims=True) + eps_norm)


def rms_back(values_in, factor, gain, grad_normed):
    scaled = grad_normed * gain
    gain_part = jnp.sum(grad_normed * values_in * factor, axis=0)
    inner = jnp.mean(scaled * values_in, axis=-1, keepdims=True)
    return factor * scaled - values_in * (factor * factor * factor) * inner, gain_part


def scatter(partial_sum, axis, dim):
    return lax.psum_scatter(partial_sum, axis, scatter_dimension=dim, tiled=True)


def line_steps(count):
    near_right = [(i, i + 1) for i in range(count - 1)]
    near_left = [(i, i - 1) for i in range(1, count)]
    return near_right, near_left


def line_gather(piece, axis):
    count, me = lax.axis_size(axis), lax.axis_index(axis)
    assert count == 4
    near_right, near_left = line_steps(count)
    one_left = lax.ppermute(piece, axis, near_right)
    one_right = lax.ppermute(piece, axis, near_left)
    two_left = lax.ppermute(one_left, axis, [(1, 2), (2, 3)])
    two_right = lax.ppermute(one_right, axis, [(1, 0), (2, 1)])
    three_left = lax.ppermute(one_left, axis, [(1, 3)])
    three_right = lax.ppermute(one_right, axis, [(2, 0)])
    slots = jnp.concatenate(
        [three_left, two_left, one_left, piece, one_right, two_right, three_right], axis=0
    )
    rows = piece.shape[0]
    return lax.dynamic_slice_in_dim(slots, (count - 1 - me) * rows, count * rows, axis=0)


def line_scatter(partial_sum, axis):
    count, me = lax.axis_size(axis), lax.axis_index(axis)
    assert count == 4
    rows = partial_sum.shape[0] // count
    near_right, near_left = line_steps(count)

    def block(offset):
        first = jnp.clip(me + offset, 0, count - 1) * rows
        return lax.dynamic_slice_in_dim(partial_sum, first, rows, axis=0)

    two_right = lax.ppermute(block(2), axis, [(0, 1), (1, 2)])
    two_left = lax.ppermute(block(-2), axis, [(3, 2), (2, 1)])
    three_right = lax.ppermute(block(3), axis, [(0, 2)])
    three_left = lax.ppermute(block(-3), axis, [(3, 1)])

    def total(*parts):
        return sum(part.astype(jnp.float32) for part in parts)

    right = lax.ppermute(
        total(block(1), two_right, three_right).astype(jnp.bfloat16), axis, near_right
    )
    left = lax.ppermute(
        total(block(-1), two_left, three_left).astype(jnp.bfloat16), axis, near_left
    )
    return total(block(0), right, left)


def plane_gather(piece, axis, sizes):
    core, across, along = ([(i, i ^ bit) for i in range(8)] for bit in (1, 2, 4))
    half = piece.shape[0] // 2
    top, low = piece[:half], piece[half:]

    def partner(part):
        return lax.ppermute(part, axis, core)

    top_x, low_y = lax.ppermute(top, axis, across), lax.ppermute(low, axis, along)
    top_y, low_x = lax.ppermute(top, axis, along), lax.ppermute(low, axis, across)
    top_xy, low_xy = lax.ppermute(top_x, axis, along), lax.ppermute(low_y, axis, across)
    held = [(top, low), (top_x, low_x), (top_y, low_y), (top_xy, low_xy)]
    parts = []
    for pair in held:
        parts += [pair, tuple(partner(part) for part in pair)]

    flat = [part for pair in parts for part in pair]
    lanes = jnp.arange(8, dtype=jnp.int32) ^ lax.axis_index(axis).astype(jnp.int32)
    return assemble(lanes * piece.shape[1], flat, sizes, 8 * piece.shape[1])


def exchange_sum(partial_sum, axis):
    count = lax.axis_size(axis)
    parts = partial_sum.reshape((count, partial_sum.shape[0] // count) + partial_sum.shape[1:])
    swapped = lax.all_to_all(parts, axis, split_axis=0, concat_axis=0, tiled=True)
    return jnp.sum(swapped.astype(jnp.float32), axis=0)


def local(
    inputs, segments, w_query, w_key, w_value, w_output, w_gate, w_up, w_down,
    gain_attn, gain_ffn, cotangent,
):
    low = jnp.bfloat16
    n_dp, n_mp = lax.axis_size("dp"), lax.axis_size("mp")
    batches, tokens, width = inputs.shape
    cols = w_query.shape[1]
    depth = w_query.shape[0]
    hidden_part = w_gate.shape[1]

    def split16(gain):
        high = gain.astype(low)
        return high, (gain - high.astype(jnp.float32)).astype(low)

    pieces = split16(gain_attn) + split16(gain_ffn)
    gain_row = jnp.concatenate(pieces + (jnp.zeros((3 * cols - 4 * depth,), low),))
    qkv_piece = jnp.concatenate(
        [
            jnp.concatenate([w_query, w_key, w_value], axis=1),
            jnp.pad(gain_row[None], ((0, 15), (0, 0))),
        ],
        axis=0,
    )
    qkv_all = lax.all_gather(qkv_piece, "dp", axis=0, tiled=False)
    w_qkv = qkv_all[:, :depth].reshape(width, 3 * cols)
    gains = qkv_all[:, depth, : 4 * depth].astype(jnp.float32).reshape(n_dp, 4, depth)
    gain_one = (gains[:, 0] + gains[:, 1]).reshape(width)
    gain_two = (gains[:, 2] + gains[:, 3]).reshape(width)

    rest_piece = jnp.concatenate([w_output, w_gate.T, w_up.T, w_down], axis=0)
    sizes = (cols, hidden_part, hidden_part, hidden_part)
    firsts = (0, cols, cols + hidden_part, cols + 2 * hidden_part)
    if n_dp == 8 and depth == 128:
        output_full, gate_full, up_full, down_full = plane_gather(line_gather(rest_piece, "mp"), "dp", sizes)
    else:
        rest_every = lax.all_gather(rest_piece, ("dp", "mp"), axis=0, tiled=False)
        rest_every = rest_every.reshape((n_dp, n_mp) + rest_piece.shape).transpose(1, 2, 0, 3)
        rest_every = rest_every.reshape(n_mp, rest_piece.shape[0], width)
        output_full, gate_full, up_full, down_full = (
            rest_every[:, first : first + size].reshape(n_mp * size, width)
            for first, size in zip(firsts, sizes)
        )

    first_rows = line_gather(inputs[0], "mp")
    first_rows, second_piece = lax.optimization_barrier((first_rows, inputs[1]))
    rows_all = [first_rows, None]

    normed, factors, qkv, tables, starts, lows, mixed, logs = [], [], [], [], [], [], [], []
    for m in range(batches):
        start = row_starts(segments[m, 0])
        cos_table, sin_table = rope_tables(start)
        tables.append((cos_table, sin_table))
        starts.append(start[None])
        lows.append(start[::BQ] // BK)
        if m == 1:
            rows_all[1] = line_gather(second_piece, "mp")
        rows = rows_all[m].astype(jnp.float32)
        factors.append(rms_factor(rows))
        normed.append((rows * factors[m] * gain_one).astype(low))
        pre = dot_dims(w_qkv, normed[m], 0, 1)
        turned_q = rotate(pre[:cols], cos_table, sin_table) * HD ** -0.5
        turned_k = rotate(pre[cols : 2 * cols], cos_table, sin_table)
        qkv.append(jnp.concatenate([turned_q, turned_k, pre[2 * cols :]], axis=0).astype(low))
        out, log = attn_fwd(qkv[m], starts[m], lows[m])
        mixed.append(out)
        logs.append(log)
    mixed_own = []
    for m in range(batches):
        mixed_own.append(
            lax.all_to_all(mixed[m], "mp", split_axis=1, concat_axis=0, tiled=True)
        )
    in_float = inputs.astype(jnp.float32).reshape(batches * tokens, width)
    mixed_both = jnp.concatenate(mixed_own, axis=1)
    hidden_in = in_float + dot_dims(mixed_both, output_full, 0, 0)
    factor_ffn = rms_factor(hidden_in)
    normed_ffn = (hidden_in * factor_ffn * gain_two).astype(low)
    grad_top = cotangent.reshape(batches * tokens, width)
    hidden, grad_gate_pre, grad_up_pre = ffn_main(
        normed_ffn, grad_top, gate_full, up_full, down_full
    )
    grad_normed_ffn = dot_dims(grad_gate_pre, gate_full, 1, 0) + dot_dims(
        grad_up_pre, up_full, 1, 0
    )
    result = (hidden_in + dot_dims(hidden, down_full, 1, 0)).astype(low)
    chunks = width // 128
    every_grad = ffn_grad(normed_ffn, grad_top, hidden, grad_gate_pre, grad_up_pre, chunks)
    if n_dp != chunks:
        every_grad = every_grad.reshape(chunks, 3, n_mp * hidden_part, n_dp // chunks, depth)
        every_grad = every_grad.transpose(0, 3, 1, 2, 4).reshape(n_dp, 3, -1, depth)
    grad_middle, gain_ffn_part = rms_back(hidden_in, factor_ffn, gain_two, grad_normed_ffn)
    grad_hidden_in = grad_top.astype(jnp.float32) + grad_middle
    grad_branch = grad_hidden_in.astype(low)
    grad_mixed = dot_dims(output_full, grad_branch, 1, 1).astype(low)
    grad_mixed_rows = []
    for m in range(batches):
        grad_mixed_rows.append(
            lax.all_to_all(
                grad_mixed[:, m * tokens : (m + 1) * tokens], "mp", split_axis=0,
                concat_axis=1, tiled=True,
            )
        )
    grad_output = dot_dims(grad_branch, mixed_both, 0, 1).astype(low)

    grad_mixed_rows[0], every_grad = lax.optimization_barrier((grad_mixed_rows[0], every_grad))
    mine = scatter(every_grad, "dp", 0)


    grad_qkv, grad_normed = [], []
    gain_attn_part = jnp.zeros((width,), jnp.float32)
    for m in range(batches):
        cos_table, sin_table = tables[m]
        back = attn_bwd(
            qkv[m], grad_mixed_rows[m], mixed[m], logs[m], starts[m], lows[m], cos_table,
            sin_table,
        ).reshape(3 * cols, n_mp * tokens)
        grad_qkv.append(back)
        spread = dot_dims(back, w_qkv, 0, 1).astype(low)
        if m == 0:
            spread, grad_mixed_rows[1] = lax.optimization_barrier((spread, grad_mixed_rows[1]))
        grad_normed.append(line_scatter(spread, "mp"))
        gain_attn_part = gain_attn_part + jnp.sum(
            spread.astype(jnp.float32) * rows_all[m].astype(jnp.float32) * factors[m], axis=0
        )
    grad_w = 0.0
    for m in range(batches):
        grad_w = grad_w + dot_dims(normed[m], grad_qkv[m], 0, 1)

    own_out = exchange_sum(grad_output, "dp").astype(low).T.reshape(n_mp, cols, depth)
    own_ffn = mine.reshape(3, n_mp, hidden_part, depth).transpose(1, 0, 2, 3)
    own_rest = jnp.concatenate([own_out, own_ffn.reshape(n_mp, -1, depth)], axis=1)
    own_rest = own_rest.reshape(-1, depth)
    own_rest = line_scatter(own_rest, "mp")
    own_output, own_gate, own_up, own_down = (
        own_rest[first : first + size] for first, size in zip(firsts, sizes)
    )
    own_qkv = exchange_sum(grad_w.astype(low), "dp")

    grad_normed_attn = jnp.concatenate(grad_normed, axis=0)
    grad_lower, _ = rms_back(in_float, rms_factor(in_float), gain_one, grad_normed_attn)
    grad_inputs = (grad_hidden_in + grad_lower).astype(low)
    grad_norms = exchange_sum(
        jnp.stack([gain_attn_part, gain_ffn_part], axis=1), ("dp", "mp")
    ).T
    return (
        result.reshape(inputs.shape),
        grad_inputs.reshape(inputs.shape),
        own_qkv[:, :cols],
        own_qkv[:, cols : 2 * cols],
        own_qkv[:, 2 * cols :],
        own_output,
        own_gate.T,
        own_up.T,
        own_down,
        grad_norms[0],
        grad_norms[1],
    )


def solution(mesh):
    row_spec = P(None, ("dp", "mp"), None)
    first, second = P("dp", "mp"), P("mp", "dp")
    both = P(("dp", "mp"))

    return jax.shard_map(
        local,
        mesh=mesh,
        in_specs=(
            row_spec, P(None, "dp", None), first, first, first, second, first, first, second,
            P("dp"), P("dp"), row_spec,
        ),
        out_specs=(
            row_spec, row_spec, first, first, first, second, first, first, second, both, both,
        ),
        check_vma=False,
    )
```

```python
import functools
import math

import jax
import jax.numpy as jnp
from jax import lax
from jax.experimental import pallas as pl
from jax.experimental.pallas import tpu as pltpu
from jax.sharding import PartitionSpec as P


HD = 64
BQ = 512
BK = 256
BK_FORWARD = 512
HPS = 4


def attn_fwd_kernel(lo_ref, q_ref, k_ref, v_ref, start_ref, o_ref, lse_ref, k_scr, *, bq, bk, heads):
    length = q_ref.shape[1]
    k_scr[...] = k_ref[...].T

    def q_step(qi, carry):
        q0 = pl.multiple_of(qi * bq, bq)
        qcols = pl.ds(q0, bq)
        q_blk = q_ref[:, qcols]
        start = start_ref[:, qcols]
        q_idx = q0 + lax.broadcasted_iota(jnp.int32, (1, bq), 1)

        def k_step(kb, state):
            k0 = pl.multiple_of(kb * bk, bk)
            k_idx = k0 + lax.broadcasted_iota(jnp.int32, (bk, bq), 0)
            allowed = (k_idx >= start) & (k_idx <= q_idx)
            out = []
            for h in range(heads):
                peak, total, acc = state[h]
                s = jnp.dot(k_scr[pl.ds(k0, bk), h * HD:(h + 1) * HD], q_blk[h * HD:(h + 1) * HD], preferred_element_type=jnp.float32)
                s = jnp.where(allowed, s, -1e30)
                new_peak = jnp.maximum(peak, jnp.max(s, axis=0, keepdims=True))
                p = jnp.exp(s - new_peak)
                fade = jnp.exp(peak - new_peak)
                total = total * fade + jnp.sum(p, axis=0, keepdims=True)
                acc = acc * fade + jnp.dot(v_ref[h * HD:(h + 1) * HD, pl.ds(k0, bk)], p.astype(jnp.bfloat16), preferred_element_type=jnp.float32)
                out.append((new_peak, total, acc))
            return tuple(out)

        init = tuple((jnp.full((1, bq), -1e30, jnp.float32), jnp.zeros((1, bq), jnp.float32), jnp.zeros((HD, bq), jnp.float32)) for _ in range(heads))
        hi = (q0 + bq - 1) // bk
        state = lax.fori_loop(lo_ref[qi], hi + 1, k_step, init)
        for h in range(heads):
            peak, total, acc = state[h]
            o_ref[h * HD:(h + 1) * HD, qcols] = (acc / total).astype(jnp.bfloat16)
            lse_ref[h, :, qcols] = peak + jnp.log(total)
        return carry

    lax.fori_loop(0, length // bq, q_step, 0)


def attn_bwd_kernel(lo_ref, q_ref, k_ref, v_ref, do_ref, o_ref, lse_ref, start_ref, cos_ref, sin_ref, out_ref, k_scr, v_scr, dk_scr, dv_scr, *, bq, bk, heads):
    length = q_ref.shape[1]
    k_scr[...] = k_ref[...].T
    v_scr[...] = v_ref[...].T
    dk_scr[...] = jnp.zeros_like(dk_scr)
    dv_scr[...] = jnp.zeros_like(dv_scr)
    half = HD // 2

    def unrotate(g, cos, sin):
        a, b = g[:half], g[half:]
        return jnp.concatenate([a * cos + b * sin, b * cos - a * sin], axis=0).astype(jnp.bfloat16)

    def q_step(qi, carry):
        q0 = pl.multiple_of(qi * bq, bq)
        qcols = pl.ds(q0, bq)
        q_blk = q_ref[:, qcols]
        do_blk = do_ref[:, qcols]
        q_t = q_blk.T
        do_t = do_blk.T
        prod = do_blk.astype(jnp.float32) * o_ref[:, qcols].astype(jnp.float32)
        start = start_ref[:, qcols]
        q_idx = q0 + lax.broadcasted_iota(jnp.int32, (1, bq), 1)
        deltas = [jnp.sum(prod[h * HD:(h + 1) * HD], axis=0, keepdims=True) for h in range(heads)]
        lses = [lse_ref[h, :, qcols] for h in range(heads)]

        def k_step(kb, state):
            k0 = pl.multiple_of(kb * bk, bk)
            rows = pl.ds(k0, bk)
            k_idx = k0 + lax.broadcasted_iota(jnp.int32, (bk, bq), 0)
            allowed = (k_idx >= start) & (k_idx <= q_idx)
            out = []
            for h in range(heads):
                hs = slice(h * HD, (h + 1) * HD)
                s = jnp.dot(k_scr[rows, hs], q_blk[hs], preferred_element_type=jnp.float32)
                p = jnp.exp(jnp.where(allowed, s - lses[h], -1e30))
                dp = jnp.dot(v_scr[rows, hs], do_blk[hs], preferred_element_type=jnp.float32)
                ds = (p * (dp - deltas[h])).astype(jnp.bfloat16)
                dv_scr[h, rows, :] += jnp.dot(p.astype(jnp.bfloat16), do_t[:, hs], preferred_element_type=jnp.float32)
                dk_scr[h, rows, :] += jnp.dot(ds, q_t[:, hs], preferred_element_type=jnp.float32)
                out.append(state[h] + jnp.dot(k_ref[hs, rows], ds, preferred_element_type=jnp.float32))
            return tuple(out)

        init = tuple(jnp.zeros((HD, bq), jnp.float32) for _ in range(heads))
        hi = (q0 + bq - 1) // bk
        state = lax.fori_loop(lo_ref[qi], hi + 1, k_step, init)
        cos, sin = cos_ref[:, qcols], sin_ref[:, qcols]
        for h in range(heads):
            out_ref[0, h * HD:(h + 1) * HD, qcols] = unrotate(state[h] * HD ** -0.5, cos, sin)
        return carry

    lax.fori_loop(0, length // bq, q_step, 0)
    for h in range(heads):
        out_ref[1, h * HD:(h + 1) * HD, :] = unrotate(dk_scr[h].T, cos_ref[...], sin_ref[...])
        out_ref[2, h * HD:(h + 1) * HD, :] = dv_scr[h].T.astype(jnp.bfloat16)


def attn_fwd(qkv_t, start, lo, bq=BQ, bk=BK_FORWARD, hps=HPS):
    cols3, length = qkv_t.shape
    cols = cols3 // 3
    steps = cols // (HD * hps)
    blk = (HD * hps, length)
    area = cols * length * length // 4
    return pl.pallas_call(
        functools.partial(attn_fwd_kernel, bq=bq, bk=bk, heads=hps),
        out_shape=(jax.ShapeDtypeStruct((cols, length), jnp.bfloat16), jax.ShapeDtypeStruct((cols // HD, 1, length), jnp.float32)),
        grid_spec=pltpu.PrefetchScalarGridSpec(
            num_scalar_prefetch=1, grid=(steps,),
            in_specs=[pl.BlockSpec(blk, lambda i, lo: (i, 0)), pl.BlockSpec(blk, lambda i, lo: (i + steps, 0)), pl.BlockSpec(blk, lambda i, lo: (i + 2 * steps, 0)),
                      pl.BlockSpec((1, length), lambda i, lo: (0, 0))],
            out_specs=[pl.BlockSpec(blk, lambda i, lo: (i, 0)), pl.BlockSpec((hps, 1, length), lambda i, lo: (i, 0, 0))],
            scratch_shapes=[pltpu.VMEM((length, HD * hps), jnp.bfloat16)]),
        cost_estimate=pl.CostEstimate(flops=16 * area, bytes_accessed=cols * length * 8, transcendentals=area // HD),
        name="attn_fwd",
    )(lo, qkv_t, qkv_t, qkv_t, start)


def attn_bwd(qkv_t, do_t, o_t, lse, start, lo, cos, sin, bq=BQ, bk=BK, hps=HPS):
    cols3, length = qkv_t.shape
    cols = cols3 // 3
    steps = cols // (HD * hps)
    blk = (HD * hps, length)
    area = cols * length * length // 4
    return pl.pallas_call(
        functools.partial(attn_bwd_kernel, bq=bq, bk=bk, heads=hps),
        out_shape=jax.ShapeDtypeStruct((3, cols, length), jnp.bfloat16),
        grid_spec=pltpu.PrefetchScalarGridSpec(
            num_scalar_prefetch=1, grid=(steps,),
            in_specs=[pl.BlockSpec(blk, lambda i, lo: (i, 0)), pl.BlockSpec(blk, lambda i, lo: (i + steps, 0)), pl.BlockSpec(blk, lambda i, lo: (i + 2 * steps, 0)),
                      pl.BlockSpec(blk, lambda i, lo: (i, 0)), pl.BlockSpec(blk, lambda i, lo: (i, 0)),
                      pl.BlockSpec((hps, 1, length), lambda i, lo: (i, 0, 0)),
                      pl.BlockSpec((1, length), lambda i, lo: (0, 0)),
                      pl.BlockSpec((HD // 2, length), lambda i, lo: (0, 0)), pl.BlockSpec((HD // 2, length), lambda i, lo: (0, 0))],
            out_specs=pl.BlockSpec((3,) + blk, lambda i, lo: (0, i, 0)),
            scratch_shapes=[pltpu.VMEM((length, HD * hps), jnp.bfloat16)] * 2 + [pltpu.VMEM((hps, length, HD), jnp.float32)] * 2),
        cost_estimate=pl.CostEstimate(flops=40 * area, bytes_accessed=cols * length * 20, transcendentals=area // HD),
        name="attn_bwd",
    )(lo, qkv_t, qkv_t, qkv_t, do_t, o_t, lse, start, cos, sin)


def assemble_kernel(lane_ref, *refs, sizes, parts):
    pieces, outs = refs[: 2 * parts], refs[2 * parts : 2 * parts + len(sizes)]
    held, in_sem, out_sem = refs[2 * parts + len(sizes) :]
    slots = held.shape[0]
    total = sum(sizes)
    steps = [
        (block, part, sum(sizes[:part])) for block in range(4) for part in range(len(sizes))
    ]

    def fetch(step):
        block, part, first = steps[step]
        rows = pl.ds((block % 2) * total + first, sizes[part])
        slot = step % slots
        return [
            pltpu.make_async_copy(
                pieces[2 * r + block // 2].at[rows],
                held.at[slot, pl.ds(0, sizes[part]), pl.ds(pl.multiple_of(lane_ref[r], 128), 128)],
                in_sem.at[slot, r],
            )
            for r in range(parts)
        ]

    def put(step):
        block, part, _ = steps[step]
        slot = step % slots
        return pltpu.make_async_copy(
            held.at[slot, pl.ds(0, sizes[part])],
            outs[part].at[pl.ds(block * sizes[part], sizes[part])],
            out_sem.at[slot],
        )

    ahead = slots // 2
    for step in range(ahead):
        for copy in fetch(step):
            copy.start()
    for step in range(len(steps)):
        later = step + ahead
        if later < len(steps):
            if later >= slots:
                put(later - slots).wait()
            for copy in fetch(later):
                copy.start()
        for copy in fetch(step):
            copy.wait()
        put(step).start()
    for step in range(len(steps) - slots, len(steps)):
        put(step).wait()


def assemble(lanes, pieces, sizes, width):
    parts = len(pieces) // 2
    whole = pl.BlockSpec(memory_space=pl.ANY)
    return pl.pallas_call(
        functools.partial(assemble_kernel, sizes=sizes, parts=parts),
        out_shape=[jax.ShapeDtypeStruct((4 * size, width), jnp.bfloat16) for size in sizes],
        grid_spec=pltpu.PrefetchScalarGridSpec(
            num_scalar_prefetch=1,
            grid=(1,),
            in_specs=[whole] * len(pieces),
            out_specs=[whole] * len(sizes),
            scratch_shapes=[
                pltpu.VMEM((4, max(sizes), width), jnp.bfloat16),
                pltpu.SemaphoreType.DMA((4, parts)),
                pltpu.SemaphoreType.DMA((4,)),
            ],
        ),
        cost_estimate=pl.CostEstimate(
            flops=0, bytes_accessed=16 * sum(sizes) * width, transcendentals=0
        ),
        name="assemble",
    )(lanes, *pieces)


def dot_in(left, right, left_dim, right_dim):
    return lax.dot_general(
        left, right, (((left_dim,), (right_dim,)), ((), ())), preferred_element_type=jnp.float32
    )


def ffn_main_kernel(x_ref, c_ref, gate_ref, up_ref, down_ref, h_ref, dg_ref, du_ref, *, step):
    for first in range(0, x_ref.shape[0], step):
        rows = slice(first, first + step)
        gate = dot_in(x_ref[rows], gate_ref[...], 1, 1)
        up = dot_in(x_ref[rows], up_ref[...], 1, 1)
        grad_hidden = dot_in(c_ref[rows], down_ref[...], 1, 1)
        sig = jax.nn.sigmoid(gate)
        silu = gate * sig
        h_ref[rows] = (silu * up).astype(jnp.bfloat16)
        dg = (grad_hidden * up * sig * (1.0 + gate * (1.0 - sig))).astype(jnp.bfloat16)
        du = (grad_hidden * silu).astype(jnp.bfloat16)
        dg_ref[rows] = dg
        du_ref[rows] = du


def ffn_grad_kernel(x_ref, c_ref, h_ref, dg_ref, du_ref, g_ref):
    for place, (left, right) in enumerate(((dg_ref, x_ref), (du_ref, x_ref), (h_ref, c_ref))):
        grad = dot_in(left[...], right[...], 0, 0).astype(jnp.bfloat16)
        for i in range(g_ref.shape[0]):
            g_ref[i, place] = grad[:, i * g_ref.shape[3] : (i + 1) * g_ref.shape[3]]


def ffn_main(x, c, gate, up, down, tile=256, step=256):
    tokens, width = x.shape
    units = gate.shape[0]
    full = pl.BlockSpec((tokens, width), lambda t: (0, 0))
    weight = pl.BlockSpec((tile, width), lambda t: (t, 0))
    column = pl.BlockSpec((tokens, tile), lambda t: (0, t))
    return pl.pallas_call(
        functools.partial(ffn_main_kernel, step=step),
        out_shape=[jax.ShapeDtypeStruct((tokens, units), jnp.bfloat16)] * 3,
        grid=(units // tile,),
        in_specs=[full, full, weight, weight, weight],
        out_specs=[column, column, column],
        cost_estimate=pl.CostEstimate(
            flops=6 * tokens * width * units, bytes_accessed=6 * units * (width + tokens),
            transcendentals=tokens * units,
        ),
        name="ffn_main",
    )(x, c, gate, up, down)


def ffn_grad(x, c, hidden, dg, du, chunks, tile=256):
    tokens, width = x.shape
    units = hidden.shape[1]
    full = pl.BlockSpec((tokens, width), lambda t: (0, 0))
    column = pl.BlockSpec((tokens, tile), lambda t: (0, t))
    piece = width // chunks
    return pl.pallas_call(
        ffn_grad_kernel,
        out_shape=jax.ShapeDtypeStruct((chunks, 3, units, piece), jnp.bfloat16),
        grid=(units // tile,),
        in_specs=[full, full, column, column, column],
        out_specs=pl.BlockSpec((chunks, 3, tile, piece), lambda t: (0, 0, t, 0)),
        cost_estimate=pl.CostEstimate(
            flops=6 * tokens * width * units, bytes_accessed=6 * units * (width + tokens),
            transcendentals=0,
        ),
        name="ffn_grad",
    )(x, c, hidden, dg, du)


eps_norm = 1e-05


def dot_dims(left, right, left_dim, right_dim):
    return lax.dot_general(
        left, right, (((left_dim,), (right_dim,)), ((), ())), preferred_element_type=jnp.float32
    )


def row_starts(seg_row):
    ones = [jnp.sum((seg_row < s).astype(jnp.int32)) for s in (1, 2, 3)]
    start = jnp.zeros_like(seg_row)
    before = 0
    for s, count in zip((1, 2, 3), ones):
        start = start + jnp.where(seg_row >= s, count - before, 0)
        before = count
    return start


def rope_tables(start):
    half_dim = HD // 2
    offsets = (jnp.arange(start.shape[0], dtype=jnp.int32) - start).astype(jnp.float32)
    frequency = jnp.exp(jnp.arange(half_dim, dtype=jnp.float32) * (-math.log(10000.0) / half_dim))
    angles = frequency[:, None] * offsets[None, :]
    return jnp.cos(angles), jnp.sin(angles)


def rotate(rows, cos_table, sin_table):
    count, length = rows.shape
    parts = rows.reshape(count // HD, 2, HD // 2, length)
    low, high = parts[:, 0], parts[:, 1]
    turned = jnp.stack(
        [low * cos_table - high * sin_table, high * cos_table + low * sin_table], axis=1
    )
    return turned.reshape(count, length)


def rms_factor(values):
    return lax.rsqrt(jnp.mean(values * values, axis=-1, keepdims=True) + eps_norm)


def rms_back(values_in, factor, gain, grad_normed):
    scaled = grad_normed * gain
    gain_part = jnp.sum(grad_normed * values_in * factor, axis=0)
    inner = jnp.mean(scaled * values_in, axis=-1, keepdims=True)
    return factor * scaled - values_in * (factor * factor * factor) * inner, gain_part


def scatter(partial_sum, axis, dim):
    return lax.psum_scatter(partial_sum, axis, scatter_dimension=dim, tiled=True)


def line_steps(count):
    near_right = [(i, i + 1) for i in range(count - 1)]
    near_left = [(i, i - 1) for i in range(1, count)]
    return near_right, near_left


def line_gather(piece, axis):
    count, me = lax.axis_size(axis), lax.axis_index(axis)
    assert count == 4
    near_right, near_left = line_steps(count)
    one_left = lax.ppermute(piece, axis, near_right)
    one_right = lax.ppermute(piece, axis, near_left)
    two_left = lax.ppermute(one_left, axis, [(1, 2), (2, 3)])
    two_right = lax.ppermute(one_right, axis, [(1, 0), (2, 1)])
    three_left = lax.ppermute(one_left, axis, [(1, 3)])
    three_right = lax.ppermute(one_right, axis, [(2, 0)])
    slots = jnp.concatenate(
        [three_left, two_left, one_left, piece, one_right, two_right, three_right], axis=0
    )
    rows = piece.shape[0]
    return lax.dynamic_slice_in_dim(slots, (count - 1 - me) * rows, count * rows, axis=0)


def line_scatter(partial_sum, axis):
    count, me = lax.axis_size(axis), lax.axis_index(axis)
    assert count == 4
    rows = partial_sum.shape[0] // count
    near_right, near_left = line_steps(count)

    def block(offset):
        first = jnp.clip(me + offset, 0, count - 1) * rows
        return lax.dynamic_slice_in_dim(partial_sum, first, rows, axis=0)

    two_right = lax.ppermute(block(2), axis, [(0, 1), (1, 2)])
    two_left = lax.ppermute(block(-2), axis, [(3, 2), (2, 1)])
    three_right = lax.ppermute(block(3), axis, [(0, 2)])
    three_left = lax.ppermute(block(-3), axis, [(3, 1)])

    def total(*parts):
        return sum(part.astype(jnp.float32) for part in parts)

    right = lax.ppermute(
        total(block(1), two_right, three_right).astype(jnp.bfloat16), axis, near_right
    )
    left = lax.ppermute(
        total(block(-1), two_left, three_left).astype(jnp.bfloat16), axis, near_left
    )
    return total(block(0), right, left)


def plane_gather(piece, axis, sizes):
    core, across, along = ([(i, i ^ bit) for i in range(8)] for bit in (1, 2, 4))
    half = piece.shape[0] // 2
    top, low = piece[:half], piece[half:]

    def partner(part):
        return lax.ppermute(part, axis, core)

    top_x, low_y = lax.ppermute(top, axis, across), lax.ppermute(low, axis, along)
    top_y, low_x = lax.ppermute(top, axis, along), lax.ppermute(low, axis, across)
    top_xy, low_xy = lax.ppermute(top_x, axis, along), lax.ppermute(low_y, axis, across)
    held = [(top, low), (top_x, low_x), (top_y, low_y), (top_xy, low_xy)]
    parts = []
    for pair in held:
        parts += [pair, tuple(partner(part) for part in pair)]

    flat = [part for pair in parts for part in pair]
    lanes = jnp.arange(8, dtype=jnp.int32) ^ lax.axis_index(axis).astype(jnp.int32)
    return assemble(lanes * piece.shape[1], flat, sizes, 8 * piece.shape[1])


def local(
    inputs, segments, w_query, w_key, w_value, w_output, w_gate, w_up, w_down,
    gain_attn, gain_ffn, cotangent,
):
    low = jnp.bfloat16
    n_dp, n_mp = lax.axis_size("dp"), lax.axis_size("mp")
    batches, tokens, width = inputs.shape
    cols = w_query.shape[1]
    depth = w_query.shape[0]
    hidden_part = w_gate.shape[1]

    def split16(gain):
        high = gain.astype(low)
        return high, (gain - high.astype(jnp.float32)).astype(low)

    pieces = split16(gain_attn) + split16(gain_ffn)
    gain_row = jnp.concatenate(pieces + (jnp.zeros((3 * cols - 4 * depth,), low),))
    qkv_piece = jnp.concatenate(
        [
            jnp.concatenate([w_query, w_key, w_value], axis=1),
            jnp.pad(gain_row[None], ((0, 15), (0, 0))),
        ],
        axis=0,
    )
    qkv_all = lax.all_gather(qkv_piece, "dp", axis=0, tiled=False)
    w_qkv = qkv_all[:, :depth].reshape(width, 3 * cols)
    gains = qkv_all[:, depth, : 4 * depth].astype(jnp.float32).reshape(n_dp, 4, depth)
    gain_one = (gains[:, 0] + gains[:, 1]).reshape(width)
    gain_two = (gains[:, 2] + gains[:, 3]).reshape(width)

    rest_piece = jnp.concatenate([w_output, w_gate.T, w_up.T, w_down], axis=0)
    sizes = (cols, hidden_part, hidden_part, hidden_part)
    firsts = (0, cols, cols + hidden_part, cols + 2 * hidden_part)
    if n_dp == 8 and depth == 128:
        output_full, gate_full, up_full, down_full = plane_gather(line_gather(rest_piece, "mp"), "dp", sizes)
    else:
        rest_every = lax.all_gather(rest_piece, ("dp", "mp"), axis=0, tiled=False)
        rest_every = rest_every.reshape((n_dp, n_mp) + rest_piece.shape).transpose(1, 2, 0, 3)
        rest_every = rest_every.reshape(n_mp, rest_piece.shape[0], width)
        output_full, gate_full, up_full, down_full = (
            rest_every[:, first : first + size].reshape(n_mp * size, width)
            for first, size in zip(firsts, sizes)
        )

    first_rows = line_gather(inputs[0], "mp")
    first_rows, second_piece = lax.optimization_barrier((first_rows, inputs[1]))
    rows_all = [first_rows, None]

    normed, factors, qkv, tables, starts, lows, mixed, logs = [], [], [], [], [], [], [], []
    for m in range(batches):
        start = row_starts(segments[m, 0])
        cos_table, sin_table = rope_tables(start)
        tables.append((cos_table, sin_table))
        starts.append(start[None])
        lows.append((start[::BQ] // BK_FORWARD, start[::BQ] // BK))
        if m == 1:
            rows_all[1] = line_gather(second_piece, "mp")
        rows = rows_all[m].astype(jnp.float32)
        factors.append(rms_factor(rows))
        normed.append((rows * factors[m] * gain_one).astype(low))
        pre = dot_dims(w_qkv, normed[m], 0, 1)
        turned_q = rotate(pre[:cols], cos_table, sin_table) * HD ** -0.5
        turned_k = rotate(pre[cols : 2 * cols], cos_table, sin_table)
        qkv.append(jnp.concatenate([turned_q, turned_k, pre[2 * cols :]], axis=0).astype(low))
        out, log = attn_fwd(qkv[m], starts[m], lows[m][0])
        mixed.append(out)
        logs.append(log)
    mixed_own = []
    for m in range(batches):
        mixed_own.append(
            lax.all_to_all(mixed[m], "mp", split_axis=1, concat_axis=0, tiled=True)
        )
    in_float = inputs.astype(jnp.float32).reshape(batches * tokens, width)
    mixed_both = jnp.concatenate(mixed_own, axis=1)
    hidden_in = in_float + dot_dims(mixed_both, output_full, 0, 0)
    factor_ffn = rms_factor(hidden_in)
    normed_ffn = (hidden_in * factor_ffn * gain_two).astype(low)
    grad_top = cotangent.reshape(batches * tokens, width)
    hidden, grad_gate_pre, grad_up_pre = ffn_main(
        normed_ffn, grad_top, gate_full, up_full, down_full
    )
    grad_normed_ffn = dot_dims(grad_gate_pre, gate_full, 1, 0) + dot_dims(
        grad_up_pre, up_full, 1, 0
    )
    result = (hidden_in + dot_dims(hidden, down_full, 1, 0)).astype(low)
    chunks = width // 128
    every_grad = ffn_grad(normed_ffn, grad_top, hidden, grad_gate_pre, grad_up_pre, chunks)
    if n_dp != chunks:
        every_grad = every_grad.reshape(chunks, 3, n_mp * hidden_part, n_dp // chunks, depth)
        every_grad = every_grad.transpose(0, 3, 1, 2, 4).reshape(n_dp, 3, -1, depth)
    grad_middle, gain_ffn_part = rms_back(hidden_in, factor_ffn, gain_two, grad_normed_ffn)
    grad_hidden_in = grad_top.astype(jnp.float32) + grad_middle
    grad_branch = grad_hidden_in.astype(low)
    grad_mixed = dot_dims(output_full, grad_branch, 1, 1).astype(low)
    grad_mixed_rows = []
    for m in range(batches):
        grad_mixed_rows.append(
            lax.all_to_all(
                grad_mixed[:, m * tokens : (m + 1) * tokens], "mp", split_axis=0,
                concat_axis=1, tiled=True,
            )
        )
    grad_output = dot_dims(grad_branch, mixed_both, 0, 1).astype(low)

    grad_mixed_rows[0], every_grad = lax.optimization_barrier((grad_mixed_rows[0], every_grad))
    mine = scatter(every_grad, "dp", 0)


    grad_qkv, grad_normed = [], []
    gain_attn_part = jnp.zeros((width,), jnp.float32)
    for m in range(batches):
        cos_table, sin_table = tables[m]
        back = attn_bwd(
            qkv[m], grad_mixed_rows[m], mixed[m], logs[m], starts[m], lows[m][1], cos_table,
            sin_table,
        ).reshape(3 * cols, n_mp * tokens)
        grad_qkv.append(back)
        spread = dot_dims(back, w_qkv, 0, 1).astype(low)
        if m == 0:
            spread, grad_mixed_rows[1] = lax.optimization_barrier((spread, grad_mixed_rows[1]))
        grad_normed.append(line_scatter(spread, "mp"))
        gain_attn_part = gain_attn_part + jnp.sum(
            spread.astype(jnp.float32) * rows_all[m].astype(jnp.float32) * factors[m], axis=0
        )
    grad_w = 0.0
    for m in range(batches):
        grad_w = grad_w + dot_dims(normed[m], grad_qkv[m], 0, 1)

    gain_parts = jnp.stack([gain_attn_part, gain_ffn_part]).astype(low)
    gain_parts = gain_parts.reshape(2, n_dp, depth).transpose(1, 0, 2).reshape(n_dp, 1, 2 * depth)
    sums = jnp.concatenate(
        [
            grad_w.astype(low).reshape(n_dp, depth, 3 * cols),
            grad_output.reshape(n_dp, depth, n_mp * cols),
        ],
        axis=2,
    )
    gain_rows = jnp.pad(gain_parts, ((0, 0), (0, 15), (0, sums.shape[2] - 2 * depth)))
    sums = jnp.concatenate([sums, gain_rows], axis=1)
    sums = lax.all_to_all(sums, "dp", split_axis=0, concat_axis=0, tiled=True)
    sums = jnp.sum(sums.astype(jnp.float32), axis=0)
    own_qkv, own_out = sums[:depth, : 3 * cols], sums[:depth, 3 * cols :]
    own_gain = sums[depth, : 2 * depth].reshape(2, n_mp, depth // n_mp).transpose(1, 0, 2)
    own_gain = own_gain.reshape(n_mp, 1, 2 * depth // n_mp)
    own_gain = jnp.pad(own_gain.astype(low), ((0, 0), (0, 15), (0, depth - own_gain.shape[2])))
    own_ffn = mine.reshape(3, n_mp, hidden_part, depth).transpose(1, 0, 2, 3)
    own_rest = jnp.concatenate(
        [
            own_out.T.astype(low).reshape(n_mp, cols, depth),
            own_ffn.reshape(n_mp, -1, depth),
            own_gain,
        ],
        axis=1,
    )
    own_rest = own_rest.reshape(-1, depth)
    own_rest = line_scatter(own_rest, "mp")
    own_output, own_gate, own_up, own_down = (
        own_rest[first : first + size] for first, size in zip(firsts, sizes)
    )
    grad_norms = own_rest[sum(sizes), : 2 * depth // n_mp].reshape(2, -1)

    grad_normed_attn = jnp.concatenate(grad_normed, axis=0)
    grad_lower, _ = rms_back(in_float, rms_factor(in_float), gain_one, grad_normed_attn)
    grad_inputs = (grad_hidden_in + grad_lower).astype(low)
    return (
        result.reshape(inputs.shape),
        grad_inputs.reshape(inputs.shape),
        own_qkv[:, :cols],
        own_qkv[:, cols : 2 * cols],
        own_qkv[:, 2 * cols :],
        own_output,
        own_gate.T,
        own_up.T,
        own_down,
        grad_norms[0],
        grad_norms[1],
    )


def solution(mesh):
    row_spec = P(None, ("dp", "mp"), None)
    first, second = P("dp", "mp"), P("mp", "dp")
    both = P(("dp", "mp"))

    return jax.shard_map(
        local,
        mesh=mesh,
        in_specs=(
            row_spec, P(None, "dp", None), first, first, first, second, first, first, second,
            P("dp"), P("dp"), row_spec,
        ),
        out_specs=(
            row_spec, row_spec, first, first, first, second, first, first, second, both, both,
        ),
        check_vma=False,
    )
```

```python
import functools
import math

import jax
import jax.numpy as jnp
from jax import lax
from jax.experimental import pallas as pl
from jax.experimental.pallas import tpu as pltpu
from jax.sharding import PartitionSpec as P


HD = 64
BQ = 512
BK = 256
BK_FORWARD = 256
HPS = 4


def attn_fwd_kernel(lo_ref, q_ref, k_ref, v_ref, start_ref, o_ref, lse_ref, k_scr, *, bq, bk, heads):
    length = q_ref.shape[1]
    k_scr[...] = k_ref[...].T

    def q_step(qi, carry):
        q0 = pl.multiple_of(qi * bq, bq)
        qcols = pl.ds(q0, bq)
        q_blk = q_ref[:, qcols]
        start = start_ref[:, qcols]
        q_idx = q0 + lax.broadcasted_iota(jnp.int32, (1, bq), 1)

        def visit(kb, state, first):
            k0 = pl.multiple_of(kb * bk, bk)
            wide = bq - first
            k_idx = k0 + lax.broadcasted_iota(jnp.int32, (bk, wide), 0)
            allowed = (k_idx >= start[:, first:]) & (k_idx <= q_idx[:, first:])
            out = []
            for h in range(heads):
                peak, total, acc = (part[:, first:] for part in state[h])
                s = jnp.dot(k_scr[pl.ds(k0, bk), h * HD:(h + 1) * HD], q_blk[h * HD:(h + 1) * HD, first:], preferred_element_type=jnp.float32)
                s = jnp.where(allowed, s, -1e30)
                new_peak = jnp.maximum(peak, jnp.max(s, axis=0, keepdims=True))
                p = jnp.exp(s - new_peak)
                fade = jnp.exp(peak - new_peak)
                total = total * fade + jnp.sum(p, axis=0, keepdims=True)
                acc = acc * fade + jnp.dot(v_ref[h * HD:(h + 1) * HD, pl.ds(k0, bk)], p.astype(jnp.bfloat16), preferred_element_type=jnp.float32)
                fresh = (new_peak, total, acc)
                if first:
                    fresh = tuple(jnp.concatenate([old[:, :first], new], axis=1) for old, new in zip(state[h], fresh))
                out.append(fresh)
            return tuple(out)

        init = tuple((jnp.full((1, bq), -1e30, jnp.float32), jnp.zeros((1, bq), jnp.float32), jnp.zeros((HD, bq), jnp.float32)) for _ in range(heads))
        hi = (q0 + bq - 1) // bk
        state = lax.fori_loop(lo_ref[qi], hi, lambda kb, state: visit(kb, state, 0), init)
        state = visit(hi, state, bq - bk)
        for h in range(heads):
            peak, total, acc = state[h]
            o_ref[h * HD:(h + 1) * HD, qcols] = (acc / total).astype(jnp.bfloat16)
            lse_ref[h, :, qcols] = peak + jnp.log(total)
        return carry

    lax.fori_loop(0, length // bq, q_step, 0)


def attn_bwd_kernel(lo_ref, q_ref, k_ref, v_ref, do_ref, o_ref, lse_ref, start_ref, cos_ref, sin_ref, out_ref, k_scr, v_scr, dk_scr, dv_scr, *, bq, bk, heads):
    length = q_ref.shape[1]
    k_scr[...] = k_ref[...].T
    v_scr[...] = v_ref[...].T
    dk_scr[...] = jnp.zeros_like(dk_scr)
    dv_scr[...] = jnp.zeros_like(dv_scr)
    half = HD // 2

    def unrotate(g, cos, sin):
        a, b = g[:half], g[half:]
        return jnp.concatenate([a * cos + b * sin, b * cos - a * sin], axis=0).astype(jnp.bfloat16)

    def q_step(qi, carry):
        q0 = pl.multiple_of(qi * bq, bq)
        qcols = pl.ds(q0, bq)
        q_blk = q_ref[:, qcols]
        do_blk = do_ref[:, qcols]
        q_t = q_blk.T
        do_t = do_blk.T
        prod = do_blk.astype(jnp.float32) * o_ref[:, qcols].astype(jnp.float32)
        start = start_ref[:, qcols]
        q_idx = q0 + lax.broadcasted_iota(jnp.int32, (1, bq), 1)
        deltas = [jnp.sum(prod[h * HD:(h + 1) * HD], axis=0, keepdims=True) for h in range(heads)]
        lses = [lse_ref[h, :, qcols] for h in range(heads)]

        def visit(kb, state, first):
            k0 = pl.multiple_of(kb * bk, bk)
            rows = pl.ds(k0, bk)
            k_idx = k0 + lax.broadcasted_iota(jnp.int32, (bk, bq - first), 0)
            allowed = (k_idx >= start[:, first:]) & (k_idx <= q_idx[:, first:])
            out = []
            for h in range(heads):
                hs = slice(h * HD, (h + 1) * HD)
                s = jnp.dot(k_scr[rows, hs], q_blk[hs, first:], preferred_element_type=jnp.float32)
                p = jnp.exp(jnp.where(allowed, s - lses[h][:, first:], -1e30))
                dp = jnp.dot(v_scr[rows, hs], do_blk[hs, first:], preferred_element_type=jnp.float32)
                ds = (p * (dp - deltas[h][:, first:])).astype(jnp.bfloat16)
                dv_scr[h, rows, :] += jnp.dot(p.astype(jnp.bfloat16), do_t[first:, hs], preferred_element_type=jnp.float32)
                dk_scr[h, rows, :] += jnp.dot(ds, q_t[first:, hs], preferred_element_type=jnp.float32)
                part = jnp.dot(k_ref[hs, rows], ds, preferred_element_type=jnp.float32)
                if first:
                    part = jnp.concatenate([state[h][:, :first], state[h][:, first:] + part], axis=1)
                else:
                    part = state[h] + part
                out.append(part)
            return tuple(out)

        init = tuple(jnp.zeros((HD, bq), jnp.float32) for _ in range(heads))
        hi = (q0 + bq - 1) // bk
        state = lax.fori_loop(lo_ref[qi], hi, lambda kb, state: visit(kb, state, 0), init)
        state = visit(hi, state, bq - bk)
        cos, sin = cos_ref[:, qcols], sin_ref[:, qcols]
        for h in range(heads):
            out_ref[0, h * HD:(h + 1) * HD, qcols] = unrotate(state[h] * HD ** -0.5, cos, sin)
        return carry

    lax.fori_loop(0, length // bq, q_step, 0)
    for h in range(heads):
        out_ref[1, h * HD:(h + 1) * HD, :] = unrotate(dk_scr[h].T, cos_ref[...], sin_ref[...])
        out_ref[2, h * HD:(h + 1) * HD, :] = dv_scr[h].T.astype(jnp.bfloat16)


def attn_fwd(qkv_t, start, lo, bq=BQ, bk=BK_FORWARD, hps=HPS):
    cols3, length = qkv_t.shape
    cols = cols3 // 3
    steps = cols // (HD * hps)
    blk = (HD * hps, length)
    area = cols * length * length // 4
    return pl.pallas_call(
        functools.partial(attn_fwd_kernel, bq=bq, bk=bk, heads=hps),
        out_shape=(jax.ShapeDtypeStruct((cols, length), jnp.bfloat16), jax.ShapeDtypeStruct((cols // HD, 1, length), jnp.float32)),
        grid_spec=pltpu.PrefetchScalarGridSpec(
            num_scalar_prefetch=1, grid=(steps,),
            in_specs=[pl.BlockSpec(blk, lambda i, lo: (i, 0)), pl.BlockSpec(blk, lambda i, lo: (i + steps, 0)), pl.BlockSpec(blk, lambda i, lo: (i + 2 * steps, 0)),
                      pl.BlockSpec((1, length), lambda i, lo: (0, 0))],
            out_specs=[pl.BlockSpec(blk, lambda i, lo: (i, 0)), pl.BlockSpec((hps, 1, length), lambda i, lo: (i, 0, 0))],
            scratch_shapes=[pltpu.VMEM((length, HD * hps), jnp.bfloat16)]),
        cost_estimate=pl.CostEstimate(flops=16 * area, bytes_accessed=cols * length * 8, transcendentals=area // HD),
        name="attn_fwd",
    )(lo, qkv_t, qkv_t, qkv_t, start)


def attn_bwd(qkv_t, do_t, o_t, lse, start, lo, cos, sin, bq=BQ, bk=BK, hps=HPS):
    cols3, length = qkv_t.shape
    cols = cols3 // 3
    steps = cols // (HD * hps)
    blk = (HD * hps, length)
    area = cols * length * length // 4
    return pl.pallas_call(
        functools.partial(attn_bwd_kernel, bq=bq, bk=bk, heads=hps),
        out_shape=jax.ShapeDtypeStruct((3, cols, length), jnp.bfloat16),
        grid_spec=pltpu.PrefetchScalarGridSpec(
            num_scalar_prefetch=1, grid=(steps,),
            in_specs=[pl.BlockSpec(blk, lambda i, lo: (i, 0)), pl.BlockSpec(blk, lambda i, lo: (i + steps, 0)), pl.BlockSpec(blk, lambda i, lo: (i + 2 * steps, 0)),
                      pl.BlockSpec(blk, lambda i, lo: (i, 0)), pl.BlockSpec(blk, lambda i, lo: (i, 0)),
                      pl.BlockSpec((hps, 1, length), lambda i, lo: (i, 0, 0)),
                      pl.BlockSpec((1, length), lambda i, lo: (0, 0)),
                      pl.BlockSpec((HD // 2, length), lambda i, lo: (0, 0)), pl.BlockSpec((HD // 2, length), lambda i, lo: (0, 0))],
            out_specs=pl.BlockSpec((3,) + blk, lambda i, lo: (0, i, 0)),
            scratch_shapes=[pltpu.VMEM((length, HD * hps), jnp.bfloat16)] * 2 + [pltpu.VMEM((hps, length, HD), jnp.float32)] * 2),
        cost_estimate=pl.CostEstimate(flops=40 * area, bytes_accessed=cols * length * 20, transcendentals=area // HD),
        name="attn_bwd",
    )(lo, qkv_t, qkv_t, qkv_t, do_t, o_t, lse, start, cos, sin)


def assemble_kernel(lane_ref, *refs, sizes, parts):
    pieces, outs = refs[: 2 * parts], refs[2 * parts : 2 * parts + len(sizes)]
    held, in_sem, out_sem = refs[2 * parts + len(sizes) :]
    slots = held.shape[0]
    total = sum(sizes)
    steps = [
        (block, part, sum(sizes[:part])) for block in range(4) for part in range(len(sizes))
    ]

    def fetch(step):
        block, part, first = steps[step]
        rows = pl.ds((block % 2) * total + first, sizes[part])
        slot = step % slots
        return [
            pltpu.make_async_copy(
                pieces[2 * r + block // 2].at[rows],
                held.at[slot, pl.ds(0, sizes[part]), pl.ds(pl.multiple_of(lane_ref[r], 128), 128)],
                in_sem.at[slot, r],
            )
            for r in range(parts)
        ]

    def put(step):
        block, part, _ = steps[step]
        slot = step % slots
        return pltpu.make_async_copy(
            held.at[slot, pl.ds(0, sizes[part])],
            outs[part].at[pl.ds(block * sizes[part], sizes[part])],
            out_sem.at[slot],
        )

    ahead = slots // 2
    for step in range(ahead):
        for copy in fetch(step):
            copy.start()
    for step in range(len(steps)):
        later = step + ahead
        if later < len(steps):
            if later >= slots:
                put(later - slots).wait()
            for copy in fetch(later):
                copy.start()
        for copy in fetch(step):
            copy.wait()
        put(step).start()
    for step in range(len(steps) - slots, len(steps)):
        put(step).wait()


def assemble(lanes, pieces, sizes, width):
    parts = len(pieces) // 2
    whole = pl.BlockSpec(memory_space=pl.ANY)
    return pl.pallas_call(
        functools.partial(assemble_kernel, sizes=sizes, parts=parts),
        out_shape=[jax.ShapeDtypeStruct((4 * size, width), jnp.bfloat16) for size in sizes],
        grid_spec=pltpu.PrefetchScalarGridSpec(
            num_scalar_prefetch=1,
            grid=(1,),
            in_specs=[whole] * len(pieces),
            out_specs=[whole] * len(sizes),
            scratch_shapes=[
                pltpu.VMEM((4, max(sizes), width), jnp.bfloat16),
                pltpu.SemaphoreType.DMA((4, parts)),
                pltpu.SemaphoreType.DMA((4,)),
            ],
        ),
        cost_estimate=pl.CostEstimate(
            flops=0, bytes_accessed=16 * sum(sizes) * width, transcendentals=0
        ),
        name="assemble",
    )(lanes, *pieces)


def dot_in(left, right, left_dim, right_dim):
    return lax.dot_general(
        left, right, (((left_dim,), (right_dim,)), ((), ())), preferred_element_type=jnp.float32
    )


def ffn_main_kernel(x_ref, c_ref, gate_ref, up_ref, down_ref, h_ref, dg_ref, du_ref, *, step):
    for first in range(0, x_ref.shape[0], step):
        rows = slice(first, first + step)
        gate = dot_in(x_ref[rows], gate_ref[...], 1, 1)
        up = dot_in(x_ref[rows], up_ref[...], 1, 1)
        grad_hidden = dot_in(c_ref[rows], down_ref[...], 1, 1)
        sig = jax.nn.sigmoid(gate)
        silu = gate * sig
        h_ref[rows] = (silu * up).astype(jnp.bfloat16)
        dg = (grad_hidden * up * sig * (1.0 + gate * (1.0 - sig))).astype(jnp.bfloat16)
        du = (grad_hidden * silu).astype(jnp.bfloat16)
        dg_ref[rows] = dg
        du_ref[rows] = du


def ffn_grad_kernel(x_ref, c_ref, h_ref, dg_ref, du_ref, g_ref):
    for place, (left, right) in enumerate(((dg_ref, x_ref), (du_ref, x_ref), (h_ref, c_ref))):
        grad = dot_in(left[...], right[...], 0, 0).astype(jnp.bfloat16)
        for i in range(g_ref.shape[0]):
            g_ref[i, place] = grad[:, i * g_ref.shape[3] : (i + 1) * g_ref.shape[3]]


def ffn_main(x, c, gate, up, down, tile=256, step=256):
    tokens, width = x.shape
    units = gate.shape[0]
    full = pl.BlockSpec((tokens, width), lambda t: (0, 0))
    weight = pl.BlockSpec((tile, width), lambda t: (t, 0))
    column = pl.BlockSpec((tokens, tile), lambda t: (0, t))
    return pl.pallas_call(
        functools.partial(ffn_main_kernel, step=step),
        out_shape=[jax.ShapeDtypeStruct((tokens, units), jnp.bfloat16)] * 3,
        grid=(units // tile,),
        in_specs=[full, full, weight, weight, weight],
        out_specs=[column, column, column],
        cost_estimate=pl.CostEstimate(
            flops=6 * tokens * width * units, bytes_accessed=6 * units * (width + tokens),
            transcendentals=tokens * units,
        ),
        name="ffn_main",
    )(x, c, gate, up, down)


def ffn_grad(x, c, hidden, dg, du, chunks, tile=256):
    tokens, width = x.shape
    units = hidden.shape[1]
    full = pl.BlockSpec((tokens, width), lambda t: (0, 0))
    column = pl.BlockSpec((tokens, tile), lambda t: (0, t))
    piece = width // chunks
    return pl.pallas_call(
        ffn_grad_kernel,
        out_shape=jax.ShapeDtypeStruct((chunks, 3, units, piece), jnp.bfloat16),
        grid=(units // tile,),
        in_specs=[full, full, column, column, column],
        out_specs=pl.BlockSpec((chunks, 3, tile, piece), lambda t: (0, 0, t, 0)),
        cost_estimate=pl.CostEstimate(
            flops=6 * tokens * width * units, bytes_accessed=6 * units * (width + tokens),
            transcendentals=0,
        ),
        name="ffn_grad",
    )(x, c, hidden, dg, du)


eps_norm = 1e-05


def dot_dims(left, right, left_dim, right_dim):
    return lax.dot_general(
        left, right, (((left_dim,), (right_dim,)), ((), ())), preferred_element_type=jnp.float32
    )


def row_starts(seg_row):
    ones = [jnp.sum((seg_row < s).astype(jnp.int32)) for s in (1, 2, 3)]
    start = jnp.zeros_like(seg_row)
    before = 0
    for s, count in zip((1, 2, 3), ones):
        start = start + jnp.where(seg_row >= s, count - before, 0)
        before = count
    return start


def rope_tables(start):
    half_dim = HD // 2
    offsets = (jnp.arange(start.shape[0], dtype=jnp.int32) - start).astype(jnp.float32)
    frequency = jnp.exp(jnp.arange(half_dim, dtype=jnp.float32) * (-math.log(10000.0) / half_dim))
    angles = frequency[:, None] * offsets[None, :]
    return jnp.cos(angles), jnp.sin(angles)


def rotate(rows, cos_table, sin_table):
    count, length = rows.shape
    parts = rows.reshape(count // HD, 2, HD // 2, length)
    low, high = parts[:, 0], parts[:, 1]
    turned = jnp.stack(
        [low * cos_table - high * sin_table, high * cos_table + low * sin_table], axis=1
    )
    return turned.reshape(count, length)


def rms_factor(values):
    return lax.rsqrt(jnp.mean(values * values, axis=-1, keepdims=True) + eps_norm)


def rms_back(values_in, factor, gain, grad_normed):
    scaled = grad_normed * gain
    gain_part = jnp.sum(grad_normed * values_in * factor, axis=0)
    inner = jnp.mean(scaled * values_in, axis=-1, keepdims=True)
    return factor * scaled - values_in * (factor * factor * factor) * inner, gain_part


def scatter(partial_sum, axis, dim):
    return lax.psum_scatter(partial_sum, axis, scatter_dimension=dim, tiled=True)


def line_steps(count):
    near_right = [(i, i + 1) for i in range(count - 1)]
    near_left = [(i, i - 1) for i in range(1, count)]
    return near_right, near_left


def line_gather(piece, axis):
    count, me = lax.axis_size(axis), lax.axis_index(axis)
    assert count == 4
    near_right, near_left = line_steps(count)
    one_left = lax.ppermute(piece, axis, near_right)
    one_right = lax.ppermute(piece, axis, near_left)
    two_left = lax.ppermute(one_left, axis, [(1, 2), (2, 3)])
    two_right = lax.ppermute(one_right, axis, [(1, 0), (2, 1)])
    three_left = lax.ppermute(one_left, axis, [(1, 3)])
    three_right = lax.ppermute(one_right, axis, [(2, 0)])
    slots = jnp.concatenate(
        [three_left, two_left, one_left, piece, one_right, two_right, three_right], axis=0
    )
    rows = piece.shape[0]
    return lax.dynamic_slice_in_dim(slots, (count - 1 - me) * rows, count * rows, axis=0)


def line_scatter(blocks, axis):
    count = lax.axis_size(axis)
    assert count == 4
    near_right, near_left = line_steps(count)
    own, next_one, opposite, last = blocks
    two_right = lax.ppermute(opposite, axis, [(0, 1), (1, 2)])
    two_left = lax.ppermute(opposite, axis, [(3, 2), (2, 1)])
    three_right = lax.ppermute(last, axis, [(0, 2)])
    three_left = lax.ppermute(next_one, axis, [(3, 1)])

    own, next_one, last = lax.optimization_barrier((own, next_one, last))

    def total(*parts):
        return sum(part.astype(jnp.float32) for part in parts)

    right = lax.ppermute(
        total(next_one, two_right, three_right).astype(jnp.bfloat16), axis, near_right
    )
    left = lax.ppermute(
        total(last, two_left, three_left).astype(jnp.bfloat16), axis, near_left
    )
    return total(own, right, left)


def turned_blocks(whole, axis, dim):
    count, me = lax.axis_size(axis), lax.axis_index(axis)
    size = whole.shape[dim] // count
    return [
        lax.dynamic_slice_in_dim(whole, (me + place) % count * size, size, axis=dim)
        for place in range(count)
    ]


def plane_gather(piece, axis, sizes):
    core, across, along = ([(i, i ^ bit) for i in range(8)] for bit in (1, 2, 4))
    half = piece.shape[0] // 2
    top, low = piece[:half], piece[half:]

    def partner(part):
        return lax.ppermute(part, axis, core)

    top_x, low_y = lax.ppermute(top, axis, across), lax.ppermute(low, axis, along)
    top_y, low_x = lax.ppermute(top, axis, along), lax.ppermute(low, axis, across)
    top_xy, low_xy = lax.ppermute(top_x, axis, along), lax.ppermute(low_y, axis, across)
    held = [(top, low), (top_x, low_x), (top_y, low_y), (top_xy, low_xy)]
    parts = []
    for pair in held:
        parts += [pair, tuple(partner(part) for part in pair)]

    flat = [part for pair in parts for part in pair]
    lanes = jnp.arange(8, dtype=jnp.int32) ^ lax.axis_index(axis).astype(jnp.int32)
    return assemble(lanes * piece.shape[1], flat, sizes, 8 * piece.shape[1])


def local(
    inputs, segments, w_query, w_key, w_value, w_output, w_gate, w_up, w_down,
    gain_attn, gain_ffn, cotangent,
):
    low = jnp.bfloat16
    n_dp, n_mp = lax.axis_size("dp"), lax.axis_size("mp")
    batches, tokens, width = inputs.shape
    cols = w_query.shape[1]
    depth = w_query.shape[0]
    hidden_part = w_gate.shape[1]

    def split16(gain):
        high = gain.astype(low)
        return high, (gain - high.astype(jnp.float32)).astype(low)

    pieces = split16(gain_attn) + split16(gain_ffn)
    gain_row = jnp.concatenate(pieces + (jnp.zeros((3 * cols - 4 * depth,), low),))
    qkv_piece = jnp.concatenate(
        [
            jnp.concatenate([w_query, w_key, w_value], axis=1),
            jnp.pad(gain_row[None], ((0, 15), (0, 0))),
        ],
        axis=0,
    )
    qkv_all = lax.all_gather(qkv_piece, "dp", axis=0, tiled=False)
    w_qkv = qkv_all[:, :depth].reshape(width, 3 * cols)
    gains = qkv_all[:, depth, : 4 * depth].astype(jnp.float32).reshape(n_dp, 4, depth)
    gain_one = (gains[:, 0] + gains[:, 1]).reshape(width)
    gain_two = (gains[:, 2] + gains[:, 3]).reshape(width)

    rest_piece = jnp.concatenate([w_output, w_gate.T, w_up.T, w_down], axis=0)
    sizes = (cols, hidden_part, hidden_part, hidden_part)
    firsts = (0, cols, cols + hidden_part, cols + 2 * hidden_part)
    if n_dp == 8 and depth == 128:
        output_full, gate_full, up_full, down_full = plane_gather(line_gather(rest_piece, "mp"), "dp", sizes)
    else:
        rest_every = lax.all_gather(rest_piece, ("dp", "mp"), axis=0, tiled=False)
        rest_every = rest_every.reshape((n_dp, n_mp) + rest_piece.shape).transpose(1, 2, 0, 3)
        rest_every = rest_every.reshape(n_mp, rest_piece.shape[0], width)
        output_full, gate_full, up_full, down_full = (
            rest_every[:, first : first + size].reshape(n_mp * size, width)
            for first, size in zip(firsts, sizes)
        )

    first_rows = line_gather(inputs[0], "mp")
    first_rows, second_piece = lax.optimization_barrier((first_rows, inputs[1]))
    rows_all = [first_rows, None]

    normed, factors, qkv, tables, starts, lows, mixed, logs = [], [], [], [], [], [], [], []
    for m in range(batches):
        start = row_starts(segments[m, 0])
        cos_table, sin_table = rope_tables(start)
        tables.append((cos_table, sin_table))
        starts.append(start[None])
        lows.append((start[::BQ] // BK_FORWARD, start[::BQ] // BK))
        if m == 1:
            rows_all[1] = line_gather(second_piece, "mp")
        rows = rows_all[m].astype(jnp.float32)
        factors.append(rms_factor(rows))
        normed.append((rows * factors[m] * gain_one).astype(low))
        pre = dot_dims(w_qkv, normed[m], 0, 1)
        turned_q = rotate(pre[:cols], cos_table, sin_table) * HD ** -0.5
        turned_k = rotate(pre[cols : 2 * cols], cos_table, sin_table)
        qkv.append(jnp.concatenate([turned_q, turned_k, pre[2 * cols :]], axis=0).astype(low))
        out, log = attn_fwd(qkv[m], starts[m], lows[m][0])
        mixed.append(out)
        logs.append(log)
    mixed_own = []
    for m in range(batches):
        mixed_own.append(
            lax.all_to_all(mixed[m], "mp", split_axis=1, concat_axis=0, tiled=True)
        )
    in_float = inputs.astype(jnp.float32).reshape(batches * tokens, width)
    mixed_both = jnp.concatenate(mixed_own, axis=1)
    hidden_in = in_float + dot_dims(mixed_both, output_full, 0, 0)
    factor_ffn = rms_factor(hidden_in)
    normed_ffn = (hidden_in * factor_ffn * gain_two).astype(low)
    grad_top = cotangent.reshape(batches * tokens, width)
    hidden, grad_gate_pre, grad_up_pre = ffn_main(
        normed_ffn, grad_top, gate_full, up_full, down_full
    )
    grad_normed_ffn = dot_dims(grad_gate_pre, gate_full, 1, 0) + dot_dims(
        grad_up_pre, up_full, 1, 0
    )
    result = (hidden_in + dot_dims(hidden, down_full, 1, 0)).astype(low)
    chunks = width // 128
    every_grad = ffn_grad(normed_ffn, grad_top, hidden, grad_gate_pre, grad_up_pre, chunks)
    if n_dp != chunks:
        every_grad = every_grad.reshape(chunks, 3, n_mp * hidden_part, n_dp // chunks, depth)
        every_grad = every_grad.transpose(0, 3, 1, 2, 4).reshape(n_dp, 3, -1, depth)
    grad_middle, gain_ffn_part = rms_back(hidden_in, factor_ffn, gain_two, grad_normed_ffn)
    grad_hidden_in = grad_top.astype(jnp.float32) + grad_middle
    grad_branch = grad_hidden_in.astype(low)
    grad_mixed = dot_dims(output_full, grad_branch, 1, 1).astype(low)
    grad_mixed_rows = []
    for m in range(batches):
        grad_mixed_rows.append(
            lax.all_to_all(
                grad_mixed[:, m * tokens : (m + 1) * tokens], "mp", split_axis=0,
                concat_axis=1, tiled=True,
            )
        )
    grad_output = dot_dims(grad_branch, mixed_both, 0, 1).astype(low)

    grad_mixed_rows[0], every_grad = lax.optimization_barrier((grad_mixed_rows[0], every_grad))
    mine = scatter(every_grad, "dp", 0)


    grad_qkv, grad_normed = [], []
    gain_attn_part = jnp.zeros((width,), jnp.float32)
    for m in range(batches):
        cos_table, sin_table = tables[m]
        back = attn_bwd(
            qkv[m], grad_mixed_rows[m], mixed[m], logs[m], starts[m], lows[m][1], cos_table,
            sin_table,
        ).reshape(3 * cols, n_mp * tokens)
        grad_qkv.append(back)
        spread = [
            dot_dims(part, w_qkv, 0, 1).astype(low) for part in turned_blocks(back, "mp", 1)
        ]
        grad_normed.append(line_scatter(spread, "mp"))
        scaled_rows = rows_all[m].astype(jnp.float32) * factors[m]
        for part, rows in zip(spread, turned_blocks(scaled_rows, "mp", 0)):
            gain_attn_part = gain_attn_part + jnp.sum(part.astype(jnp.float32) * rows, axis=0)
    grad_w = 0.0
    for m in range(batches):
        grad_w = grad_w + dot_dims(normed[m], grad_qkv[m], 0, 1)

    gain_parts = jnp.stack([gain_attn_part, gain_ffn_part]).astype(low)
    gain_parts = gain_parts.reshape(2, n_dp, depth).transpose(1, 0, 2).reshape(n_dp, 1, 2 * depth)
    sums = jnp.concatenate(
        [
            grad_w.astype(low).reshape(n_dp, depth, 3 * cols),
            grad_output.reshape(n_dp, depth, n_mp * cols),
        ],
        axis=2,
    )
    gain_rows = jnp.pad(gain_parts, ((0, 0), (0, 15), (0, sums.shape[2] - 2 * depth)))
    sums = jnp.concatenate([sums, gain_rows], axis=1)
    sums = lax.all_to_all(sums, "dp", split_axis=0, concat_axis=0, tiled=True)
    sums = jnp.sum(sums.astype(jnp.float32), axis=0)
    own_qkv, own_out = sums[:depth, : 3 * cols], sums[:depth, 3 * cols :]
    own_gain = sums[depth, : 2 * depth].reshape(2, n_mp, depth // n_mp).transpose(1, 0, 2)
    own_gain = own_gain.reshape(n_mp, 1, 2 * depth // n_mp)
    own_gain = jnp.pad(own_gain.astype(low), ((0, 0), (0, 15), (0, depth - own_gain.shape[2])))
    own_ffn = mine.reshape(3, n_mp, hidden_part, depth).transpose(1, 0, 2, 3)
    own_rest = jnp.concatenate(
        [
            own_out.T.astype(low).reshape(n_mp, cols, depth),
            own_ffn.reshape(n_mp, -1, depth),
            own_gain,
        ],
        axis=1,
    )
    own_rest = own_rest.reshape(-1, depth)
    own_rest = turned_blocks(own_rest, "mp", 0)
    own_rest = line_scatter(own_rest, "mp")
    own_output, own_gate, own_up, own_down = (
        own_rest[first : first + size] for first, size in zip(firsts, sizes)
    )
    grad_norms = own_rest[sum(sizes), : 2 * depth // n_mp].reshape(2, -1)

    grad_normed_attn = jnp.concatenate(grad_normed, axis=0)
    grad_lower, _ = rms_back(in_float, rms_factor(in_float), gain_one, grad_normed_attn)
    grad_inputs = (grad_hidden_in + grad_lower).astype(low)
    return (
        result.reshape(inputs.shape),
        grad_inputs.reshape(inputs.shape),
        own_qkv[:, :cols],
        own_qkv[:, cols : 2 * cols],
        own_qkv[:, 2 * cols :],
        own_output,
        own_gate.T,
        own_up.T,
        own_down,
        grad_norms[0],
        grad_norms[1],
    )


def solution(mesh):
    row_spec = P(None, ("dp", "mp"), None)
    first, second = P("dp", "mp"), P("mp", "dp")
    both = P(("dp", "mp"))

    return jax.shard_map(
        local,
        mesh=mesh,
        in_specs=(
            row_spec, P(None, "dp", None), first, first, first, second, first, first, second,
            P("dp"), P("dp"), row_spec,
        ),
        out_specs=(
            row_spec, row_spec, first, first, first, second, first, first, second, both, both,
        ),
        check_vma=False,
    )
```

```python
import functools
import math

import jax
import jax.numpy as jnp
from jax import lax
from jax.experimental import pallas as pl
from jax.experimental.pallas import tpu as pltpu
from jax.sharding import PartitionSpec as P


HD = 64
BQ = 512
BK = 256
BK_FORWARD = 256
HPS = 4


def attn_fwd_kernel(lo_ref, q_ref, k_ref, v_ref, start_ref, o_ref, lse_ref, k_scr, *, bq, bk, heads):
    length = q_ref.shape[1]
    k_scr[...] = k_ref[...].T

    def q_step(qi, carry):
        q0 = pl.multiple_of(qi * bq, bq)
        qcols = pl.ds(q0, bq)
        q_blk = q_ref[:, qcols]
        start = start_ref[:, qcols]
        q_idx = q0 + lax.broadcasted_iota(jnp.int32, (1, bq), 1)

        def visit(kb, state, first):
            k0 = pl.multiple_of(kb * bk, bk)
            wide = bq - first
            k_idx = k0 + lax.broadcasted_iota(jnp.int32, (bk, wide), 0)
            allowed = (k_idx >= start[:, first:]) & (k_idx <= q_idx[:, first:])
            out = []
            for h in range(heads):
                peak, total, acc = (part[:, first:] for part in state[h])
                s = jnp.dot(k_scr[pl.ds(k0, bk), h * HD:(h + 1) * HD], q_blk[h * HD:(h + 1) * HD, first:], preferred_element_type=jnp.float32)
                s = jnp.where(allowed, s, -1e30)
                new_peak = jnp.maximum(peak, jnp.max(s, axis=0, keepdims=True))
                p = jnp.exp(s - new_peak)
                fade = jnp.exp(peak - new_peak)
                total = total * fade + jnp.sum(p, axis=0, keepdims=True)
                acc = acc * fade + jnp.dot(v_ref[h * HD:(h + 1) * HD, pl.ds(k0, bk)], p.astype(jnp.bfloat16), preferred_element_type=jnp.float32)
                fresh = (new_peak, total, acc)
                if first:
                    fresh = tuple(jnp.concatenate([old[:, :first], new], axis=1) for old, new in zip(state[h], fresh))
                out.append(fresh)
            return tuple(out)

        init = tuple((jnp.full((1, bq), -1e30, jnp.float32), jnp.zeros((1, bq), jnp.float32), jnp.zeros((HD, bq), jnp.float32)) for _ in range(heads))
        hi = (q0 + bq - 1) // bk
        state = lax.fori_loop(lo_ref[qi], hi, lambda kb, state: visit(kb, state, 0), init)
        state = visit(hi, state, bq - bk)
        for h in range(heads):
            peak, total, acc = state[h]
            o_ref[h * HD:(h + 1) * HD, qcols] = (acc / total).astype(jnp.bfloat16)
            lse_ref[h, :, qcols] = peak + jnp.log(total)
        return carry

    lax.fori_loop(0, length // bq, q_step, 0)


def attn_bwd_kernel(lo_ref, q_ref, k_ref, v_ref, do_ref, o_ref, lse_ref, start_ref, cos_ref, sin_ref, out_ref, k_scr, v_scr, dk_scr, dv_scr, *, bq, bk, heads):
    length = q_ref.shape[1]
    k_scr[...] = k_ref[...].T
    v_scr[...] = v_ref[...].T
    dk_scr[...] = jnp.zeros_like(dk_scr)
    dv_scr[...] = jnp.zeros_like(dv_scr)
    half = HD // 2

    def unrotate(g, cos, sin):
        a, b = g[:half], g[half:]
        return jnp.concatenate([a * cos + b * sin, b * cos - a * sin], axis=0).astype(jnp.bfloat16)

    def q_step(qi, carry):
        q0 = pl.multiple_of(qi * bq, bq)
        qcols = pl.ds(q0, bq)
        q_blk = q_ref[:, qcols]
        do_blk = do_ref[:, qcols]
        q_t = q_blk.T
        do_t = do_blk.T
        prod = do_blk.astype(jnp.float32) * o_ref[:, qcols].astype(jnp.float32)
        start = start_ref[:, qcols]
        q_idx = q0 + lax.broadcasted_iota(jnp.int32, (1, bq), 1)
        deltas = [jnp.sum(prod[h * HD:(h + 1) * HD], axis=0, keepdims=True) for h in range(heads)]
        lses = [lse_ref[h, :, qcols] for h in range(heads)]

        def visit(kb, state, first):
            k0 = pl.multiple_of(kb * bk, bk)
            rows = pl.ds(k0, bk)
            k_idx = k0 + lax.broadcasted_iota(jnp.int32, (bk, bq - first), 0)
            allowed = (k_idx >= start[:, first:]) & (k_idx <= q_idx[:, first:])
            out = []
            for h in range(heads):
                hs = slice(h * HD, (h + 1) * HD)
                s = jnp.dot(k_scr[rows, hs], q_blk[hs, first:], preferred_element_type=jnp.float32)
                p = jnp.exp(jnp.where(allowed, s - lses[h][:, first:], -1e30))
                dp = jnp.dot(v_scr[rows, hs], do_blk[hs, first:], preferred_element_type=jnp.float32)
                ds = (p * (dp - deltas[h][:, first:])).astype(jnp.bfloat16)
                dv_scr[h, rows, :] += jnp.dot(p.astype(jnp.bfloat16), do_t[first:, hs], preferred_element_type=jnp.float32)
                dk_scr[h, rows, :] += jnp.dot(ds, q_t[first:, hs], preferred_element_type=jnp.float32)
                part = jnp.dot(k_ref[hs, rows], ds, preferred_element_type=jnp.float32)
                if first:
                    part = jnp.concatenate([state[h][:, :first], state[h][:, first:] + part], axis=1)
                else:
                    part = state[h] + part
                out.append(part)
            return tuple(out)

        init = tuple(jnp.zeros((HD, bq), jnp.float32) for _ in range(heads))
        hi = (q0 + bq - 1) // bk
        state = lax.fori_loop(lo_ref[qi], hi, lambda kb, state: visit(kb, state, 0), init)
        state = visit(hi, state, bq - bk)
        cos, sin = cos_ref[:, qcols], sin_ref[:, qcols]
        for h in range(heads):
            out_ref[0, h * HD:(h + 1) * HD, qcols] = unrotate(state[h] * HD ** -0.5, cos, sin)
        return carry

    lax.fori_loop(0, length // bq, q_step, 0)
    for h in range(heads):
        out_ref[1, h * HD:(h + 1) * HD, :] = unrotate(dk_scr[h].T, cos_ref[...], sin_ref[...])
        out_ref[2, h * HD:(h + 1) * HD, :] = dv_scr[h].T.astype(jnp.bfloat16)


def attn_fwd(qkv_t, start, lo, bq=BQ, bk=BK_FORWARD, hps=HPS):
    cols3, length = qkv_t.shape
    cols = cols3 // 3
    steps = cols // (HD * hps)
    blk = (HD * hps, length)
    area = cols * length * length // 4
    return pl.pallas_call(
        functools.partial(attn_fwd_kernel, bq=bq, bk=bk, heads=hps),
        out_shape=(jax.ShapeDtypeStruct((cols, length), jnp.bfloat16), jax.ShapeDtypeStruct((cols // HD, 1, length), jnp.float32)),
        grid_spec=pltpu.PrefetchScalarGridSpec(
            num_scalar_prefetch=1, grid=(steps,),
            in_specs=[pl.BlockSpec(blk, lambda i, lo: (i, 0)), pl.BlockSpec(blk, lambda i, lo: (i + steps, 0)), pl.BlockSpec(blk, lambda i, lo: (i + 2 * steps, 0)),
                      pl.BlockSpec((1, length), lambda i, lo: (0, 0))],
            out_specs=[pl.BlockSpec(blk, lambda i, lo: (i, 0)), pl.BlockSpec((hps, 1, length), lambda i, lo: (i, 0, 0))],
            scratch_shapes=[pltpu.VMEM((length, HD * hps), jnp.bfloat16)]),
        cost_estimate=pl.CostEstimate(flops=16 * area, bytes_accessed=cols * length * 8, transcendentals=area // HD),
        name="attn_fwd",
    )(lo, qkv_t, qkv_t, qkv_t, start)


def attn_bwd(qkv_t, do_t, o_t, lse, start, lo, cos, sin, bq=BQ, bk=BK, hps=HPS):
    cols3, length = qkv_t.shape
    cols = cols3 // 3
    steps = cols // (HD * hps)
    blk = (HD * hps, length)
    area = cols * length * length // 4
    return pl.pallas_call(
        functools.partial(attn_bwd_kernel, bq=bq, bk=bk, heads=hps),
        out_shape=jax.ShapeDtypeStruct((3, cols, length), jnp.bfloat16),
        grid_spec=pltpu.PrefetchScalarGridSpec(
            num_scalar_prefetch=1, grid=(steps,),
            in_specs=[pl.BlockSpec(blk, lambda i, lo: (i, 0)), pl.BlockSpec(blk, lambda i, lo: (i + steps, 0)), pl.BlockSpec(blk, lambda i, lo: (i + 2 * steps, 0)),
                      pl.BlockSpec(blk, lambda i, lo: (i, 0)), pl.BlockSpec(blk, lambda i, lo: (i, 0)),
                      pl.BlockSpec((hps, 1, length), lambda i, lo: (i, 0, 0)),
                      pl.BlockSpec((1, length), lambda i, lo: (0, 0)),
                      pl.BlockSpec((HD // 2, length), lambda i, lo: (0, 0)), pl.BlockSpec((HD // 2, length), lambda i, lo: (0, 0))],
            out_specs=pl.BlockSpec((3,) + blk, lambda i, lo: (0, i, 0)),
            scratch_shapes=[pltpu.VMEM((length, HD * hps), jnp.bfloat16)] * 2 + [pltpu.VMEM((hps, length, HD), jnp.float32)] * 2),
        cost_estimate=pl.CostEstimate(flops=40 * area, bytes_accessed=cols * length * 20, transcendentals=area // HD),
        name="attn_bwd",
    )(lo, qkv_t, qkv_t, qkv_t, do_t, o_t, lse, start, cos, sin)


def assemble_kernel(lane_ref, *refs, sizes, parts):
    pieces, outs = refs[: 2 * parts], refs[2 * parts : 2 * parts + len(sizes)]
    held, in_sem, out_sem = refs[2 * parts + len(sizes) :]
    slots = held.shape[0]
    total = sum(sizes)
    steps = [
        (block, part, sum(sizes[:part])) for block in range(4) for part in range(len(sizes))
    ]

    def fetch(step):
        block, part, first = steps[step]
        rows = pl.ds((block % 2) * total + first, sizes[part])
        slot = step % slots
        return [
            pltpu.make_async_copy(
                pieces[2 * r + block // 2].at[rows],
                held.at[slot, pl.ds(0, sizes[part]), pl.ds(pl.multiple_of(lane_ref[r], 128), 128)],
                in_sem.at[slot, r],
            )
            for r in range(parts)
        ]

    def put(step):
        block, part, _ = steps[step]
        slot = step % slots
        return pltpu.make_async_copy(
            held.at[slot, pl.ds(0, sizes[part])],
            outs[part].at[pl.ds(block * sizes[part], sizes[part])],
            out_sem.at[slot],
        )

    ahead = slots // 2
    for step in range(ahead):
        for copy in fetch(step):
            copy.start()
    for step in range(len(steps)):
        later = step + ahead
        if later < len(steps):
            if later >= slots:
                put(later - slots).wait()
            for copy in fetch(later):
                copy.start()
        for copy in fetch(step):
            copy.wait()
        put(step).start()
    for step in range(len(steps) - slots, len(steps)):
        put(step).wait()


def assemble(lanes, pieces, sizes, width):
    parts = len(pieces) // 2
    whole = pl.BlockSpec(memory_space=pl.ANY)
    return pl.pallas_call(
        functools.partial(assemble_kernel, sizes=sizes, parts=parts),
        out_shape=[jax.ShapeDtypeStruct((4 * size, width), jnp.bfloat16) for size in sizes],
        grid_spec=pltpu.PrefetchScalarGridSpec(
            num_scalar_prefetch=1,
            grid=(1,),
            in_specs=[whole] * len(pieces),
            out_specs=[whole] * len(sizes),
            scratch_shapes=[
                pltpu.VMEM((4, max(sizes), width), jnp.bfloat16),
                pltpu.SemaphoreType.DMA((4, parts)),
                pltpu.SemaphoreType.DMA((4,)),
            ],
        ),
        cost_estimate=pl.CostEstimate(
            flops=0, bytes_accessed=16 * sum(sizes) * width, transcendentals=0
        ),
        name="assemble",
    )(lanes, *pieces)


def dot_in(left, right, left_dim, right_dim):
    return lax.dot_general(
        left, right, (((left_dim,), (right_dim,)), ((), ())), preferred_element_type=jnp.float32
    )


def ffn_main_kernel(x_ref, c_ref, gate_ref, up_ref, down_ref, h_ref, dg_ref, du_ref, *, step):
    for first in range(0, x_ref.shape[0], step):
        rows = slice(first, first + step)
        gate = dot_in(x_ref[rows], gate_ref[...], 1, 1)
        up = dot_in(x_ref[rows], up_ref[...], 1, 1)
        grad_hidden = dot_in(c_ref[rows], down_ref[...], 1, 1)
        sig = jax.nn.sigmoid(gate)
        silu = gate * sig
        h_ref[rows] = (silu * up).astype(jnp.bfloat16)
        dg = (grad_hidden * up * sig * (1.0 + gate * (1.0 - sig))).astype(jnp.bfloat16)
        du = (grad_hidden * silu).astype(jnp.bfloat16)
        dg_ref[rows] = dg
        du_ref[rows] = du


def ffn_grad_kernel(x_ref, c_ref, h_ref, dg_ref, du_ref, g_ref):
    for place, (left, right) in enumerate(((dg_ref, x_ref), (du_ref, x_ref), (h_ref, c_ref))):
        grad = dot_in(left[...], right[...], 0, 0).astype(jnp.bfloat16)
        for i in range(g_ref.shape[0]):
            g_ref[i, place] = grad[:, i * g_ref.shape[3] : (i + 1) * g_ref.shape[3]]


def ffn_main(x, c, gate, up, down, tile=256, step=256):
    tokens, width = x.shape
    units = gate.shape[0]
    full = pl.BlockSpec((tokens, width), lambda t: (0, 0))
    weight = pl.BlockSpec((tile, width), lambda t: (t, 0))
    column = pl.BlockSpec((tokens, tile), lambda t: (0, t))
    return pl.pallas_call(
        functools.partial(ffn_main_kernel, step=step),
        out_shape=[jax.ShapeDtypeStruct((tokens, units), jnp.bfloat16)] * 3,
        grid=(units // tile,),
        in_specs=[full, full, weight, weight, weight],
        out_specs=[column, column, column],
        cost_estimate=pl.CostEstimate(
            flops=6 * tokens * width * units, bytes_accessed=6 * units * (width + tokens),
            transcendentals=tokens * units,
        ),
        name="ffn_main",
    )(x, c, gate, up, down)


def ffn_grad(x, c, hidden, dg, du, chunks, tile=256):
    tokens, width = x.shape
    units = hidden.shape[1]
    full = pl.BlockSpec((tokens, width), lambda t: (0, 0))
    column = pl.BlockSpec((tokens, tile), lambda t: (0, t))
    piece = width // chunks
    return pl.pallas_call(
        ffn_grad_kernel,
        out_shape=jax.ShapeDtypeStruct((chunks, 3, units, piece), jnp.bfloat16),
        grid=(units // tile,),
        in_specs=[full, full, column, column, column],
        out_specs=pl.BlockSpec((chunks, 3, tile, piece), lambda t: (0, 0, t, 0)),
        cost_estimate=pl.CostEstimate(
            flops=6 * tokens * width * units, bytes_accessed=6 * units * (width + tokens),
            transcendentals=0,
        ),
        name="ffn_grad",
    )(x, c, hidden, dg, du)


eps_norm = 1e-05


def dot_dims(left, right, left_dim, right_dim):
    return lax.dot_general(
        left, right, (((left_dim,), (right_dim,)), ((), ())), preferred_element_type=jnp.float32
    )


def row_starts(seg_row):
    ones = [jnp.sum((seg_row < s).astype(jnp.int32)) for s in (1, 2, 3)]
    start = jnp.zeros_like(seg_row)
    before = 0
    for s, count in zip((1, 2, 3), ones):
        start = start + jnp.where(seg_row >= s, count - before, 0)
        before = count
    return start


def rope_tables(start):
    half_dim = HD // 2
    offsets = (jnp.arange(start.shape[0], dtype=jnp.int32) - start).astype(jnp.float32)
    frequency = jnp.exp(jnp.arange(half_dim, dtype=jnp.float32) * (-math.log(10000.0) / half_dim))
    angles = frequency[:, None] * offsets[None, :]
    return jnp.cos(angles), jnp.sin(angles)


def rotate(rows, cos_table, sin_table):
    count, length = rows.shape
    parts = rows.reshape(count // HD, 2, HD // 2, length)
    low, high = parts[:, 0], parts[:, 1]
    turned = jnp.stack(
        [low * cos_table - high * sin_table, high * cos_table + low * sin_table], axis=1
    )
    return turned.reshape(count, length)


def rms_factor(values):
    return lax.rsqrt(jnp.mean(values * values, axis=-1, keepdims=True) + eps_norm)


def rms_back(values_in, factor, gain, grad_normed):
    scaled = grad_normed * gain
    gain_part = jnp.sum(grad_normed * values_in * factor, axis=0)
    inner = jnp.mean(scaled * values_in, axis=-1, keepdims=True)
    return factor * scaled - values_in * (factor * factor * factor) * inner, gain_part


def scatter(partial_sum, axis, dim):
    return lax.psum_scatter(partial_sum, axis, scatter_dimension=dim, tiled=True)


def line_steps(count):
    near_right = [(i, i + 1) for i in range(count - 1)]
    near_left = [(i, i - 1) for i in range(1, count)]
    return near_right, near_left


def line_gather(piece, axis):
    count, me = lax.axis_size(axis), lax.axis_index(axis)
    assert count == 4
    near_right, near_left = line_steps(count)
    one_left = lax.ppermute(piece, axis, near_right)
    one_right = lax.ppermute(piece, axis, near_left)
    two_left = lax.ppermute(one_left, axis, [(1, 2), (2, 3)])
    two_right = lax.ppermute(one_right, axis, [(1, 0), (2, 1)])
    three_left = lax.ppermute(one_left, axis, [(1, 3)])
    three_right = lax.ppermute(one_right, axis, [(2, 0)])
    slots = jnp.concatenate(
        [three_left, two_left, one_left, piece, one_right, two_right, three_right], axis=0
    )
    rows = piece.shape[0]
    return lax.dynamic_slice_in_dim(slots, (count - 1 - me) * rows, count * rows, axis=0)


def line_scatter(blocks, axis):
    count = lax.axis_size(axis)
    assert count == 4
    near_right, near_left = line_steps(count)
    own, next_one, opposite, last = blocks
    two_right = lax.ppermute(opposite, axis, [(0, 1), (1, 2)])
    two_left = lax.ppermute(opposite, axis, [(3, 2), (2, 1)])
    three_right = lax.ppermute(last, axis, [(0, 2)])
    three_left = lax.ppermute(next_one, axis, [(3, 1)])

    own, next_one, last = lax.optimization_barrier((own, next_one, last))

    def total(*parts):
        return sum(part.astype(jnp.float32) for part in parts)

    right = lax.ppermute(
        total(next_one, two_right, three_right).astype(jnp.bfloat16), axis, near_right
    )
    left = lax.ppermute(
        total(last, two_left, three_left).astype(jnp.bfloat16), axis, near_left
    )
    return total(own, right, left)


def turned_blocks(whole, axis, dim):
    count, me = lax.axis_size(axis), lax.axis_index(axis)
    size = whole.shape[dim] // count
    return [
        lax.dynamic_slice_in_dim(whole, (me + place) % count * size, size, axis=dim)
        for place in range(count)
    ]


def plane_gather(piece, axis, sizes):
    core, across, along = ([(i, i ^ bit) for i in range(8)] for bit in (1, 2, 4))
    half = piece.shape[0] // 2
    top, low = piece[:half], piece[half:]

    def partner(part):
        return lax.ppermute(part, axis, core)

    top_x, low_y = lax.ppermute(top, axis, across), lax.ppermute(low, axis, along)
    top_y, low_x = lax.ppermute(top, axis, along), lax.ppermute(low, axis, across)
    top_xy, low_xy = lax.ppermute(top_x, axis, along), lax.ppermute(low_y, axis, across)
    held = [(top, low), (top_x, low_x), (top_y, low_y), (top_xy, low_xy)]
    parts = []
    for pair in held:
        parts += [pair, tuple(partner(part) for part in pair)]

    flat = [part for pair in parts for part in pair]
    lanes = jnp.arange(8, dtype=jnp.int32) ^ lax.axis_index(axis).astype(jnp.int32)
    return assemble(lanes * piece.shape[1], flat, sizes, 8 * piece.shape[1])


def local(
    inputs, segments, w_query, w_key, w_value, w_output, w_gate, w_up, w_down,
    gain_attn, gain_ffn, cotangent,
):
    low = jnp.bfloat16
    n_dp, n_mp = lax.axis_size("dp"), lax.axis_size("mp")
    batches, tokens, width = inputs.shape
    cols = w_query.shape[1]
    depth = w_query.shape[0]
    hidden_part = w_gate.shape[1]

    def split16(gain):
        high = gain.astype(low)
        return high, (gain - high.astype(jnp.float32)).astype(low)

    pieces = split16(gain_attn) + split16(gain_ffn)
    gain_row = jnp.concatenate(pieces + (jnp.zeros((3 * cols - 4 * depth,), low),))
    qkv_piece = jnp.concatenate(
        [
            jnp.concatenate([w_query, w_key, w_value], axis=1),
            jnp.pad(gain_row[None], ((0, 15), (0, 0))),
        ],
        axis=0,
    )
    qkv_all = lax.all_gather(qkv_piece, "dp", axis=0, tiled=False)
    w_qkv = qkv_all[:, :depth].reshape(width, 3 * cols)
    gains = qkv_all[:, depth, : 4 * depth].astype(jnp.float32).reshape(n_dp, 4, depth)
    gain_one = (gains[:, 0] + gains[:, 1]).reshape(width)
    gain_two = (gains[:, 2] + gains[:, 3]).reshape(width)

    rest_piece = jnp.concatenate([w_output, w_gate.T, w_up.T, w_down], axis=0)
    sizes = (cols, hidden_part, hidden_part, hidden_part)
    firsts = (0, cols, cols + hidden_part, cols + 2 * hidden_part)
    if n_dp == 8 and depth == 128:
        output_full, gate_full, up_full, down_full = plane_gather(line_gather(rest_piece, "mp"), "dp", sizes)
    else:
        rest_every = lax.all_gather(rest_piece, ("dp", "mp"), axis=0, tiled=False)
        rest_every = rest_every.reshape((n_dp, n_mp) + rest_piece.shape).transpose(1, 2, 0, 3)
        rest_every = rest_every.reshape(n_mp, rest_piece.shape[0], width)
        output_full, gate_full, up_full, down_full = (
            rest_every[:, first : first + size].reshape(n_mp * size, width)
            for first, size in zip(firsts, sizes)
        )

    first_rows = line_gather(inputs[0], "mp")
    first_rows, second_piece = lax.optimization_barrier((first_rows, inputs[1]))
    rows_all = [first_rows, None]

    normed, factors, qkv, tables, starts, lows, mixed, logs = [], [], [], [], [], [], [], []
    for m in range(batches):
        start = row_starts(segments[m, 0])
        cos_table, sin_table = rope_tables(start)
        tables.append((cos_table, sin_table))
        starts.append(start[None])
        lows.append((start[::BQ] // BK_FORWARD, start[::BQ] // BK))
        if m == 1:
            rows_all[1] = line_gather(second_piece, "mp")
        rows = rows_all[m].astype(jnp.float32)
        factors.append(rms_factor(rows))
        normed.append((rows * factors[m] * gain_one).astype(low))
        pre = dot_dims(w_qkv, normed[m], 0, 1)
        turned_q = rotate(pre[:cols], cos_table, sin_table) * HD ** -0.5
        turned_k = rotate(pre[cols : 2 * cols], cos_table, sin_table)
        qkv.append(jnp.concatenate([turned_q, turned_k, pre[2 * cols :]], axis=0).astype(low))
        out, log = attn_fwd(qkv[m], starts[m], lows[m][0])
        mixed.append(out)
        logs.append(log)
    mixed_own = []
    for m in range(batches):
        mixed_own.append(
            lax.all_to_all(mixed[m], "mp", split_axis=1, concat_axis=0, tiled=True)
        )
    in_float = inputs.astype(jnp.float32).reshape(batches * tokens, width)
    mixed_both = jnp.concatenate(mixed_own, axis=1)
    hidden_in = in_float + dot_dims(mixed_both, output_full, 0, 0)
    factor_ffn = rms_factor(hidden_in)
    normed_ffn = (hidden_in * factor_ffn * gain_two).astype(low)
    grad_top = cotangent.reshape(batches * tokens, width)
    hidden, grad_gate_pre, grad_up_pre = ffn_main(
        normed_ffn, grad_top, gate_full, up_full, down_full
    )
    grad_normed_ffn = dot_dims(grad_gate_pre, gate_full, 1, 0) + dot_dims(
        grad_up_pre, up_full, 1, 0
    )
    result = (hidden_in + dot_dims(hidden, down_full, 1, 0)).astype(low)
    chunks = width // 128
    every_grad = ffn_grad(normed_ffn, grad_top, hidden, grad_gate_pre, grad_up_pre, chunks)
    if n_dp != chunks:
        every_grad = every_grad.reshape(chunks, 3, n_mp * hidden_part, n_dp // chunks, depth)
        every_grad = every_grad.transpose(0, 3, 1, 2, 4).reshape(n_dp, 3, -1, depth)
    grad_middle, gain_ffn_part = rms_back(hidden_in, factor_ffn, gain_two, grad_normed_ffn)
    grad_hidden_in = grad_top.astype(jnp.float32) + grad_middle
    grad_branch = grad_hidden_in.astype(low)
    grad_mixed = dot_dims(output_full, grad_branch, 1, 1).astype(low)
    grad_mixed_rows = []
    for m in range(batches):
        grad_mixed_rows.append(
            lax.all_to_all(
                grad_mixed[:, m * tokens : (m + 1) * tokens], "mp", split_axis=0,
                concat_axis=1, tiled=True,
            )
        )
    grad_output = dot_dims(grad_branch, mixed_both, 0, 1).astype(low)

    grad_mixed_rows[0], every_grad = lax.optimization_barrier((grad_mixed_rows[0], every_grad))
    mine = scatter(every_grad, "dp", 0)


    grad_qkv, grad_normed = [], []
    gain_attn_part = jnp.zeros((width,), jnp.float32)
    for m in range(batches):
        cos_table, sin_table = tables[m]
        back = attn_bwd(
            qkv[m], grad_mixed_rows[m], mixed[m], logs[m], starts[m], lows[m][1], cos_table,
            sin_table,
        ).reshape(3 * cols, n_mp * tokens)
        grad_qkv.append(back)
        spread = [
            dot_dims(part, w_qkv, 0, 1).astype(low) for part in turned_blocks(back, "mp", 1)
        ]
        grad_normed.append(line_scatter(spread, "mp"))
        own_rows = turned_blocks(rows_all[m], "mp", 0)
        own_factors = turned_blocks(factors[m], "mp", 0)
        for part, rows, factor in zip(spread, own_rows, own_factors):
            gain_attn_part = gain_attn_part + jnp.sum(
                part.astype(jnp.float32) * rows.astype(jnp.float32) * factor, axis=0
            )
    grad_w = 0.0
    for m in range(batches):
        grad_w = grad_w + dot_dims(normed[m], grad_qkv[m], 0, 1)

    gain_parts = jnp.stack([gain_attn_part, gain_ffn_part]).astype(low)
    gain_parts = gain_parts.reshape(2, n_dp, depth).transpose(1, 0, 2).reshape(n_dp, 1, 2 * depth)
    sums = jnp.concatenate(
        [
            grad_w.astype(low).reshape(n_dp, depth, 3 * cols),
            grad_output.reshape(n_dp, depth, n_mp * cols),
        ],
        axis=2,
    )
    gain_rows = jnp.pad(gain_parts, ((0, 0), (0, 15), (0, sums.shape[2] - 2 * depth)))
    sums = jnp.concatenate([sums, gain_rows], axis=1)
    sums = lax.all_to_all(sums, "dp", split_axis=0, concat_axis=0, tiled=True)
    sums = jnp.sum(sums.astype(jnp.float32), axis=0)
    own_qkv, own_out = sums[:depth, : 3 * cols], sums[:depth, 3 * cols :]
    own_gain = sums[depth, : 2 * depth].reshape(2, n_mp, depth // n_mp).transpose(1, 0, 2)
    own_gain = own_gain.reshape(n_mp, 1, 2 * depth // n_mp)
    own_gain = jnp.pad(own_gain.astype(low), ((0, 0), (0, 15), (0, depth - own_gain.shape[2])))
    own_ffn = mine.reshape(3, n_mp, hidden_part, depth).transpose(1, 0, 2, 3)
    own_rest = jnp.concatenate(
        [
            own_out.T.astype(low).reshape(n_mp, cols, depth),
            own_ffn.reshape(n_mp, -1, depth),
            own_gain,
        ],
        axis=1,
    )
    own_rest = own_rest.reshape(-1, depth)
    own_rest = turned_blocks(own_rest, "mp", 0)
    own_rest = line_scatter(own_rest, "mp")
    own_output, own_gate, own_up, own_down = (
        own_rest[first : first + size] for first, size in zip(firsts, sizes)
    )
    grad_norms = own_rest[sum(sizes), : 2 * depth // n_mp].reshape(2, -1)

    grad_normed_attn = jnp.concatenate(grad_normed, axis=0)
    grad_lower, _ = rms_back(in_float, rms_factor(in_float), gain_one, grad_normed_attn)
    grad_inputs = (grad_hidden_in + grad_lower).astype(low)
    return (
        result.reshape(inputs.shape),
        grad_inputs.reshape(inputs.shape),
        own_qkv[:, :cols],
        own_qkv[:, cols : 2 * cols],
        own_qkv[:, 2 * cols :],
        own_output,
        own_gate.T,
        own_up.T,
        own_down,
        grad_norms[0],
        grad_norms[1],
    )


def solution(mesh):
    row_spec = P(None, ("dp", "mp"), None)
    first, second = P("dp", "mp"), P("mp", "dp")
    both = P(("dp", "mp"))

    return jax.shard_map(
        local,
        mesh=mesh,
        in_specs=(
            row_spec, P(None, "dp", None), first, first, first, second, first, first, second,
            P("dp"), P("dp"), row_spec,
        ),
        out_specs=(
            row_spec, row_spec, first, first, first, second, first, first, second, both, both,
        ),
        check_vma=False,
    )
```

```python
import functools
import math

import jax
import jax.numpy as jnp
from jax import lax
from jax.experimental import pallas as pl
from jax.experimental.pallas import tpu as pltpu
from jax.sharding import PartitionSpec as P


HD = 64
BQ = 512
BK = 256
BK_FORWARD = 256
HPS = 2


def attn_fwd_kernel(lo_ref, q_ref, k_ref, v_ref, start_ref, o_ref, lse_ref, k_scr, *, bq, bk, heads):
    length = q_ref.shape[1]
    k_scr[...] = k_ref[...].T

    def q_step(qi, carry):
        q0 = pl.multiple_of(qi * bq, bq)
        qcols = pl.ds(q0, bq)
        q_blk = q_ref[:, qcols]
        start = start_ref[:, qcols]
        q_idx = q0 + lax.broadcasted_iota(jnp.int32, (1, bq), 1)

        def visit(kb, state, first):
            k0 = pl.multiple_of(kb * bk, bk)
            wide = bq - first
            k_idx = k0 + lax.broadcasted_iota(jnp.int32, (bk, wide), 0)
            allowed = (k_idx >= start[:, first:]) & (k_idx <= q_idx[:, first:])
            out = []
            for h in range(heads):
                peak, total, acc = (part[:, first:] for part in state[h])
                s = jnp.dot(k_scr[pl.ds(k0, bk), h * HD:(h + 1) * HD], q_blk[h * HD:(h + 1) * HD, first:], preferred_element_type=jnp.float32)
                s = jnp.where(allowed, s, -1e30)
                new_peak = jnp.maximum(peak, jnp.max(s, axis=0, keepdims=True))
                p = jnp.exp(s - new_peak)
                fade = jnp.exp(peak - new_peak)
                total = total * fade + jnp.sum(p, axis=0, keepdims=True)
                acc = acc * fade + jnp.dot(v_ref[h * HD:(h + 1) * HD, pl.ds(k0, bk)], p.astype(jnp.bfloat16), preferred_element_type=jnp.float32)
                fresh = (new_peak, total, acc)
                if first:
                    fresh = tuple(jnp.concatenate([old[:, :first], new], axis=1) for old, new in zip(state[h], fresh))
                out.append(fresh)
            return tuple(out)

        init = tuple((jnp.full((1, bq), -1e30, jnp.float32), jnp.zeros((1, bq), jnp.float32), jnp.zeros((HD, bq), jnp.float32)) for _ in range(heads))
        hi = (q0 + bq - 1) // bk
        state = lax.fori_loop(lo_ref[qi], hi, lambda kb, state: visit(kb, state, 0), init)
        state = visit(hi, state, bq - bk)
        for h in range(heads):
            peak, total, acc = state[h]
            o_ref[h * HD:(h + 1) * HD, qcols] = (acc / total).astype(jnp.bfloat16)
            lse_ref[h, :, qcols] = peak + jnp.log(total)
        return carry

    lax.fori_loop(0, length // bq, q_step, 0)


def attn_bwd_kernel(lo_ref, q_ref, k_ref, v_ref, do_ref, o_ref, lse_ref, start_ref, cos_ref, sin_ref, out_ref, k_scr, v_scr, dk_scr, dv_scr, *, bq, bk, heads):
    length = q_ref.shape[1]
    k_scr[...] = k_ref[...].T
    v_scr[...] = v_ref[...].T
    dk_scr[...] = jnp.zeros_like(dk_scr)
    dv_scr[...] = jnp.zeros_like(dv_scr)
    half = HD // 2

    def unrotate(g, cos, sin):
        a, b = g[:half], g[half:]
        return jnp.concatenate([a * cos + b * sin, b * cos - a * sin], axis=0).astype(jnp.bfloat16)

    def q_step(qi, carry):
        q0 = pl.multiple_of(qi * bq, bq)
        qcols = pl.ds(q0, bq)
        q_blk = q_ref[:, qcols]
        do_blk = do_ref[:, qcols]
        q_t = q_blk.T
        do_t = do_blk.T
        prod = do_blk.astype(jnp.float32) * o_ref[:, qcols].astype(jnp.float32)
        start = start_ref[:, qcols]
        q_idx = q0 + lax.broadcasted_iota(jnp.int32, (1, bq), 1)
        deltas = [jnp.sum(prod[h * HD:(h + 1) * HD], axis=0, keepdims=True) for h in range(heads)]
        lses = [lse_ref[h, :, qcols] for h in range(heads)]

        def visit(kb, state, first):
            k0 = pl.multiple_of(kb * bk, bk)
            rows = pl.ds(k0, bk)
            k_idx = k0 + lax.broadcasted_iota(jnp.int32, (bk, bq - first), 0)
            allowed = (k_idx >= start[:, first:]) & (k_idx <= q_idx[:, first:])
            out = []
            for h in range(heads):
                hs = slice(h * HD, (h + 1) * HD)
                s = jnp.dot(k_scr[rows, hs], q_blk[hs, first:], preferred_element_type=jnp.float32)
                p = jnp.exp(jnp.where(allowed, s - lses[h][:, first:], -1e30))
                dp = jnp.dot(v_scr[rows, hs], do_blk[hs, first:], preferred_element_type=jnp.float32)
                ds = (p * (dp - deltas[h][:, first:])).astype(jnp.bfloat16)
                dv_scr[h, rows, :] += jnp.dot(p.astype(jnp.bfloat16), do_t[first:, hs], preferred_element_type=jnp.float32)
                dk_scr[h, rows, :] += jnp.dot(ds, q_t[first:, hs], preferred_element_type=jnp.float32)
                part = jnp.dot(k_ref[hs, rows], ds, preferred_element_type=jnp.float32)
                if first:
                    part = jnp.concatenate([state[h][:, :first], state[h][:, first:] + part], axis=1)
                else:
                    part = state[h] + part
                out.append(part)
            return tuple(out)

        init = tuple(jnp.zeros((HD, bq), jnp.float32) for _ in range(heads))
        hi = (q0 + bq - 1) // bk
        state = lax.fori_loop(lo_ref[qi], hi, lambda kb, state: visit(kb, state, 0), init)
        state = visit(hi, state, bq - bk)
        cos, sin = cos_ref[:, qcols], sin_ref[:, qcols]
        for h in range(heads):
            out_ref[0, h * HD:(h + 1) * HD, qcols] = unrotate(state[h] * HD ** -0.5, cos, sin)
        return carry

    lax.fori_loop(0, length // bq, q_step, 0)
    for h in range(heads):
        out_ref[1, h * HD:(h + 1) * HD, :] = unrotate(dk_scr[h].T, cos_ref[...], sin_ref[...])
        out_ref[2, h * HD:(h + 1) * HD, :] = dv_scr[h].T.astype(jnp.bfloat16)


def attn_fwd(qkv_t, start, lo, bq=BQ, bk=BK_FORWARD, hps=HPS):
    cols3, length = qkv_t.shape
    cols = cols3 // 3
    steps = cols // (HD * hps)
    blk = (HD * hps, length)
    area = cols * length * length // 4
    return pl.pallas_call(
        functools.partial(attn_fwd_kernel, bq=bq, bk=bk, heads=hps),
        out_shape=(jax.ShapeDtypeStruct((cols, length), jnp.bfloat16), jax.ShapeDtypeStruct((cols // HD, 1, length), jnp.float32)),
        grid_spec=pltpu.PrefetchScalarGridSpec(
            num_scalar_prefetch=1, grid=(steps,),
            in_specs=[pl.BlockSpec(blk, lambda i, lo: (i, 0)), pl.BlockSpec(blk, lambda i, lo: (i + steps, 0)), pl.BlockSpec(blk, lambda i, lo: (i + 2 * steps, 0)),
                      pl.BlockSpec((1, length), lambda i, lo: (0, 0))],
            out_specs=[pl.BlockSpec(blk, lambda i, lo: (i, 0)), pl.BlockSpec((hps, 1, length), lambda i, lo: (i, 0, 0))],
            scratch_shapes=[pltpu.VMEM((length, HD * hps), jnp.bfloat16)]),
        cost_estimate=pl.CostEstimate(flops=16 * area, bytes_accessed=cols * length * 8, transcendentals=area // HD),
        name="attn_fwd",
    )(lo, qkv_t, qkv_t, qkv_t, start)


def attn_bwd(qkv_t, do_t, o_t, lse, start, lo, cos, sin, bq=BQ, bk=BK, hps=HPS):
    cols3, length = qkv_t.shape
    cols = cols3 // 3
    steps = cols // (HD * hps)
    blk = (HD * hps, length)
    area = cols * length * length // 4
    return pl.pallas_call(
        functools.partial(attn_bwd_kernel, bq=bq, bk=bk, heads=hps),
        out_shape=jax.ShapeDtypeStruct((3, cols, length), jnp.bfloat16),
        grid_spec=pltpu.PrefetchScalarGridSpec(
            num_scalar_prefetch=1, grid=(steps,),
            in_specs=[pl.BlockSpec(blk, lambda i, lo: (i, 0)), pl.BlockSpec(blk, lambda i, lo: (i + steps, 0)), pl.BlockSpec(blk, lambda i, lo: (i + 2 * steps, 0)),
                      pl.BlockSpec(blk, lambda i, lo: (i, 0)), pl.BlockSpec(blk, lambda i, lo: (i, 0)),
                      pl.BlockSpec((hps, 1, length), lambda i, lo: (i, 0, 0)),
                      pl.BlockSpec((1, length), lambda i, lo: (0, 0)),
                      pl.BlockSpec((HD // 2, length), lambda i, lo: (0, 0)), pl.BlockSpec((HD // 2, length), lambda i, lo: (0, 0))],
            out_specs=pl.BlockSpec((3,) + blk, lambda i, lo: (0, i, 0)),
            scratch_shapes=[pltpu.VMEM((length, HD * hps), jnp.bfloat16)] * 2 + [pltpu.VMEM((hps, length, HD), jnp.float32)] * 2),
        cost_estimate=pl.CostEstimate(flops=40 * area, bytes_accessed=cols * length * 20, transcendentals=area // HD),
        name="attn_bwd",
    )(lo, qkv_t, qkv_t, qkv_t, do_t, o_t, lse, start, cos, sin)


def assemble_kernel(lane_ref, *refs, sizes, parts):
    pieces, outs = refs[: 2 * parts], refs[2 * parts : 2 * parts + len(sizes)]
    held, in_sem, out_sem = refs[2 * parts + len(sizes) :]
    slots = held.shape[0]
    total = sum(sizes)
    steps = [
        (block, part, sum(sizes[:part])) for block in range(4) for part in range(len(sizes))
    ]

    def fetch(step):
        block, part, first = steps[step]
        rows = pl.ds((block % 2) * total + first, sizes[part])
        slot = step % slots
        return [
            pltpu.make_async_copy(
                pieces[2 * r + block // 2].at[rows],
                held.at[slot, pl.ds(0, sizes[part]), pl.ds(pl.multiple_of(lane_ref[r], 128), 128)],
                in_sem.at[slot, r],
            )
            for r in range(parts)
        ]

    def put(step):
        block, part, _ = steps[step]
        slot = step % slots
        return pltpu.make_async_copy(
            held.at[slot, pl.ds(0, sizes[part])],
            outs[part].at[pl.ds(block * sizes[part], sizes[part])],
            out_sem.at[slot],
        )

    ahead = slots // 2
    for step in range(ahead):
        for copy in fetch(step):
            copy.start()
    for step in range(len(steps)):
        later = step + ahead
        if later < len(steps):
            if later >= slots:
                put(later - slots).wait()
            for copy in fetch(later):
                copy.start()
        for copy in fetch(step):
            copy.wait()
        put(step).start()
    for step in range(len(steps) - slots, len(steps)):
        put(step).wait()


def assemble(lanes, pieces, sizes, width):
    parts = len(pieces) // 2
    whole = pl.BlockSpec(memory_space=pl.ANY)
    return pl.pallas_call(
        functools.partial(assemble_kernel, sizes=sizes, parts=parts),
        out_shape=[jax.ShapeDtypeStruct((4 * size, width), jnp.bfloat16) for size in sizes],
        grid_spec=pltpu.PrefetchScalarGridSpec(
            num_scalar_prefetch=1,
            grid=(1,),
            in_specs=[whole] * len(pieces),
            out_specs=[whole] * len(sizes),
            scratch_shapes=[
                pltpu.VMEM((4, max(sizes), width), jnp.bfloat16),
                pltpu.SemaphoreType.DMA((4, parts)),
                pltpu.SemaphoreType.DMA((4,)),
            ],
        ),
        cost_estimate=pl.CostEstimate(
            flops=0, bytes_accessed=16 * sum(sizes) * width, transcendentals=0
        ),
        name="assemble",
    )(lanes, *pieces)


def dot_in(left, right, left_dim, right_dim):
    return lax.dot_general(
        left, right, (((left_dim,), (right_dim,)), ((), ())), preferred_element_type=jnp.float32
    )


def ffn_main_kernel(x_ref, c_ref, gate_ref, up_ref, down_ref, h_ref, dg_ref, du_ref, *, step):
    for first in range(0, x_ref.shape[0], step):
        rows = slice(first, first + step)
        gate = dot_in(x_ref[rows], gate_ref[...], 1, 1)
        up = dot_in(x_ref[rows], up_ref[...], 1, 1)
        grad_hidden = dot_in(c_ref[rows], down_ref[...], 1, 1)
        sig = jax.nn.sigmoid(gate)
        silu = gate * sig
        h_ref[rows] = (silu * up).astype(jnp.bfloat16)
        dg = (grad_hidden * up * sig * (1.0 + gate * (1.0 - sig))).astype(jnp.bfloat16)
        du = (grad_hidden * silu).astype(jnp.bfloat16)
        dg_ref[rows] = dg
        du_ref[rows] = du


def ffn_grad_kernel(x_ref, c_ref, h_ref, dg_ref, du_ref, g_ref):
    for place, (left, right) in enumerate(((dg_ref, x_ref), (du_ref, x_ref), (h_ref, c_ref))):
        grad = dot_in(left[...], right[...], 0, 0).astype(jnp.bfloat16)
        for i in range(g_ref.shape[0]):
            g_ref[i, place] = grad[:, i * g_ref.shape[3] : (i + 1) * g_ref.shape[3]]


def ffn_main(x, c, gate, up, down, tile=256, step=256):
    tokens, width = x.shape
    units = gate.shape[0]
    full = pl.BlockSpec((tokens, width), lambda t: (0, 0))
    weight = pl.BlockSpec((tile, width), lambda t: (t, 0))
    column = pl.BlockSpec((tokens, tile), lambda t: (0, t))
    return pl.pallas_call(
        functools.partial(ffn_main_kernel, step=step),
        out_shape=[jax.ShapeDtypeStruct((tokens, units), jnp.bfloat16)] * 3,
        grid=(units // tile,),
        in_specs=[full, full, weight, weight, weight],
        out_specs=[column, column, column],
        cost_estimate=pl.CostEstimate(
            flops=6 * tokens * width * units, bytes_accessed=6 * units * (width + tokens),
            transcendentals=tokens * units,
        ),
        name="ffn_main",
    )(x, c, gate, up, down)


def ffn_grad(x, c, hidden, dg, du, chunks, tile=256):
    tokens, width = x.shape
    units = hidden.shape[1]
    full = pl.BlockSpec((tokens, width), lambda t: (0, 0))
    column = pl.BlockSpec((tokens, tile), lambda t: (0, t))
    piece = width // chunks
    return pl.pallas_call(
        ffn_grad_kernel,
        out_shape=jax.ShapeDtypeStruct((chunks, 3, units, piece), jnp.bfloat16),
        grid=(units // tile,),
        in_specs=[full, full, column, column, column],
        out_specs=pl.BlockSpec((chunks, 3, tile, piece), lambda t: (0, 0, t, 0)),
        cost_estimate=pl.CostEstimate(
            flops=6 * tokens * width * units, bytes_accessed=6 * units * (width + tokens),
            transcendentals=0,
        ),
        name="ffn_grad",
    )(x, c, hidden, dg, du)


def spread_kernel(place_ref, back_ref, w_ref, out_ref):
    out_ref[...] = dot_in(back_ref[...], w_ref[...], 0, 0).astype(jnp.bfloat16)


def spread_block(back, w_turned, place, rows, tile=512):
    depth, width = w_turned.shape
    return pl.pallas_call(
        spread_kernel,
        out_shape=jax.ShapeDtypeStruct((rows, width), jnp.bfloat16),
        grid_spec=pltpu.PrefetchScalarGridSpec(
            num_scalar_prefetch=1,
            grid=(width // tile,),
            in_specs=[
                pl.BlockSpec((depth, rows), lambda t, place: (0, place[0])),
                pl.BlockSpec((depth, tile), lambda t, place: (0, t)),
            ],
            out_specs=pl.BlockSpec((rows, tile), lambda t, place: (0, t)),
        ),
        cost_estimate=pl.CostEstimate(
            flops=2 * rows * width * depth, bytes_accessed=2 * (rows + width) * depth,
            transcendentals=0,
        ),
        name="spread_block",
    )(place.astype(jnp.int32)[None], back, w_turned)


eps_norm = 1e-05


def dot_dims(left, right, left_dim, right_dim):
    return lax.dot_general(
        left, right, (((left_dim,), (right_dim,)), ((), ())), preferred_element_type=jnp.float32
    )


def row_starts(seg_row):
    ones = [jnp.sum((seg_row < s).astype(jnp.int32)) for s in (1, 2, 3)]
    start = jnp.zeros_like(seg_row)
    before = 0
    for s, count in zip((1, 2, 3), ones):
        start = start + jnp.where(seg_row >= s, count - before, 0)
        before = count
    return start


def rope_tables(start):
    half_dim = HD // 2
    offsets = (jnp.arange(start.shape[0], dtype=jnp.int32) - start).astype(jnp.float32)
    frequency = jnp.exp(jnp.arange(half_dim, dtype=jnp.float32) * (-math.log(10000.0) / half_dim))
    angles = frequency[:, None] * offsets[None, :]
    return jnp.cos(angles), jnp.sin(angles)


def rotate(rows, cos_table, sin_table):
    count, length = rows.shape
    parts = rows.reshape(count // HD, 2, HD // 2, length)
    low, high = parts[:, 0], parts[:, 1]
    turned = jnp.stack(
        [low * cos_table - high * sin_table, high * cos_table + low * sin_table], axis=1
    )
    return turned.reshape(count, length)


def rms_factor(values):
    return lax.rsqrt(jnp.mean(values * values, axis=-1, keepdims=True) + eps_norm)


def rms_back(values_in, factor, gain, grad_normed):
    scaled = grad_normed * gain
    gain_part = jnp.sum(grad_normed * values_in * factor, axis=0)
    inner = jnp.mean(scaled * values_in, axis=-1, keepdims=True)
    return factor * scaled - values_in * (factor * factor * factor) * inner, gain_part


def scatter(partial_sum, axis, dim):
    return lax.psum_scatter(partial_sum, axis, scatter_dimension=dim, tiled=True)


def line_steps(count):
    near_right = [(i, i + 1) for i in range(count - 1)]
    near_left = [(i, i - 1) for i in range(1, count)]
    return near_right, near_left


def line_gather(piece, axis):
    count, me = lax.axis_size(axis), lax.axis_index(axis)
    assert count == 4
    near_right, near_left = line_steps(count)
    one_left = lax.ppermute(piece, axis, near_right)
    one_right = lax.ppermute(piece, axis, near_left)
    two_left = lax.ppermute(one_left, axis, [(1, 2), (2, 3)])
    two_right = lax.ppermute(one_right, axis, [(1, 0), (2, 1)])
    three_left = lax.ppermute(one_left, axis, [(1, 3)])
    three_right = lax.ppermute(one_right, axis, [(2, 0)])
    slots = jnp.concatenate(
        [three_left, two_left, one_left, piece, one_right, two_right, three_right], axis=0
    )
    rows = piece.shape[0]
    return lax.dynamic_slice_in_dim(slots, (count - 1 - me) * rows, count * rows, axis=0)


def line_scatter(blocks, axis):
    count = lax.axis_size(axis)
    assert count == 4
    near_right, near_left = line_steps(count)
    own, next_one, opposite, last = blocks
    two_right = lax.ppermute(opposite, axis, [(0, 1), (1, 2)])
    two_left = lax.ppermute(opposite, axis, [(3, 2), (2, 1)])
    three_right = lax.ppermute(last, axis, [(0, 2)])
    three_left = lax.ppermute(next_one, axis, [(3, 1)])

    own, next_one, last = lax.optimization_barrier((own, next_one, last))

    def total(*parts):
        return sum(part.astype(jnp.float32) for part in parts)

    right = lax.ppermute(
        total(next_one, two_right, three_right).astype(jnp.bfloat16), axis, near_right
    )
    left = lax.ppermute(
        total(last, two_left, three_left).astype(jnp.bfloat16), axis, near_left
    )
    return total(own, right, left)


def turned_blocks(whole, axis, dim):
    count, me = lax.axis_size(axis), lax.axis_index(axis)
    size = whole.shape[dim] // count
    return [
        lax.dynamic_slice_in_dim(whole, (me + place) % count * size, size, axis=dim)
        for place in range(count)
    ]


def plane_gather(piece, axis, sizes):
    core, across, along = ([(i, i ^ bit) for i in range(8)] for bit in (1, 2, 4))
    half = piece.shape[0] // 2
    top, low = piece[:half], piece[half:]

    def partner(part):
        return lax.ppermute(part, axis, core)

    top_x, low_y = lax.ppermute(top, axis, across), lax.ppermute(low, axis, along)
    top_y, low_x = lax.ppermute(top, axis, along), lax.ppermute(low, axis, across)
    top_xy, low_xy = lax.ppermute(top_x, axis, along), lax.ppermute(low_y, axis, across)
    held = [(top, low), (top_x, low_x), (top_y, low_y), (top_xy, low_xy)]
    parts = []
    for pair in held:
        parts += [pair, tuple(partner(part) for part in pair)]

    flat = [part for pair in parts for part in pair]
    lanes = jnp.arange(8, dtype=jnp.int32) ^ lax.axis_index(axis).astype(jnp.int32)
    return assemble(lanes * piece.shape[1], flat, sizes, 8 * piece.shape[1])


def local(
    inputs, segments, w_query, w_key, w_value, w_output, w_gate, w_up, w_down,
    gain_attn, gain_ffn, cotangent,
):
    low = jnp.bfloat16
    n_dp, n_mp = lax.axis_size("dp"), lax.axis_size("mp")
    batches, tokens, width = inputs.shape
    cols = w_query.shape[1]
    depth = w_query.shape[0]
    hidden_part = w_gate.shape[1]

    def split16(gain):
        high = gain.astype(low)
        return high, (gain - high.astype(jnp.float32)).astype(low)

    pieces = split16(gain_attn) + split16(gain_ffn)
    gain_row = jnp.concatenate(pieces + (jnp.zeros((3 * cols - 4 * depth,), low),))
    qkv_piece = jnp.concatenate(
        [
            jnp.concatenate([w_query, w_key, w_value], axis=1),
            jnp.pad(gain_row[None], ((0, 15), (0, 0))),
        ],
        axis=0,
    )
    qkv_all = lax.all_gather(qkv_piece, "dp", axis=0, tiled=False)
    w_qkv = qkv_all[:, :depth].reshape(width, 3 * cols)
    gains = qkv_all[:, depth, : 4 * depth].astype(jnp.float32).reshape(n_dp, 4, depth)
    gain_one = (gains[:, 0] + gains[:, 1]).reshape(width)
    gain_two = (gains[:, 2] + gains[:, 3]).reshape(width)

    rest_piece = jnp.concatenate([w_output, w_gate.T, w_up.T, w_down], axis=0)
    sizes = (cols, hidden_part, hidden_part, hidden_part)
    firsts = (0, cols, cols + hidden_part, cols + 2 * hidden_part)
    if n_dp == 8 and depth == 128:
        output_full, gate_full, up_full, down_full = plane_gather(line_gather(rest_piece, "mp"), "dp", sizes)
    else:
        rest_every = lax.all_gather(rest_piece, ("dp", "mp"), axis=0, tiled=False)
        rest_every = rest_every.reshape((n_dp, n_mp) + rest_piece.shape).transpose(1, 2, 0, 3)
        rest_every = rest_every.reshape(n_mp, rest_piece.shape[0], width)
        output_full, gate_full, up_full, down_full = (
            rest_every[:, first : first + size].reshape(n_mp * size, width)
            for first, size in zip(firsts, sizes)
        )

    first_rows = line_gather(inputs[0], "mp")
    first_rows, second_piece = lax.optimization_barrier((first_rows, inputs[1]))
    rows_all = [first_rows, None]

    normed, factors, qkv, tables, starts, lows, mixed, logs = [], [], [], [], [], [], [], []
    for m in range(batches):
        start = row_starts(segments[m, 0])
        cos_table, sin_table = rope_tables(start)
        tables.append((cos_table, sin_table))
        starts.append(start[None])
        lows.append((start[::BQ] // BK_FORWARD, start[::BQ] // BK))
        if m == 1:
            rows_all[1] = line_gather(second_piece, "mp")
        rows = rows_all[m].astype(jnp.float32)
        factors.append(rms_factor(rows))
        normed.append((rows * factors[m] * gain_one).astype(low))
        pre = dot_dims(w_qkv, normed[m], 0, 1)
        turned_q = rotate(pre[:cols], cos_table, sin_table) * HD ** -0.5
        turned_k = rotate(pre[cols : 2 * cols], cos_table, sin_table)
        qkv.append(jnp.concatenate([turned_q, turned_k, pre[2 * cols :]], axis=0).astype(low))
        out, log = attn_fwd(qkv[m], starts[m], lows[m][0])
        mixed.append(out)
        logs.append(log)
    mixed_own = []
    for m in range(batches):
        mixed_own.append(
            lax.all_to_all(mixed[m], "mp", split_axis=1, concat_axis=0, tiled=True)
        )
    in_float = inputs.astype(jnp.float32).reshape(batches * tokens, width)
    mixed_both = jnp.concatenate(mixed_own, axis=1)
    hidden_in = in_float + dot_dims(mixed_both, output_full, 0, 0)
    factor_ffn = rms_factor(hidden_in)
    normed_ffn = (hidden_in * factor_ffn * gain_two).astype(low)
    grad_top = cotangent.reshape(batches * tokens, width)
    hidden, grad_gate_pre, grad_up_pre = ffn_main(
        normed_ffn, grad_top, gate_full, up_full, down_full
    )
    grad_normed_ffn = dot_dims(grad_gate_pre, gate_full, 1, 0) + dot_dims(
        grad_up_pre, up_full, 1, 0
    )
    result = (hidden_in + dot_dims(hidden, down_full, 1, 0)).astype(low)
    chunks = width // 128
    every_grad = ffn_grad(normed_ffn, grad_top, hidden, grad_gate_pre, grad_up_pre, chunks)
    if n_dp != chunks:
        every_grad = every_grad.reshape(chunks, 3, n_mp * hidden_part, n_dp // chunks, depth)
        every_grad = every_grad.transpose(0, 3, 1, 2, 4).reshape(n_dp, 3, -1, depth)
    grad_middle, gain_ffn_part = rms_back(hidden_in, factor_ffn, gain_two, grad_normed_ffn)
    grad_hidden_in = grad_top.astype(jnp.float32) + grad_middle
    grad_branch = grad_hidden_in.astype(low)
    grad_mixed = dot_dims(output_full, grad_branch, 1, 1).astype(low)
    grad_mixed_rows = []
    for m in range(batches):
        grad_mixed_rows.append(
            lax.all_to_all(
                grad_mixed[:, m * tokens : (m + 1) * tokens], "mp", split_axis=0,
                concat_axis=1, tiled=True,
            )
        )
    grad_output = dot_dims(grad_branch, mixed_both, 0, 1).astype(low)

    grad_mixed_rows[0], every_grad = lax.optimization_barrier((grad_mixed_rows[0], every_grad))
    own_out = lax.all_to_all(
        grad_output.reshape(n_dp, depth, n_mp * cols), "dp", split_axis=0, concat_axis=0,
        tiled=True,
    )
    own_out = jnp.sum(own_out.astype(jnp.float32), axis=0).astype(low)
    mine = scatter(every_grad, "dp", 0)


    grad_qkv, grad_normed = [], []
    w_turned = w_qkv.T
    gain_attn_part = jnp.zeros((width,), jnp.float32)
    for m in range(batches):
        cos_table, sin_table = tables[m]
        back = attn_bwd(
            qkv[m], grad_mixed_rows[m], mixed[m], logs[m], starts[m], lows[m][1], cos_table,
            sin_table,
        ).reshape(3 * cols, n_mp * tokens)
        grad_qkv.append(back)
        spread = [spread_block(back, w_turned, (lax.axis_index("mp") + place) % n_mp, tokens) for place in range(n_mp)]
        grad_normed.append(line_scatter(spread, "mp"))
        own_rows = turned_blocks(rows_all[m], "mp", 0)
        own_factors = turned_blocks(factors[m], "mp", 0)
        for part, rows, factor in zip(spread, own_rows, own_factors):
            gain_attn_part = gain_attn_part + jnp.sum(
                part.astype(jnp.float32) * rows.astype(jnp.float32) * factor, axis=0
            )
    grad_w = 0.0
    for m in range(batches):
        grad_w = grad_w + dot_dims(normed[m], grad_qkv[m], 0, 1)

    gain_parts = jnp.stack([gain_attn_part, gain_ffn_part]).astype(low)
    gain_parts = gain_parts.reshape(2, n_dp, depth).transpose(1, 0, 2).reshape(n_dp, 1, 2 * depth)
    sums = grad_w.astype(low).reshape(n_dp, depth, 3 * cols)
    assert 2 * depth <= 3 * cols
    gain_rows = jnp.pad(gain_parts, ((0, 0), (0, 15), (0, sums.shape[2] - 2 * depth)))
    sums = jnp.concatenate([sums, gain_rows], axis=1)
    sums = lax.all_to_all(sums, "dp", split_axis=0, concat_axis=0, tiled=True)
    sums = jnp.sum(sums.astype(jnp.float32), axis=0)
    own_qkv = sums[:depth]
    own_gain = sums[depth, : 2 * depth].reshape(2, n_mp, depth // n_mp).transpose(1, 0, 2)
    own_gain = own_gain.reshape(n_mp, 1, 2 * depth // n_mp)
    own_gain = jnp.pad(own_gain.astype(low), ((0, 0), (0, 15), (0, depth - own_gain.shape[2])))
    own_ffn = mine.reshape(3, n_mp, hidden_part, depth).transpose(1, 0, 2, 3)
    own_rest = jnp.concatenate(
        [
            own_out.T.reshape(n_mp, cols, depth),
            own_ffn.reshape(n_mp, -1, depth),
            own_gain,
        ],
        axis=1,
    )
    own_rest = own_rest.reshape(-1, depth)
    own_rest = turned_blocks(own_rest, "mp", 0)
    own_rest = line_scatter(own_rest, "mp")
    own_output, own_gate, own_up, own_down = (
        own_rest[first : first + size] for first, size in zip(firsts, sizes)
    )
    grad_norms = own_rest[sum(sizes), : 2 * depth // n_mp].reshape(2, -1)

    grad_normed_attn = jnp.concatenate(grad_normed, axis=0)
    grad_lower, _ = rms_back(in_float, rms_factor(in_float), gain_one, grad_normed_attn)
    grad_inputs = (grad_hidden_in + grad_lower).astype(low)
    return (
        result.reshape(inputs.shape),
        grad_inputs.reshape(inputs.shape),
        own_qkv[:, :cols],
        own_qkv[:, cols : 2 * cols],
        own_qkv[:, 2 * cols :],
        own_output,
        own_gate.T,
        own_up.T,
        own_down,
        grad_norms[0],
        grad_norms[1],
    )


def solution(mesh):
    row_spec = P(None, ("dp", "mp"), None)
    first, second = P("dp", "mp"), P("mp", "dp")
    both = P(("dp", "mp"))

    return jax.shard_map(
        local,
        mesh=mesh,
        in_specs=(
            row_spec, P(None, "dp", None), first, first, first, second, first, first, second,
            P("dp"), P("dp"), row_spec,
        ),
        out_specs=(
            row_spec, row_spec, first, first, first, second, first, first, second, both, both,
        ),
        check_vma=False,
    )
```
